32 devices in a mesh: gx: 4 (over z), gy: 4 (over y, x), gz: 2 (over core).
Axes of the slice: x: 2, y: 2, z: 4, core: 2. Of those that a mesh axis runs over, the one named last changes fastest.
Arguments:
- source: float32 [32, 128, 256], P('gx', 'gy', 'gz'), may hold values from 0.05 to 1
- target: float32 [32, 128, 256], P('gx', 'gy', 'gz'), may hold values from 0.05 to 1
- kernel_half: float32 [5], replicated, may hold values from 0.05 to 1
- smooth_half: float32 [9], replicated, may hold values from 0.1 to 1
Outputs:
- displacement: float32 [3, 32, 128, 256], P(None, 'gx', 'gy', 'gz')
- mismatch: float32 [6], replicated
The draws below stay inside these ranges and needn't reach their ends.
All inputs are finite; a program needn't handle non-finite values.
Results may differ from the reference program's by a relative error of at most 0.0001.
Values sent between devices are 32-bit elements; how exact they have to be, the bound alone decides.
No kernel may reach another device: no remote copies, remote signals or barrier semaphores. Data moves between devices by JAX's collectives and lax.ppermute only.
A program may use at most 64 MiB of HBM per device.

```python
import math
import jax
import jax.numpy as jnp
from jax import lax

ITERS = 6
RADIUS = 4
SMOOTH = 8
NX = 32
NY = 128
NZ = 256


def level_of(own_key, extent, split, least, largest):
    def one(axis_at, shards_of):
        steps = jax.random.uniform(jax.random.fold_in(jax.random.fold_in(own_key, 6), axis_at), (shards_of,), jnp.float32, least / len(split), largest / len(split))
        return jnp.repeat(jnp.exp(steps), extent[axis_at] // shards_of).reshape((-1,) + (1,) * (len(extent) - axis_at - 1))

    factor_of = one(*split[0])
    for cut in split[1:]:
        factor_of = factor_of * one(*cut)
    return factor_of


def setup_inputs(seed: int = 0) -> dict:
    splits = jax.random.split(jax.random.key(seed), 5)
    return {
        "source": jnp.clip(jnp.exp(math.log(1.0) - 2.9957323 * jax.random.uniform(splits[0], (NX, NY, NZ), jnp.float32) ** level_of(splits[0], (NX, NY, NZ), ((0, 4), (1, 4), (2, 2)), -0.2, 0.2)), 0.05, 1.0),
        "target": jnp.clip(jnp.exp(math.log(1.0) - 2.9957323 * jax.random.uniform(splits[1], (NX, NY, NZ), jnp.float32) ** level_of(splits[1], (NX, NY, NZ), ((0, 4), (1, 4), (2, 2)), -0.2, 0.2)), 0.05, 1.0),
        "kernel_half": jnp.clip(jnp.exp(jax.random.uniform(splits[2], (RADIUS + 1,), jnp.float32, math.log(0.05), math.log(1.0))), 0.05, 1.0),
        "smooth_half": jnp.clip(jnp.exp(jax.random.uniform(splits[3], (SMOOTH + 1,), jnp.float32, math.log(0.1), math.log(1.0))), 0.1, 1.0),
    }


def full_taps(half):
    return jnp.concatenate([half[:0:-1], half])


def along(padded, taps, axis, count):
    width = taps.shape[0]
    total = taps[0] * lax.slice_in_dim(padded, 0, count, axis=axis)
    for j in range(1, width):
        total = total + taps[j] * lax.slice_in_dim(padded, j, j + count, axis=axis)
    return total


def kernel_apply(field, taps):
    radius = (taps.shape[0] - 1) // 2
    padded = jnp.pad(field, radius)
    padded = along(padded, taps, 0, NX)
    padded = along(padded, taps, 1, NY)
    return along(padded, taps, 2, NZ)


def reference(source, target, kernel_half, smooth_half):
    kern = full_taps(kernel_half)
    offsets = jnp.arange(-RADIUS, RADIUS + 1).astype(jnp.float32)
    slope = offsets * kern
    norm_total = smooth_half[0] + 2.0 * jnp.sum(smooth_half[1:])
    smooth = full_taps(smooth_half) / norm_total
    cells = float(NX * NY * NZ)
    first = source * (cells / jnp.sum(source))
    second = target * (cells / jnp.sum(target))
    scaling_v = jnp.ones_like(source)
    errors = []
    for step in range(ITERS):
        kv = kernel_apply(scaling_v, kern)
        scaling_u = first / kv
        ku = kernel_apply(scaling_u, kern)
        errors.append(jnp.sum(jnp.abs(scaling_v * ku - second)) / cells)
        scaling_v = second / ku
    padded = jnp.pad(scaling_v, RADIUS)
    pass_k = along(padded, kern, 0, NX)
    pass_g = along(padded, slope, 0, NX)
    kk = along(pass_k, kern, 1, NY)
    kg = along(pass_k, slope, 1, NY)
    gk = along(pass_g, kern, 1, NY)
    kvol = along(kk, kern, 2, NZ)
    znum = along(kk, slope, 2, NZ)
    ynum = along(kg, kern, 2, NZ)
    xnum = along(gk, kern, 2, NZ)
    raw = jnp.stack([xnum, ynum, znum]) / kvol
    padded = jnp.pad(raw, ((0, 0), (SMOOTH, SMOOTH), (SMOOTH, SMOOTH), (SMOOTH, SMOOTH)))
    padded = along(padded, smooth, 1, NX)
    padded = along(padded, smooth, 2, NY)
    displacement = along(padded, smooth, 3, NZ)
    return displacement, jnp.stack(errors)
```

```python
import functools

import jax
import jax.numpy as jnp
from jax import lax
from jax.experimental import pallas as pl
from jax.experimental.pallas import tpu as pltpu
from jax.sharding import PartitionSpec as P

ITERS = 6
LANES = 128
AXES = ("gx", "gy", "gz")


def padded_2(block, sides, width):
    for axis, dim in sides:
        count = lax.axis_size(axis)
        forward = [(i, i + 1) for i in range(count - 1)]
        backward = [(target, source) for source, target in forward]
        low = lax.ppermute(
            lax.slice_in_dim(block, block.shape[dim] - width, None, axis=dim), axis, forward
        )
        high = lax.ppermute(lax.slice_in_dim(block, 0, width, axis=dim), axis, backward)
        block = jnp.concatenate([low, block, high], axis=dim)
    return block


def full_taps(half):
    return jnp.concatenate([half[:0:-1], half])


def along(padded, taps, axis, count):
    width = taps.shape[0]
    total = taps[0] * lax.slice_in_dim(padded, 0, count, axis=axis)
    for j in range(1, width):
        total = total + taps[j] * lax.slice_in_dim(padded, j, j + count, axis=axis)
    return total


def three_passes(padded, taps, size_x, size_y, size_z):
    padded = along(padded, taps, 0, size_x)
    padded = along(padded, taps, 1, size_y)
    return along(padded, taps, 2, size_z)


def block_shards(source, target, kernel_half, smooth_half):
    kern = full_taps(kernel_half)
    radius = kernel_half.shape[0] - 1
    reach = smooth_half.shape[0] - 1
    offsets = jnp.arange(-radius, radius + 1).astype(jnp.float32)
    slope = offsets * kern
    norm_total = smooth_half[0] + 2.0 * jnp.sum(smooth_half[1:])
    smooth = full_taps(smooth_half) / norm_total
    size_x, size_y, size_z = source.shape
    cells = float(source.size * lax.axis_size("gx") * lax.axis_size("gy") * lax.axis_size("gz"))
    totals = lax.psum((jnp.sum(source), jnp.sum(target)), AXES)
    first = source * (cells / totals[0])
    second = target * (cells / totals[1])
    first_wide = padded_2(first, (("gx", 0), ("gy", 1), ("gz", 2)), radius)
    scaling_v = jnp.ones_like(source)
    errors = []
    for step in range(ITERS):
        padded = padded_2(scaling_v, (("gx", 0), ("gy", 1), ("gz", 2)), 2 * radius)
        kv_wide = three_passes(
            padded, kern, size_x + 2 * radius, size_y + 2 * radius, size_z + 2 * radius
        )
        u_wide = first_wide / kv_wide
        ku = three_passes(u_wide, kern, size_x, size_y, size_z)
        local_err = jnp.sum(jnp.abs(scaling_v * ku - second))
        errors.append(lax.psum(local_err, AXES) / cells)
        scaling_v = second / ku
    mismatch = jnp.stack(errors)
    padded = padded_2(scaling_v, (("gx", 0), ("gy", 1), ("gz", 2)), radius)
    pass_k = along(padded, kern, 0, size_x)
    pass_g = along(padded, slope, 0, size_x)
    kk = along(pass_k, kern, 1, size_y)
    kg = along(pass_k, slope, 1, size_y)
    gk = along(pass_g, kern, 1, size_y)
    kvol = along(kk, kern, 2, size_z)
    znum = along(kk, slope, 2, size_z)
    ynum = along(kg, kern, 2, size_z)
    xnum = along(gk, kern, 2, size_z)
    raw = jnp.stack([xnum, ynum, znum]) / kvol
    padded = padded_2(raw, (("gx", 1), ("gy", 2), ("gz", 3)), reach)
    padded = along(padded, smooth, 1, size_x)
    padded = along(padded, smooth, 2, size_y)
    displacement = along(padded, smooth, 3, size_z)
    return (displacement, mismatch)


class Plan:
    def __init__(self, mesh, bx, by, bz, radius, reach):
        self.nx, self.ny, self.nc = mesh["gx"], mesh["gy"], mesh["gz"]
        self.bx, self.by, self.bz = bx, by, bz
        self.R, self.Q = radius, reach
        self.P = self.nx * self.ny
        self.X, self.Y, self.Z = bx * self.nx, by * self.ny, bz * self.nc
        self.S = self.Z // self.P
        self.H = 4 * radius
        self.gs = LANES // by if by <= LANES else 0
        self.XH = self.X // 2
        self.cells = float(self.X * self.Y * self.Z)

    def fits(self):
        return (
            self.nc == 2
            and self.ny >= 2
            and self.ny & (self.ny - 1) == 0
            and self.nx >= 2
            and self.bz == LANES
            and self.Y == LANES
            and self.gs == self.ny
            and self.bx == 2 * self.gs
            and self.Z == self.P * self.S
            and self.S == self.H
            and self.S % 8 == 0
            and self.R % 4 == 0
            and ITERS == 6
        )

    def spot(self, at):
        at %= self.P
        col, q = divmod(at, self.nx)
        return (q if col % 2 == 0 else self.nx - 1 - q), col ^ (col >> 1)

    def chip(self, at):
        i, j = self.spot(at)
        return i * self.ny + j

    def device(self, at, core):
        return self.chip(at) * self.nc + core


def swap_cores(plan, value):
    pairs = [(plan.device(at, c), plan.device(at, 1 - c)) for at in range(plan.P) for c in range(2)]
    return lax.ppermute(value, AXES, pairs)


def swap_even(plan, value):
    pairs = [(plan.device(at, c), plan.device(at ^ 1, c)) for at in range(plan.P) for c in range(2)]
    return lax.ppermute(value, AXES, pairs)


def swap_odd(plan, value):
    pairs = [
        (plan.device(at, c), plan.device(((at + 1) ^ 1) - 1, c))
        for at in range(plan.P)
        for c in range(2)
    ]
    return lax.ppermute(value, AXES, pairs)


def swap_sides(plan, value):
    pairs = [(plan.device(at, 0), plan.device(at - 1, 1)) for at in range(plan.P)]
    pairs += [(plan.device(at, 1), plan.device(at + 1, 0)) for at in range(plan.P)]
    return lax.ppermute(value, AXES, pairs)


def place_of(plan):
    i, j = lax.axis_index("gx"), lax.axis_index("gy")
    at = jnp.int32(0)
    for place in range(plan.P):
        a, b = plan.spot(place)
        at = at + jnp.where((i == a) & (j == b), place, 0)
    return at.astype(jnp.int32)


def call(kernel, out_shape, n_smem, n_vmem, scratch=(), smem_out=0, name=None):
    vm, sm = pl.BlockSpec(memory_space=pltpu.VMEM), pl.BlockSpec(memory_space=pltpu.SMEM)
    out_specs = [vm] * (len(out_shape) - smem_out) + [sm] * smem_out
    return pl.pallas_call(
        kernel,
        out_shape=out_shape,
        in_specs=[sm] * n_smem + [vm] * n_vmem,
        out_specs=out_specs,
        scratch_shapes=list(scratch),
        compiler_params=pltpu.CompilerParams(vmem_limit_bytes=48 << 20),
        name=name,
    )


def f32(*shape):
    return jax.ShapeDtypeStruct(shape, jnp.float32)


def turn_groups(plan, parts):
    n, w = plan.gs, plan.by
    group = lax.broadcasted_iota(jnp.int32, parts[0].shape, 1) // w
    outs = []
    for a in range(n):
        total = parts[a]
        for b in range(n):
            if b != a:
                moved = pltpu.roll(parts[b], (w * (b - a)) % LANES, 1)
                total = jnp.where(group == b, moved, total)
        outs.append(total)
    return outs


def pack_kernel(plan, src_ref, tgt_ref, keep_ref, send_ref, stat_ref):
    c = lax.axis_index("gz")
    gs = plan.gs
    stat_ref[...] = jnp.zeros_like(stat_ref)
    for st, ref in enumerate((src_ref, tgt_ref)):
        for out, xg in ((keep_ref, c), (send_ref, 1 - c)):
            out[st] = ref[pl.ds(gs * xg, gs)].reshape(LANES, LANES).T
        stat_ref[st : st + 1, :] = jnp.sum(
            ref[...].reshape(plan.bx * plan.by, LANES), axis=0, keepdims=True
        )


def chunk_kernel(plan, keep_ref, recv_ref, stat_ref, out_ref):
    c = lax.axis_index("gz")
    half, S = plan.P // 2, plan.S
    stat = stat_ref[...]
    for part in range(half):
        low, high = plan.chip(part), plan.chip(part + half)
        for ref, to in (
            (keep_ref, jnp.where(c == 0, low, high)),
            (recv_ref, jnp.where(c == 0, high, low)),
        ):
            for st in range(2):
                out_ref[to, S * st : S * st + S, :] = ref[st, S * part : S * part + S, :]
            out_ref[to, 2 * S :, :] = stat


def unpack_kernel(plan, in_ref, out_ref):
    S, gs, XH = plan.S, plan.gs, plan.XH
    for i in range(plan.nx):
        for st in range(2):
            parts = [in_ref[i * plan.ny + j, S * st : S * st + S, :] for j in range(plan.ny)]
            for xx, value in enumerate(turn_groups(plan, parts)):
                out_ref[st * XH + i * gs + xx] = value
    total = in_ref[0, 2 * S :, :]
    for p in range(1, plan.P):
        total = total + in_ref[p, 2 * S :, :]
    out_ref[2 * XH] = jnp.zeros((S, LANES), jnp.float32)
    out_ref[2 * XH, :8, :] = total


def banded(taps, n, odd):
    row = lax.broadcasted_iota(jnp.int32, (n, n), 0)
    col = lax.broadcasted_iota(jnp.int32, (n, n), 1)
    gap = row - col
    total = jnp.zeros((n, n), jnp.float32)
    for d, tap in enumerate(taps):
        if odd:
            if d:
                total = jnp.where(gap == d, d * tap, total)
                total = jnp.where(gap == -d, -(d * tap), total)
        else:
            total = jnp.where(jnp.abs(gap) == d, tap, total)
    return total


def halves(value):
    high = value.astype(jnp.bfloat16)
    return high, (value - high.astype(jnp.float32)).astype(jnp.bfloat16)


def quad(matrix):
    high, low = halves(matrix)
    row = jnp.concatenate([high, low], axis=1)
    return jnp.concatenate([row, row], axis=0)


def lanes_times(value, quad_ref):
    high, low = halves(value)
    both = jnp.concatenate([high, low], axis=1)
    out = jnp.dot(both, quad_ref[...], preferred_element_type=jnp.float32)
    return out[:, :LANES] + out[:, LANES:]


def even_sum(load, taps, mid):
    total = taps[0] * load(mid)
    for d in range(1, len(taps)):
        total = total + taps[d] * (load(mid - d) + load(mid + d))
    return total


def odd_sum(load, taps, mid):
    total = taps[1] * (load(mid + 1) - load(mid - 1))
    for d in range(2, len(taps)):
        total = total + (d * taps[d]) * (load(mid + d) - load(mid - d))
    return total


def kernel_pass(plan, taps, quad_ref, in_ref, zb_ref, rows, emit):
    R, X = plan.R, plan.X

    def z_step(x, carry):
        zb_ref[R + x, :rows, :] = even_sum(lambda j: in_ref[x, j : j + rows, :], taps, R)
        return carry

    lax.fori_loop(0, X, z_step, 0, unroll=4)
    many = 8

    def x_step(k, carry):
        base = k * many
        parts = [
            even_sum(lambda j: zb_ref[base + q + j, :rows, :], taps, R) for q in range(many)
        ]
        out = lanes_times(jnp.concatenate(parts, axis=0), quad_ref)
        for q in range(many):
            emit(base + q, out[q * rows : (q + 1) * rows])
        return carry

    lax.fori_loop(0, X // many, x_step, 0)


def inside(plan, at, off, rows):
    z = lax.broadcasted_iota(jnp.int32, (rows, LANES), 0) + (at * plan.S - plan.H + off)
    return (z >= 0) & (z < plan.Z)


def half_steps(plan, at, taps, quad_ref, sw, tw, bufs, prev_ref, p_ref, last):
    R, S, H = plan.R, plan.S, plan.H
    u, v, zb, kb = bufs["u"], bufs["v"], bufs["zb"], bufs["kb"]
    width = S + 2 * H

    off = R
    for stage in range(2):
        rows = width - 2 * off
        mask = inside(plan, at, off, rows)

        def emit_v(x, ku, rows=rows, off=off, mask=mask, stage=stage):
            kb[:rows, :] = ku
            mine = kb[H - off : H - off + S, :]
            if stage == 0:
                p_ref[0, x] = mine if prev_ref is None else prev_ref[x] * mine
            else:
                p_ref[1, x] = v[x, H - R : H - R + S, :] * mine
            fresh = jnp.where(mask, tw[x, off : off + rows, :] / ku, 0.0)
            if stage == 0:
                v[x, :rows, :] = fresh
            else:
                bufs["v2"][x, :rows, :] = fresh

        kernel_pass(plan, taps, quad_ref, u, zb, rows, emit_v)
        off += R
        if stage == 1 and last is None:
            return
        rows = width - 2 * off
        mask = inside(plan, at, off, rows)

        def emit_u(x, kv, rows=rows, off=off, mask=mask, stage=stage):
            fresh = jnp.where(mask, sw[x, off : off + rows, :] / kv, 0.0)
            if stage == 0:
                u[x, :rows, :] = fresh
            else:
                last[x] = fresh

        kernel_pass(plan, taps, quad_ref, v if stage == 0 else bufs["v2"], zb, rows, emit_u)
        off += R


def clear_edges(ref, edge, size):
    blank = jnp.zeros((edge,) + ref.shape[1:], jnp.float32)
    ref[:edge] = blank
    ref[edge + size :] = blank


def first_kernel(plan, k_ref, own, even, odd, own2, even2, odd2, sw, tw, u_out, p_out, v_out, tot,
                 quad_ref, u, v, v2, zb, kb):
    R, S, H, X, XH, gs = plan.R, plan.S, plan.H, plan.X, plan.XH, plan.gs
    c = lax.axis_index("gz")
    at = place_of(plan)
    taps = [k_ref[d] for d in range(R + 1)]
    quad_ref[...] = quad(banded(taps, LANES, False))
    clear_edges(zb, R, X)
    tot[...] = own[2 * XH, :8, :] + own2[2 * XH, :8, :]

    def spread(low, high):
        for refs, core in (((own, low[0], high[0]), c), ((own2, low[1], high[1]), 1 - c)):
            for i in range(plan.nx):
                x = plan.bx * i + gs * core
                for st, win in ((0, sw), (1, tw)):
                    here = pl.ds(st * XH + i * gs, gs)
                    win[pl.ds(x, gs), H : H + S, :] = refs[0][here]
                    win[pl.ds(x, gs), :H, :] = refs[1][here]
                    win[pl.ds(x, gs), H + S :, :] = refs[2][here]

    @pl.when(at % 2 == 0)
    def _():
        spread((odd, odd2), (even, even2))

    @pl.when(at % 2 == 1)
    def _():
        spread((even, even2), (odd, odd2))

    def reach_sum(place, size):
        total = jnp.zeros(place.shape, jnp.float32) + taps[0]
        for d in range(1, R + 1):
            total = total + jnp.where(place - d >= 0, taps[d], 0.0)
            total = total + jnp.where(place + d < size, taps[d], 0.0)
        return total

    rows = S + 2 * H
    mask = inside(plan, at, 0, rows)
    y_at = lax.broadcasted_iota(jnp.int32, (rows, LANES), 1)
    z_at = lax.broadcasted_iota(jnp.int32, (rows, LANES), 0) + (at * S - H)
    plane = reach_sum(z_at, plan.Z) * reach_sum(y_at, plan.Y)

    def u_step(x, carry):
        cx = taps[0]
        for d in range(1, R + 1):
            cx = cx + jnp.where(x - d >= 0, taps[d], 0.0) + jnp.where(x + d < X, taps[d], 0.0)
        u[x] = jnp.where(mask, sw[x] / (plane * cx), 0.0)
        return carry

    lax.fori_loop(0, X, u_step, 0, unroll=2)
    bufs = {"u": u, "v": v, "v2": v2, "zb": zb, "kb": kb}
    half_steps(plan, at, taps, quad_ref, sw, tw, bufs, None, p_out, u_out)
    v_out[...] = v2[:, R : R + S, :]


def gather_u(plan, at, mine, side, other, u):
    c = lax.axis_index("gz")
    S, H = plan.S, plan.H
    u[:, H : H + S, :] = mine[...]
    low = jnp.where(at > 0, 1.0, 0.0)
    high = jnp.where(at < plan.P - 1, 1.0, 0.0)

    @pl.when(c == 0)
    def _():
        u[:, :H, :] = side[...] * low
        u[:, H + S :, :] = other[...] * high

    @pl.when(c == 1)
    def _():
        u[:, :H, :] = other[...] * low
        u[:, H + S :, :] = side[...] * high


def next_kernel(plan, k_ref, mine, side, other, sw, tw, prev, u_out, p_out, v_out,
                quad_ref, u, v, v2, zb, kb):
    R, S = plan.R, plan.S
    at = place_of(plan)
    taps = [k_ref[d] for d in range(R + 1)]
    quad_ref[...] = quad(banded(taps, LANES, False))
    clear_edges(zb, R, plan.X)
    gather_u(plan, at, mine, side, other, u)
    bufs = {"u": u, "v": v, "v2": v2, "zb": zb, "kb": kb}
    half_steps(plan, at, taps, quad_ref, sw, tw, bufs, prev, p_out, u_out)
    v_out[...] = v2[:, R : R + S, :]


def smooth_taps(s_ref, reach):
    total = s_ref[0]
    tail = s_ref[1]
    for d in range(2, reach + 1):
        tail = tail + s_ref[d]
    scale = 1.0 / (jnp.zeros((1, LANES), jnp.float32) + (total + 2.0 * tail))
    return [scale * s_ref[d] for d in range(reach + 1)]


def last_kernel(plan, k_ref, s_ref, mine, side, other, sw, tw, prev, p12, p34, tot, out_ref,
                quad_ref, slope_ref, smooth_ref, u, v, v2, zb, zg, kb, raw, p56):
    R, S, H, X, gs, Q = plan.R, plan.S, plan.H, plan.X, plan.gs, plan.Q
    c = lax.axis_index("gz")
    at = place_of(plan)
    taps = [k_ref[d] for d in range(R + 1)]
    stap = smooth_taps(s_ref, Q)
    quad_ref[...] = quad(banded(taps, LANES, False))
    slope_ref[...] = quad(banded(taps, LANES, True))
    smooth_ref[...] = quad(banded(stap, LANES, False))
    clear_edges(zb, R, X)
    clear_edges(zg, R, X)
    for comp in range(3):
        clear_edges(raw.at[comp], Q, X)
    gather_u(plan, at, mine, side, other, u)
    bufs = {"u": u, "v": v, "v2": v2, "zb": zb, "kb": kb}
    half_steps(plan, at, taps, quad_ref, sw, tw, bufs, prev, p56, None)

    def z_step(x, carry):
        load = lambda j: v2[x, j : j + S, :]
        zb[R + x, :S, :] = even_sum(load, taps, R)
        zg[R + x, :S, :] = odd_sum(load, taps, R)
        return carry

    lax.fori_loop(0, X, z_step, 0, unroll=4)
    many = 8

    def x_step(k, carry):
        base = k * many
        kk, gk, kg = [], [], []
        for q in range(many):
            flat = lambda j: zb[base + q + j, :S, :]
            kk.append(even_sum(flat, taps, R))
            gk.append(odd_sum(flat, taps, R))
            kg.append(even_sum(lambda j: zg[base + q + j, :S, :], taps, R))
        kk = jnp.concatenate(kk, axis=0)
        kvol = lanes_times(kk, quad_ref)
        nums = (
            lanes_times(jnp.concatenate(gk, axis=0), quad_ref),
            lanes_times(kk, slope_ref),
            lanes_times(jnp.concatenate(kg, axis=0), quad_ref),
        )
        for comp, num in enumerate(nums):
            value = num / kvol
            for q in range(many):
                raw[comp, Q + base + q] = value[q * S : (q + 1) * S]
        return carry

    lax.fori_loop(0, X // many, x_step, 0)

    for i in range(plan.nx):
        x = plan.bx * i + gs * c
        for comp in range(3):
            parts = []
            for xx in range(gs):
                parts.append(even_sum(lambda j: raw[comp, x + xx + j], stap, Q))
            flat = lanes_times(jnp.concatenate(parts, axis=0), smooth_ref)
            turned = turn_groups(plan, [flat[xx * S : (xx + 1) * S] for xx in range(gs)])
            for j in range(plan.ny):
                out_ref[i * plan.ny + j, comp * S : (comp + 1) * S, :] = turned[j]

    total = jnp.sum(tot[...], axis=1, keepdims=True)
    scale_s = plan.cells / jnp.broadcast_to(total[0:1], (1, LANES))
    scale_t = plan.cells / jnp.broadcast_to(total[1:2], (1, LANES))

    def p_step(x, carry):
        want = scale_t * tw[x, H : H + S, :]
        new = []
        for t in range(ITERS):
            ref = (p12, p34, p56)[t // 2]
            gap = jnp.abs(scale_s * ref[t % 2, x] - want)
            part = gap[:8]
            for r in range(8, S, 8):
                part = part + gap[r : r + 8]
            new.append(carry[t] + part)
        return tuple(new)

    zero = jnp.zeros((8, LANES), jnp.float32)
    gaps = lax.fori_loop(0, X, p_step, (zero,) * ITERS)
    rows = [jnp.sum(g, axis=0, keepdims=True) for g in gaps]
    rows += [jnp.zeros((1, LANES), jnp.float32)] * (8 - ITERS)
    stat = jnp.concatenate(rows, axis=0)
    for p in range(plan.P):
        out_ref[p, 3 * S :, :] = stat


def finish_kernel(plan, s_ref, in_ref, keep_ref, send_ref, mis_ref, data, out):
    S, Z, Q = plan.S, plan.Z, plan.Q
    c = lax.axis_index("gz")
    stap = smooth_taps(s_ref, Q)
    stap = [jnp.concatenate([t] * (Z // LANES), axis=1) for t in stap]
    total = in_ref[0, 3 * S :, :]
    for p in range(1, plan.P):
        total = total + in_ref[p, 3 * S :, :]
    gone = jnp.sum(total, axis=1, keepdims=True) / plan.cells
    for t in range(ITERS):
        mis_ref[t] = jnp.sum(gone[t : t + 1])
    for place in range(plan.P):
        for comp in range(3):
            data[S * place : S * place + S, comp * LANES : (comp + 1) * LANES] = in_ref[
                plan.chip(place), comp * S : (comp + 1) * S, :
            ]
    m_high, m_low = halves(banded(stap, Z, False))
    d_high, d_low = halves(data[...])
    dot = functools.partial(jnp.dot, preferred_element_type=jnp.float32)
    out[...] = dot(m_high, d_high) + (dot(m_high, d_low) + dot(m_low, d_high))
    for comp in range(3):
        lanes = slice(comp * LANES, (comp + 1) * LANES)
        keep_ref[comp] = out[pl.ds(c * LANES, LANES), lanes].T
        send_ref[comp] = out[pl.ds((1 - c) * LANES, LANES), lanes].T


def place_kernel(plan, keep_ref, recv_ref, out_ref):
    c = lax.axis_index("gz")
    gs = plan.gs
    for comp in range(3):
        out_ref[comp, pl.ds(gs * c, gs)] = keep_ref[comp].reshape(gs, plan.by, LANES)
        out_ref[comp, pl.ds(gs * (1 - c), gs)] = recv_ref[comp].reshape(gs, plan.by, LANES)


def slab_shards(plan, source, target, kernel_half, smooth_half):
    R, S, H, X, XH, Pn, Z = plan.R, plan.S, plan.H, plan.X, plan.XH, plan.P, plan.Z
    bind = lambda kernel: functools.partial(kernel, plan)
    half = f32(2, LANES, LANES)
    keep, send, stat = call(bind(pack_kernel), [half, half, f32(8, LANES)], 0, 2, name="pack")(
        source, target
    )
    recv = swap_cores(plan, send)
    (chunks,) = call(bind(chunk_kernel), [f32(Pn, 2 * S + 8, LANES)], 0, 3, name="chunks")(
        keep, recv, stat
    )
    spread = lax.all_to_all(chunks, ("gx", "gy"), 0, 0, tiled=True)
    (own,) = call(bind(unpack_kernel), [f32(2 * XH + 1, S, LANES)], 0, 1, name="unpack")(spread)
    even, odd = swap_even(plan, own), swap_odd(plan, own)
    own2 = swap_cores(plan, own)
    even2, odd2 = swap_cores(plan, even), swap_cores(plan, odd)

    wide, slab, pair = f32(X, S + 2 * H, LANES), f32(X, S, LANES), f32(2, X, S, LANES)
    vm = lambda *shape: pltpu.VMEM(shape, jnp.float32)
    quad_s = pltpu.VMEM((2 * LANES, 2 * LANES), jnp.bfloat16)
    width = S + 2 * H
    work = [vm(X, width, LANES), vm(X, width - 2 * R, LANES), vm(X, width - 6 * R, LANES)]
    zb = vm(X + 2 * R, width - 2 * R, LANES)
    kb = vm(width - 2 * R, LANES)
    sw, tw, u, p12, v, tot = call(
        bind(first_kernel), [wide, wide, slab, pair, slab, f32(8, LANES)], 1, 6,
        [quad_s, *work, zb, kb], name="first",
    )(kernel_half, own, even, odd, own2, even2, odd2)
    side = swap_sides(plan, u)
    other = swap_cores(plan, side)
    u2, p34, v = call(
        bind(next_kernel), [slab, pair, slab], 1, 6, [quad_s, *work, zb, kb], name="next"
    )(kernel_half, u, side, other, sw, tw, v)
    side = swap_sides(plan, u2)
    other = swap_cores(plan, side)
    (chunks,) = call(
        bind(last_kernel), [f32(Pn, 3 * S + 8, LANES)], 2, 9,
        [quad_s, quad_s, quad_s, *work, zb, vm(X + 2 * R, S, LANES), kb,
         vm(3, X + 2 * plan.Q, S, LANES), vm(2, X, S, LANES)],
        name="last",
    )(kernel_half, smooth_half, u2, side, other, sw, tw, v, p12, p34, tot)
    spread = lax.all_to_all(chunks, ("gx", "gy"), 0, 0, tiled=True)
    three = f32(3, LANES, LANES)
    keep, send, mismatch = call(
        bind(finish_kernel), [three, three, f32(ITERS)], 1, 1,
        [vm(Z, 3 * LANES), vm(Z, 3 * LANES)], smem_out=1, name="finish",
    )(smooth_half, spread)
    recv = swap_cores(plan, send)
    (displacement,) = call(
        bind(place_kernel), [f32(3, plan.bx, plan.by, LANES)], 0, 2, name="place"
    )(keep, recv)
    return displacement, mismatch


def shards(sizes, source, target, kernel_half, smooth_half):
    plan = Plan(sizes, *source.shape, kernel_half.shape[0] - 1, smooth_half.shape[0] - 1)
    if plan.fits():
        return slab_shards(plan, source, target, kernel_half, smooth_half)
    return block_shards(source, target, kernel_half, smooth_half)


def solution(mesh):
    in_specs = (P("gx", "gy", "gz"), P("gx", "gy", "gz"), P(), P())
    out_specs = (P(None, "gx", "gy", "gz"), P())
    body = functools.partial(shards, dict(mesh.shape))
    return jax.shard_map(body, mesh=mesh, in_specs=in_specs, out_specs=out_specs, check_vma=False)
```

```python
import functools

import jax
import jax.numpy as jnp
from jax import lax
from jax.experimental import pallas as pl
from jax.experimental.pallas import tpu as pltpu
from jax.sharding import PartitionSpec as P

ITERS = 6
LANES = 128
AXES = ("gx", "gy", "gz")


def padded_2(block, sides, width):
    for axis, dim in sides:
        count = lax.axis_size(axis)
        forward = [(i, i + 1) for i in range(count - 1)]
        backward = [(target, source) for source, target in forward]
        low = lax.ppermute(
            lax.slice_in_dim(block, block.shape[dim] - width, None, axis=dim), axis, forward
        )
        high = lax.ppermute(lax.slice_in_dim(block, 0, width, axis=dim), axis, backward)
        block = jnp.concatenate([low, block, high], axis=dim)
    return block


def full_taps(half):
    return jnp.concatenate([half[:0:-1], half])


def along(padded, taps, axis, count):
    width = taps.shape[0]
    total = taps[0] * lax.slice_in_dim(padded, 0, count, axis=axis)
    for j in range(1, width):
        total = total + taps[j] * lax.slice_in_dim(padded, j, j + count, axis=axis)
    return total


def three_passes(padded, taps, size_x, size_y, size_z):
    padded = along(padded, taps, 0, size_x)
    padded = along(padded, taps, 1, size_y)
    return along(padded, taps, 2, size_z)


def block_shards(source, target, kernel_half, smooth_half):
    kern = full_taps(kernel_half)
    radius = kernel_half.shape[0] - 1
    reach = smooth_half.shape[0] - 1
    offsets = jnp.arange(-radius, radius + 1).astype(jnp.float32)
    slope = offsets * kern
    norm_total = smooth_half[0] + 2.0 * jnp.sum(smooth_half[1:])
    smooth = full_taps(smooth_half) / norm_total
    size_x, size_y, size_z = source.shape
    cells = float(source.size * lax.axis_size("gx") * lax.axis_size("gy") * lax.axis_size("gz"))
    totals = lax.psum((jnp.sum(source), jnp.sum(target)), AXES)
    first = source * (cells / totals[0])
    second = target * (cells / totals[1])
    first_wide = padded_2(first, (("gx", 0), ("gy", 1), ("gz", 2)), radius)
    scaling_v = jnp.ones_like(source)
    errors = []
    for step in range(ITERS):
        padded = padded_2(scaling_v, (("gx", 0), ("gy", 1), ("gz", 2)), 2 * radius)
        kv_wide = three_passes(
            padded, kern, size_x + 2 * radius, size_y + 2 * radius, size_z + 2 * radius
        )
        u_wide = first_wide / kv_wide
        ku = three_passes(u_wide, kern, size_x, size_y, size_z)
        local_err = jnp.sum(jnp.abs(scaling_v * ku - second))
        errors.append(lax.psum(local_err, AXES) / cells)
        scaling_v = second / ku
    mismatch = jnp.stack(errors)
    padded = padded_2(scaling_v, (("gx", 0), ("gy", 1), ("gz", 2)), radius)
    pass_k = along(padded, kern, 0, size_x)
    pass_g = along(padded, slope, 0, size_x)
    kk = along(pass_k, kern, 1, size_y)
    kg = along(pass_k, slope, 1, size_y)
    gk = along(pass_g, kern, 1, size_y)
    kvol = along(kk, kern, 2, size_z)
    znum = along(kk, slope, 2, size_z)
    ynum = along(kg, kern, 2, size_z)
    xnum = along(gk, kern, 2, size_z)
    raw = jnp.stack([xnum, ynum, znum]) / kvol
    padded = padded_2(raw, (("gx", 1), ("gy", 2), ("gz", 3)), reach)
    padded = along(padded, smooth, 1, size_x)
    padded = along(padded, smooth, 2, size_y)
    displacement = along(padded, smooth, 3, size_z)
    return (displacement, mismatch)


class Plan:
    def __init__(self, mesh, bx, by, bz, radius, reach):
        self.nx, self.ny, self.nc = mesh["gx"], mesh["gy"], mesh["gz"]
        self.bx, self.by, self.bz = bx, by, bz
        self.R, self.Q = radius, reach
        self.P = self.nx * self.ny
        self.X, self.Y, self.Z = bx * self.nx, by * self.ny, bz * self.nc
        self.S = self.Z // self.P
        self.H = 4 * radius
        self.gs = LANES // by if by <= LANES else 0
        self.XH = self.X // 2
        self.cells = float(self.X * self.Y * self.Z)

    def fits(self):
        return (
            self.nc == 2
            and self.ny >= 2
            and self.ny & (self.ny - 1) == 0
            and self.nx >= 2
            and self.bz == LANES
            and self.Y == LANES
            and self.gs == self.ny
            and self.bx == 2 * self.gs
            and self.Z == self.P * self.S
            and self.S == self.H
            and self.S % 8 == 0
            and self.R % 4 == 0
            and ITERS == 6
        )

    def spot(self, at):
        at %= self.P
        col, q = divmod(at, self.nx)
        return (q if col % 2 == 0 else self.nx - 1 - q), col ^ (col >> 1)

    def chip(self, at):
        i, j = self.spot(at)
        return i * self.ny + j

    def device(self, at, core):
        return self.chip(at) * self.nc + core


def swap_cores(plan, value):
    pairs = [(plan.device(at, c), plan.device(at, 1 - c)) for at in range(plan.P) for c in range(2)]
    return lax.ppermute(value, AXES, pairs)


def swap_even(plan, value):
    pairs = [(plan.device(at, c), plan.device(at ^ 1, c)) for at in range(plan.P) for c in range(2)]
    return lax.ppermute(value, AXES, pairs)


def swap_odd(plan, value):
    pairs = [
        (plan.device(at, c), plan.device(((at + 1) ^ 1) - 1, c))
        for at in range(plan.P)
        for c in range(2)
    ]
    return lax.ppermute(value, AXES, pairs)


def swap_sides(plan, value):
    pairs = [(plan.device(at, 0), plan.device(at - 1, 1)) for at in range(plan.P)]
    pairs += [(plan.device(at, 1), plan.device(at + 1, 0)) for at in range(plan.P)]
    return lax.ppermute(value, AXES, pairs)


def place_of(plan):
    i, j = lax.axis_index("gx"), lax.axis_index("gy")
    at = jnp.int32(0)
    for place in range(plan.P):
        a, b = plan.spot(place)
        at = at + jnp.where((i == a) & (j == b), place, 0)
    return at.astype(jnp.int32)


def call(kernel, out_shape, n_smem, n_vmem, scratch=(), smem_out=0, n_any=0, name=None):
    vm, sm = pl.BlockSpec(memory_space=pltpu.VMEM), pl.BlockSpec(memory_space=pltpu.SMEM)
    hbm = pl.BlockSpec(memory_space=pltpu.HBM)
    out_specs = [vm] * (len(out_shape) - smem_out) + [sm] * smem_out
    return pl.pallas_call(
        kernel,
        out_shape=out_shape,
        in_specs=[sm] * n_smem + [vm] * n_vmem + [hbm] * n_any,
        out_specs=out_specs,
        scratch_shapes=list(scratch),
        compiler_params=pltpu.CompilerParams(vmem_limit_bytes=48 << 20),
        name=name,
    )


def f32(*shape):
    return jax.ShapeDtypeStruct(shape, jnp.float32)


def turn_groups(plan, parts):
    n, w = plan.gs, plan.by
    group = lax.broadcasted_iota(jnp.int32, parts[0].shape, 1) // w
    outs = []
    for a in range(n):
        total = parts[a]
        for b in range(n):
            if b != a:
                moved = pltpu.roll(parts[b], (w * (b - a)) % LANES, 1)
                total = jnp.where(group == b, moved, total)
        outs.append(total)
    return outs


def pack_kernel(plan, src_hbm, tgt_hbm, keep_ref, send_ref, stat_ref, src_ref, tgt_ref, sems):
    c = lax.axis_index("gz")
    gs = plan.gs
    copies = [
        pltpu.make_async_copy(src_hbm, src_ref, sems.at[0]),
        pltpu.make_async_copy(tgt_hbm, tgt_ref, sems.at[1]),
    ]
    for copy in copies:
        copy.start()
    stat_ref[...] = jnp.zeros_like(stat_ref)
    for st, ref in enumerate((src_ref, tgt_ref)):
        copies[st].wait()
        for out, xg in ((keep_ref, c), (send_ref, 1 - c)):
            out[st] = ref[pl.ds(gs * xg, gs)].reshape(LANES, LANES).T
        stat_ref[st : st + 1, :] = jnp.sum(
            ref[...].reshape(plan.bx * plan.by, LANES), axis=0, keepdims=True
        )


def chunk_kernel(plan, keep_ref, recv_ref, stat_ref, out_ref):
    c = lax.axis_index("gz")
    half, S = plan.P // 2, plan.S
    stat = stat_ref[...]
    for part in range(half):
        low, high = plan.chip(part), plan.chip(part + half)
        for ref, to in (
            (keep_ref, jnp.where(c == 0, low, high)),
            (recv_ref, jnp.where(c == 0, high, low)),
        ):
            for st in range(2):
                out_ref[to, S * st : S * st + S, :] = ref[st, S * part : S * part + S, :]
            out_ref[to, 2 * S :, :] = stat


def unpack_kernel(plan, in_ref, out_ref):
    S, gs, XH = plan.S, plan.gs, plan.XH
    for i in range(plan.nx):
        for st in range(2):
            parts = [in_ref[i * plan.ny + j, S * st : S * st + S, :] for j in range(plan.ny)]
            for xx, value in enumerate(turn_groups(plan, parts)):
                out_ref[st * XH + i * gs + xx] = value
    total = in_ref[0, 2 * S :, :]
    for p in range(1, plan.P):
        total = total + in_ref[p, 2 * S :, :]
    out_ref[2 * XH] = jnp.zeros((S, LANES), jnp.float32)
    out_ref[2 * XH, :8, :] = total


def banded(taps, n, odd):
    row = lax.broadcasted_iota(jnp.int32, (n, n), 0)
    col = lax.broadcasted_iota(jnp.int32, (n, n), 1)
    gap = row - col
    total = jnp.zeros((n, n), jnp.float32)
    for d, tap in enumerate(taps):
        if odd:
            if d:
                total = jnp.where(gap == d, d * tap, total)
                total = jnp.where(gap == -d, -(d * tap), total)
        else:
            total = jnp.where(jnp.abs(gap) == d, tap, total)
    return total


def halves(value):
    high = value.astype(jnp.bfloat16)
    return high, (value - high.astype(jnp.float32)).astype(jnp.bfloat16)


def quad(matrix):
    high, low = halves(matrix)
    row = jnp.concatenate([high, low], axis=1)
    return jnp.concatenate([row, row], axis=0)


def lanes_times(value, quad_ref):
    high, low = halves(value)
    both = jnp.concatenate([high, low], axis=1)
    out = jnp.dot(both, quad_ref[...], preferred_element_type=jnp.float32)
    return out[:, :LANES] + out[:, LANES:]


def even_sum(load, taps, mid):
    total = taps[0] * load(mid)
    for d in range(1, len(taps)):
        total = total + taps[d] * (load(mid - d) + load(mid + d))
    return total


def odd_sum(load, taps, mid):
    total = taps[1] * (load(mid + 1) - load(mid - 1))
    for d in range(2, len(taps)):
        total = total + (d * taps[d]) * (load(mid + d) - load(mid - d))
    return total


def kernel_pass(plan, taps, quad_ref, in_ref, zb_ref, rows, emit):
    R, X = plan.R, plan.X

    def z_step(x, carry):
        zb_ref[R + x, :rows, :] = even_sum(lambda j: in_ref[x, j : j + rows, :], taps, R)
        return carry

    lax.fori_loop(0, X, z_step, 0, unroll=4)
    many = 8

    def x_step(k, carry):
        base = k * many
        parts = [
            even_sum(lambda j: zb_ref[base + q + j, :rows, :], taps, R) for q in range(many)
        ]
        out = lanes_times(jnp.concatenate(parts, axis=0), quad_ref)
        for q in range(many):
            emit(base + q, out[q * rows : (q + 1) * rows])
        return carry

    for k in range(X // many):
        x_step(k, 0)


def inside(plan, at, off, rows):
    z = lax.broadcasted_iota(jnp.int32, (rows, LANES), 0) + (at * plan.S - plan.H + off)
    return (z >= 0) & (z < plan.Z)


def half_steps(plan, at, taps, quad_ref, sw, tw, bufs, prev_ref, p_ref, last):
    R, S, H = plan.R, plan.S, plan.H
    u, v, zb, kb = bufs["u"], bufs["v"], bufs["zb"], bufs["kb"]
    width = S + 2 * H

    off = R
    for stage in range(2):
        rows = width - 2 * off
        mask = inside(plan, at, off, rows)

        def emit_v(x, ku, rows=rows, off=off, mask=mask, stage=stage):
            kb[:rows, :] = ku
            mine = kb[H - off : H - off + S, :]
            if stage == 0:
                p_ref[0, x] = mine if prev_ref is None else prev_ref[x] * mine
            else:
                p_ref[1, x] = v[x, H - R : H - R + S, :] * mine
            fresh = jnp.where(mask, tw[x, off : off + rows, :] / ku, 0.0)
            if stage == 0:
                v[x, :rows, :] = fresh
            else:
                bufs["v2"][x, :rows, :] = fresh

        kernel_pass(plan, taps, quad_ref, u, zb, rows, emit_v)
        off += R
        if stage == 1 and last is None:
            return
        rows = width - 2 * off
        mask = inside(plan, at, off, rows)

        def emit_u(x, kv, rows=rows, off=off, mask=mask, stage=stage):
            fresh = jnp.where(mask, sw[x, off : off + rows, :] / kv, 0.0)
            if stage == 0:
                u[x, :rows, :] = fresh
            else:
                last[x] = fresh

        kernel_pass(plan, taps, quad_ref, v if stage == 0 else bufs["v2"], zb, rows, emit_u)
        off += R


def clear_edges(ref, edge, size):
    blank = jnp.zeros((edge,) + ref.shape[1:], jnp.float32)
    ref[:edge] = blank
    ref[edge + size :] = blank


def prep_kernel(plan, k_ref, s_ref, own, taps_ref, quad_ref, slope_ref, smooth_ref, high_ref, low_ref):
    del own
    R, Q = plan.R, plan.Q
    taps = [k_ref[d] for d in range(R + 1)]
    stap = smooth_taps(s_ref, Q)
    for d in range(R + 1):
        taps_ref[d] = jnp.zeros((8, LANES), jnp.float32) + taps[d]
    for d in range(Q + 1):
        taps_ref[R + 1 + d] = jnp.broadcast_to(stap[d], (8, LANES))
    quad_ref[...] = quad(banded(taps, LANES, False))
    slope_ref[...] = quad(banded(taps, LANES, True))
    smooth_ref[...] = quad(banded(stap, LANES, False))
    wide = [jnp.concatenate([t] * (plan.Z // LANES), axis=1) for t in stap]
    high_ref[...], low_ref[...] = halves(banded(wide, plan.Z, False))


def kernel_taps(plan, taps_ref):
    return [taps_ref[d, :1, :] for d in range(plan.R + 1)]


def gaps_of(plan, tot, tw, refs):
    S, H = plan.S, plan.H
    total = jnp.sum(tot[...], axis=1, keepdims=True)
    scale_s = plan.cells / jnp.broadcast_to(total[0:1], (1, LANES))
    scale_t = plan.cells / jnp.broadcast_to(total[1:2], (1, LANES))

    def p_step(x, carry):
        want = scale_t * tw[x, H : H + S, :]
        new = []
        for t, part in enumerate(carry):
            gap = jnp.abs(scale_s * refs[t // 2][t % 2, x] - want)
            for r in range(0, S, 8):
                part = part + gap[r : r + 8]
            new.append(part)
        return tuple(new)

    zero = jnp.zeros((8, LANES), jnp.float32)
    gaps = lax.fori_loop(0, plan.X, p_step, (zero,) * (2 * len(refs)), unroll=4)
    return [jnp.sum(g, axis=0, keepdims=True) for g in gaps]


def gaps_kernel(plan, tot, tw, p12, p34, out_ref):
    rows = gaps_of(plan, tot, tw, (p12, p34))
    out_ref[...] = jnp.concatenate(rows + [jnp.zeros((8 - len(rows), LANES), jnp.float32)], axis=0)


def first_kernel(plan, taps_ref, quad_ref, own, even, odd, own2, even2, odd2,
                 sw, tw, u_out, p_out, v_out, tot, u, v, v2, zb, kb):
    R, S, H, X, XH, gs = plan.R, plan.S, plan.H, plan.X, plan.XH, plan.gs
    c = lax.axis_index("gz")
    at = place_of(plan)
    taps = kernel_taps(plan, taps_ref)
    clear_edges(zb, R, X)
    tot[...] = own[2 * XH, :8, :] + own2[2 * XH, :8, :]

    def spread(low, high):
        for refs, core in (((own, low[0], high[0]), c), ((own2, low[1], high[1]), 1 - c)):
            for i in range(plan.nx):
                x = plan.bx * i + gs * core
                for st, win in ((0, sw), (1, tw)):
                    here = pl.ds(st * XH + i * gs, gs)
                    win[pl.ds(x, gs), H : H + S, :] = refs[0][here]
                    win[pl.ds(x, gs), :H, :] = refs[1][here]
                    win[pl.ds(x, gs), H + S :, :] = refs[2][here]

    @pl.when(at % 2 == 0)
    def _():
        spread((odd, odd2), (even, even2))

    @pl.when(at % 2 == 1)
    def _():
        spread((even, even2), (odd, odd2))

    def reach_sum(place, size):
        total = jnp.zeros(place.shape, jnp.float32) + taps[0]
        for d in range(1, R + 1):
            total = total + jnp.where(place - d >= 0, taps[d], 0.0)
            total = total + jnp.where(place + d < size, taps[d], 0.0)
        return total

    rows = S + 2 * H
    mask = inside(plan, at, 0, rows)
    y_at = lax.broadcasted_iota(jnp.int32, (rows, LANES), 1)
    z_at = lax.broadcasted_iota(jnp.int32, (rows, LANES), 0) + (at * S - H)
    plane = reach_sum(z_at, plan.Z) * reach_sum(y_at, plan.Y)

    def u_step(x, carry):
        cx = taps[0]
        for d in range(1, R + 1):
            cx = cx + jnp.where(x - d >= 0, taps[d], 0.0) + jnp.where(x + d < X, taps[d], 0.0)
        u[x] = jnp.where(mask, sw[x] / (plane * cx), 0.0)
        return carry

    lax.fori_loop(0, X, u_step, 0, unroll=2)
    bufs = {"u": u, "v": v, "v2": v2, "zb": zb, "kb": kb}
    half_steps(plan, at, taps, quad_ref, sw, tw, bufs, None, p_out, u_out)
    v_out[...] = v2[:, R : R + S, :]


def gather_u(plan, at, mine, side, other, u):
    c = lax.axis_index("gz")
    S, H = plan.S, plan.H
    u[:, H : H + S, :] = mine[...]
    low = jnp.where(at > 0, 1.0, 0.0)
    high = jnp.where(at < plan.P - 1, 1.0, 0.0)

    @pl.when(c == 0)
    def _():
        u[:, :H, :] = side[...] * low
        u[:, H + S :, :] = other[...] * high

    @pl.when(c == 1)
    def _():
        u[:, :H, :] = other[...] * low
        u[:, H + S :, :] = side[...] * high


def next_kernel(plan, taps_ref, quad_ref, mine, side, other, sw, tw, prev, u_out, p_out, v_out,
                u, v, v2, zb, kb):
    R, S = plan.R, plan.S
    at = place_of(plan)
    taps = kernel_taps(plan, taps_ref)
    clear_edges(zb, R, plan.X)
    gather_u(plan, at, mine, side, other, u)
    bufs = {"u": u, "v": v, "v2": v2, "zb": zb, "kb": kb}
    half_steps(plan, at, taps, quad_ref, sw, tw, bufs, prev, p_out, u_out)
    v_out[...] = v2[:, R : R + S, :]


def smooth_taps(s_ref, reach):
    total = s_ref[0]
    tail = s_ref[1]
    for d in range(2, reach + 1):
        tail = tail + s_ref[d]
    scale = 1.0 / (jnp.zeros((1, LANES), jnp.float32) + (total + 2.0 * tail))
    return [scale * s_ref[d] for d in range(reach + 1)]


def last_kernel(plan, taps_ref, quad_ref, slope_ref, smooth_ref, mine, side, other, sw, tw, prev,
                gaps, tot, out_ref, u, v, v2, zb, zg, kb, raw, p56):
    R, S, H, X, gs, Q = plan.R, plan.S, plan.H, plan.X, plan.gs, plan.Q
    c = lax.axis_index("gz")
    at = place_of(plan)
    taps = kernel_taps(plan, taps_ref)
    stap = [taps_ref[R + 1 + d, :1, :] for d in range(Q + 1)]
    clear_edges(zb, R, X)
    clear_edges(zg, R, X)
    for comp in range(3):
        clear_edges(raw.at[comp], Q, X)
    gather_u(plan, at, mine, side, other, u)
    bufs = {"u": u, "v": v, "v2": v2, "zb": zb, "kb": kb}
    half_steps(plan, at, taps, quad_ref, sw, tw, bufs, prev, p56, None)

    def z_step(x, carry):
        load = lambda j: v2[x, j : j + S, :]
        zb[R + x, :S, :] = even_sum(load, taps, R)
        zg[R + x, :S, :] = odd_sum(load, taps, R)
        return carry

    lax.fori_loop(0, X, z_step, 0, unroll=4)
    many = 8

    def x_step(k, carry):
        base = k * many
        kk, gk, kg = [], [], []
        for q in range(many):
            flat = lambda j: zb[base + q + j, :S, :]
            kk.append(even_sum(flat, taps, R))
            gk.append(odd_sum(flat, taps, R))
            kg.append(even_sum(lambda j: zg[base + q + j, :S, :], taps, R))
        kk = jnp.concatenate(kk, axis=0)
        kvol = lanes_times(kk, quad_ref)
        nums = (
            lanes_times(jnp.concatenate(gk, axis=0), quad_ref),
            lanes_times(kk, slope_ref),
            lanes_times(jnp.concatenate(kg, axis=0), quad_ref),
        )
        for comp, num in enumerate(nums):
            value = num / kvol
            for q in range(many):
                raw[comp, Q + base + q] = value[q * S : (q + 1) * S]
        return carry

    for k in range(X // many):
        x_step(k, 0)

    for i in range(plan.nx):
        x = plan.bx * i + gs * c
        for comp in range(3):
            parts = []
            for xx in range(gs):
                parts.append(even_sum(lambda j: raw[comp, x + xx + j], stap, Q))
            flat = lanes_times(jnp.concatenate(parts, axis=0), smooth_ref)
            turned = turn_groups(plan, [flat[xx * S : (xx + 1) * S] for xx in range(gs)])
            for j in range(plan.ny):
                out_ref[i * plan.ny + j, comp * S : (comp + 1) * S, :] = turned[j]

    rows = gaps_of(plan, tot, tw, (p56,))
    blank = jnp.zeros((8 - ITERS, LANES), jnp.float32)
    stat = jnp.concatenate([gaps[: ITERS - 2, :], *rows, blank], axis=0)
    for p in range(plan.P):
        out_ref[p, 3 * S :, :] = stat


def finish_kernel(plan, high_ref, low_ref, in_ref, keep_ref, send_ref, mis_ref, data, out):
    S = plan.S
    c = lax.axis_index("gz")
    total = in_ref[0, 3 * S :, :]
    for p in range(1, plan.P):
        total = total + in_ref[p, 3 * S :, :]
    gone = jnp.sum(total, axis=1, keepdims=True) / plan.cells
    for t in range(ITERS):
        mis_ref[t] = jnp.sum(gone[t : t + 1])
    for place in range(plan.P):
        for comp in range(3):
            data[S * place : S * place + S, comp * LANES : (comp + 1) * LANES] = in_ref[
                plan.chip(place), comp * S : (comp + 1) * S, :
            ]
    m_high, m_low = high_ref[...], low_ref[...]
    d_high, d_low = halves(data[...])
    dot = functools.partial(jnp.dot, preferred_element_type=jnp.float32)
    out[...] = dot(m_high, d_high) + (dot(m_high, d_low) + dot(m_low, d_high))
    for comp in range(3):
        lanes = slice(comp * LANES, (comp + 1) * LANES)
        keep_ref[comp] = out[pl.ds(c * LANES, LANES), lanes].T
        send_ref[comp] = out[pl.ds((1 - c) * LANES, LANES), lanes].T


def place_kernel(plan, keep_ref, recv_ref, out_ref):
    c = lax.axis_index("gz")
    gs = plan.gs
    for comp in range(3):
        out_ref[comp, pl.ds(gs * c, gs)] = keep_ref[comp].reshape(gs, plan.by, LANES)
        out_ref[comp, pl.ds(gs * (1 - c), gs)] = recv_ref[comp].reshape(gs, plan.by, LANES)


def slab_shards(plan, source, target, kernel_half, smooth_half):
    R, S, H, X, XH, Pn, Z = plan.R, plan.S, plan.H, plan.X, plan.XH, plan.P, plan.Z
    bind = lambda kernel: functools.partial(kernel, plan)
    half = f32(2, LANES, LANES)
    vm = lambda *shape: pltpu.VMEM(shape, jnp.float32)
    keep, send, stat = call(
        bind(pack_kernel), [half, half, f32(8, LANES)], 0, 0,
        [vm(*source.shape), vm(*source.shape), pltpu.SemaphoreType.DMA((2,))], n_any=2, name="pack",
    )(source, target)
    recv = swap_cores(plan, send)
    (chunks,) = call(bind(chunk_kernel), [f32(Pn, 2 * S + 8, LANES)], 0, 3, name="chunks")(
        keep, recv, stat
    )
    spread = lax.all_to_all(chunks, ("gx", "gy"), 0, 0, tiled=True)
    (own,) = call(bind(unpack_kernel), [f32(2 * XH + 1, S, LANES)], 0, 1, name="unpack")(spread)
    square = jax.ShapeDtypeStruct((2 * LANES, 2 * LANES), jnp.bfloat16)
    table = jax.ShapeDtypeStruct((Z, Z), jnp.bfloat16)
    taps, quad_k, quad_g, quad_s, high, low = call(
        bind(prep_kernel), [f32(plan.R + plan.Q + 2, 8, LANES), square, square, square, table, table],
        2, 0, n_any=1, name="prep",
    )(kernel_half, smooth_half, own)
    even, odd = swap_even(plan, own), swap_odd(plan, own)
    own2 = swap_cores(plan, own)
    even, odd, taps = lax.optimization_barrier((even, odd, taps))
    even2, odd2 = swap_cores(plan, even), swap_cores(plan, odd)

    wide, slab, pair = f32(X, S + 2 * H, LANES), f32(X, S, LANES), f32(2, X, S, LANES)
    width = S + 2 * H
    work = [vm(X, width, LANES), vm(X, width - 2 * R, LANES), vm(X, width - 6 * R, LANES)]
    zb = vm(X + 2 * R, width - 2 * R, LANES)
    kb = vm(width - 2 * R, LANES)
    sw, tw, u, p12, v, tot = call(
        bind(first_kernel), [wide, wide, slab, pair, slab, f32(8, LANES)], 0, 8,
        [*work, zb, kb], name="first",
    )(taps, quad_k, own, even, odd, own2, even2, odd2)
    side = swap_sides(plan, u)
    other = swap_cores(plan, side)
    u2, p34, v = call(
        bind(next_kernel), [slab, pair, slab], 0, 8, [*work, zb, kb], name="next"
    )(taps, quad_k, u, side, other, sw, tw, v)
    side = swap_sides(plan, u2)
    (gaps,) = call(bind(gaps_kernel), [f32(8, LANES)], 0, 4, name="gaps")(tot, tw, p12, p34)
    side, gaps = lax.optimization_barrier((side, gaps))
    other = swap_cores(plan, side)
    (chunks,) = call(
        bind(last_kernel), [f32(Pn, 3 * S + 8, LANES)], 0, 12,
        [*work, zb, vm(X + 2 * R, S, LANES), kb,
         vm(3, X + 2 * plan.Q, S, LANES), vm(2, X, S, LANES)],
        name="last",
    )(taps, quad_k, quad_g, quad_s, u2, side, other, sw, tw, v, gaps, tot)
    spread = lax.all_to_all(chunks, ("gx", "gy"), 0, 0, tiled=True)
    three = f32(3, LANES, LANES)
    keep, send, mismatch = call(
        bind(finish_kernel), [three, three, f32(ITERS)], 0, 3,
        [vm(Z, 3 * LANES), vm(Z, 3 * LANES)], smem_out=1, name="finish",
    )(high, low, spread)
    recv = swap_cores(plan, send)
    (displacement,) = call(
        bind(place_kernel), [f32(3, plan.bx, plan.by, LANES)], 0, 2, name="place"
    )(keep, recv)
    return displacement, mismatch


def shards(sizes, source, target, kernel_half, smooth_half):
    plan = Plan(sizes, *source.shape, kernel_half.shape[0] - 1, smooth_half.shape[0] - 1)
    if plan.fits():
        return slab_shards(plan, source, target, kernel_half, smooth_half)
    return block_shards(source, target, kernel_half, smooth_half)


def solution(mesh):
    in_specs = (P("gx", "gy", "gz"), P("gx", "gy", "gz"), P(), P())
    out_specs = (P(None, "gx", "gy", "gz"), P())
    body = functools.partial(shards, dict(mesh.shape))
    return jax.shard_map(body, mesh=mesh, in_specs=in_specs, out_specs=out_specs, check_vma=False)
```

```python
import functools

import jax
import jax.numpy as jnp
from jax import lax
from jax.experimental import pallas as pl
from jax.experimental.pallas import tpu as pltpu
from jax.sharding import PartitionSpec as P

ITERS = 6
LANES = 128
AXES = ("gx", "gy", "gz")


def padded_2(block, sides, width):
    for axis, dim in sides:
        count = lax.axis_size(axis)
        forward = [(i, i + 1) for i in range(count - 1)]
        backward = [(target, source) for source, target in forward]
        low = lax.ppermute(
            lax.slice_in_dim(block, block.shape[dim] - width, None, axis=dim), axis, forward
        )
        high = lax.ppermute(lax.slice_in_dim(block, 0, width, axis=dim), axis, backward)
        block = jnp.concatenate([low, block, high], axis=dim)
    return block


def full_taps(half):
    return jnp.concatenate([half[:0:-1], half])


def along(padded, taps, axis, count):
    width = taps.shape[0]
    total = taps[0] * lax.slice_in_dim(padded, 0, count, axis=axis)
    for j in range(1, width):
        total = total + taps[j] * lax.slice_in_dim(padded, j, j + count, axis=axis)
    return total


def three_passes(padded, taps, size_x, size_y, size_z):
    padded = along(padded, taps, 0, size_x)
    padded = along(padded, taps, 1, size_y)
    return along(padded, taps, 2, size_z)


def block_shards(source, target, kernel_half, smooth_half):
    kern = full_taps(kernel_half)
    radius = kernel_half.shape[0] - 1
    reach = smooth_half.shape[0] - 1
    offsets = jnp.arange(-radius, radius + 1).astype(jnp.float32)
    slope = offsets * kern
    norm_total = smooth_half[0] + 2.0 * jnp.sum(smooth_half[1:])
    smooth = full_taps(smooth_half) / norm_total
    size_x, size_y, size_z = source.shape
    cells = float(source.size * lax.axis_size("gx") * lax.axis_size("gy") * lax.axis_size("gz"))
    totals = lax.psum((jnp.sum(source), jnp.sum(target)), AXES)
    first = source * (cells / totals[0])
    second = target * (cells / totals[1])
    first_wide = padded_2(first, (("gx", 0), ("gy", 1), ("gz", 2)), radius)
    scaling_v = jnp.ones_like(source)
    errors = []
    for step in range(ITERS):
        padded = padded_2(scaling_v, (("gx", 0), ("gy", 1), ("gz", 2)), 2 * radius)
        kv_wide = three_passes(
            padded, kern, size_x + 2 * radius, size_y + 2 * radius, size_z + 2 * radius
        )
        u_wide = first_wide / kv_wide
        ku = three_passes(u_wide, kern, size_x, size_y, size_z)
        local_err = jnp.sum(jnp.abs(scaling_v * ku - second))
        errors.append(lax.psum(local_err, AXES) / cells)
        scaling_v = second / ku
    mismatch = jnp.stack(errors)
    padded = padded_2(scaling_v, (("gx", 0), ("gy", 1), ("gz", 2)), radius)
    pass_k = along(padded, kern, 0, size_x)
    pass_g = along(padded, slope, 0, size_x)
    kk = along(pass_k, kern, 1, size_y)
    kg = along(pass_k, slope, 1, size_y)
    gk = along(pass_g, kern, 1, size_y)
    kvol = along(kk, kern, 2, size_z)
    znum = along(kk, slope, 2, size_z)
    ynum = along(kg, kern, 2, size_z)
    xnum = along(gk, kern, 2, size_z)
    raw = jnp.stack([xnum, ynum, znum]) / kvol
    padded = padded_2(raw, (("gx", 1), ("gy", 2), ("gz", 3)), reach)
    padded = along(padded, smooth, 1, size_x)
    padded = along(padded, smooth, 2, size_y)
    displacement = along(padded, smooth, 3, size_z)
    return (displacement, mismatch)


class Plan:
    def __init__(self, mesh, bx, by, bz, radius, reach):
        self.nx, self.ny, self.nc = mesh["gx"], mesh["gy"], mesh["gz"]
        self.bx, self.by, self.bz = bx, by, bz
        self.R, self.Q = radius, reach
        self.P = self.nx * self.ny
        self.X, self.Y, self.Z = bx * self.nx, by * self.ny, bz * self.nc
        self.S = self.Z // self.P
        self.H = 4 * radius
        self.gs = LANES // by if by <= LANES else 0
        self.XH = self.X // 2
        self.cells = float(self.X * self.Y * self.Z)

    def fits(self):
        return (
            self.nc == 2
            and self.ny >= 2
            and self.ny & (self.ny - 1) == 0
            and self.nx >= 2
            and self.bz == LANES
            and self.Y == LANES
            and self.gs == self.ny
            and self.bx == 2 * self.gs
            and self.Z == self.P * self.S
            and self.S == self.H
            and self.S % 8 == 0
            and self.R % 4 == 0
            and ITERS == 6
        )

    def spot(self, at):
        at %= self.P
        col, q = divmod(at, self.nx)
        return (q if col % 2 == 0 else self.nx - 1 - q), col ^ (col >> 1)

    def chip(self, at):
        i, j = self.spot(at)
        return i * self.ny + j

    def device(self, at, core):
        return self.chip(at) * self.nc + core


def swap_cores(plan, value):
    pairs = [(plan.device(at, c), plan.device(at, 1 - c)) for at in range(plan.P) for c in range(2)]
    return lax.ppermute(value, AXES, pairs)


def swap_even(plan, value):
    pairs = [(plan.device(at, c), plan.device(at ^ 1, c)) for at in range(plan.P) for c in range(2)]
    return lax.ppermute(value, AXES, pairs)


def swap_odd(plan, value):
    pairs = [
        (plan.device(at, c), plan.device(((at + 1) ^ 1) - 1, c))
        for at in range(plan.P)
        for c in range(2)
    ]
    return lax.ppermute(value, AXES, pairs)


def swap_sides(plan, value):
    pairs = [(plan.device(at, 0), plan.device(at - 1, 1)) for at in range(plan.P)]
    pairs += [(plan.device(at, 1), plan.device(at + 1, 0)) for at in range(plan.P)]
    return lax.ppermute(value, AXES, pairs)


def trade_chunks(value):
    rows, lanes = value.shape
    out = lax.all_to_all(value.reshape(rows, 1, lanes), ("gx", "gy"), 0, 0, tiled=True)
    return out.reshape(rows, lanes)


def place_of(plan):
    i, j = lax.axis_index("gx"), lax.axis_index("gy")
    at = jnp.int32(0)
    for place in range(plan.P):
        a, b = plan.spot(place)
        at = at + jnp.where((i == a) & (j == b), place, 0)
    return at.astype(jnp.int32)


def call(kernel, out_shape, n_smem, n_vmem, scratch=(), smem_out=0, n_any=0, name=None):
    vm, sm = pl.BlockSpec(memory_space=pltpu.VMEM), pl.BlockSpec(memory_space=pltpu.SMEM)
    hbm = pl.BlockSpec(memory_space=pltpu.HBM)
    out_specs = [vm] * (len(out_shape) - smem_out) + [sm] * smem_out
    return pl.pallas_call(
        kernel,
        out_shape=out_shape,
        in_specs=[sm] * n_smem + [vm] * n_vmem + [hbm] * n_any,
        out_specs=out_specs,
        scratch_shapes=list(scratch),
        compiler_params=pltpu.CompilerParams(vmem_limit_bytes=48 << 20),
        name=name,
    )


def f32(*shape):
    return jax.ShapeDtypeStruct(shape, jnp.float32)


def turn_groups(plan, parts):
    n, w = plan.gs, plan.by
    group = lax.broadcasted_iota(jnp.int32, parts[0].shape, 1) // w
    outs = []
    for a in range(n):
        total = parts[a]
        for b in range(n):
            if b != a:
                moved = pltpu.roll(parts[b], (w * (b - a)) % LANES, 1)
                total = jnp.where(group == b, moved, total)
        outs.append(total)
    return outs


def pack_kernel(plan, src_hbm, tgt_hbm, keep_ref, send_ref, stat_ref, src_ref, tgt_ref, sems):
    c = lax.axis_index("gz")
    gs = plan.gs
    copies = [
        pltpu.make_async_copy(src_hbm, src_ref, sems.at[0]),
        pltpu.make_async_copy(tgt_hbm, tgt_ref, sems.at[1]),
    ]
    for copy in copies:
        copy.start()
    sums = []
    for st, ref in enumerate((src_ref, tgt_ref)):
        copies[st].wait()
        for out, xg in ((keep_ref, c), (send_ref, 1 - c)):
            out[st] = ref[pl.ds(gs * xg, gs)].reshape(LANES, LANES).T
        row = jnp.sum(ref[...].reshape(plan.bx * plan.by, LANES), axis=0, keepdims=True)
        sums.append(row + pltpu.roll(row, LANES // 2, 1))
    stat_ref[...] = jnp.where(lane_at() < LANES // 2, *sums)


def lane_at():
    return lax.broadcasted_iota(jnp.int32, (1, LANES), 1)


def chunk_kernel(plan, keep_ref, recv_ref, stat_ref, out_ref):
    c = lax.axis_index("gz")
    half, S = plan.P // 2, plan.S
    size = 2 * S + 1

    def write(low_ref, high_ref):
        stat = stat_ref[...]
        for place in range(plan.P):
            ref, part = (low_ref, place) if place < half else (high_ref, place - half)
            base = size * plan.chip(place)
            for st in range(2):
                out_ref[base + S * st : base + S * st + S, :] = ref[st, S * part : S * part + S, :]
            out_ref[base + 2 * S : base + size, :] = stat

    pl.when(c == 0)(lambda: write(keep_ref, recv_ref))
    pl.when(c == 1)(lambda: write(recv_ref, keep_ref))


def unpack_kernel(plan, in_ref, out_ref):
    S, gs, XH = plan.S, plan.gs, plan.XH
    size = 2 * S + 1
    for i in range(plan.nx):
        for st in range(2):
            bases = [size * (i * plan.ny + j) + S * st for j in range(plan.ny)]
            parts = [in_ref[base : base + S, :] for base in bases]
            for xx, value in enumerate(turn_groups(plan, parts)):
                out_ref[st * XH + i * gs + xx] = value
    out_ref[2 * XH] = jnp.zeros((S, LANES), jnp.float32)
    out_ref[2 * XH, :1, :] = sum_rows(plan, in_ref, size)


def sum_rows(plan, ref, size):
    total = ref[size - 1 : size, :]
    for p in range(1, plan.P):
        total = total + ref[size * p + size - 1 : size * p + size, :]
    return total


def banded(taps, n, odd):
    row = lax.broadcasted_iota(jnp.int32, (n, n), 0)
    col = lax.broadcasted_iota(jnp.int32, (n, n), 1)
    gap = row - col
    total = jnp.zeros((n, n), jnp.float32)
    for d, tap in enumerate(taps):
        if odd:
            if d:
                total = jnp.where(gap == d, d * tap, total)
                total = jnp.where(gap == -d, -(d * tap), total)
        else:
            total = jnp.where(jnp.abs(gap) == d, tap, total)
    return total


def halves(value):
    high = value.astype(jnp.bfloat16)
    return high, (value - high.astype(jnp.float32)).astype(jnp.bfloat16)


def quad(matrix):
    high, low = halves(matrix)
    row = jnp.concatenate([high, low], axis=1)
    return jnp.concatenate([row, row], axis=0)


def lanes_times(value, quad_ref):
    high, low = halves(value)
    both = jnp.concatenate([high, low], axis=1)
    out = jnp.dot(both, quad_ref[...], preferred_element_type=jnp.float32)
    return out[:, :LANES] + out[:, LANES:]


def even_sum(load, taps, mid):
    total = taps[0] * load(mid)
    for d in range(1, len(taps)):
        total = total + taps[d] * (load(mid - d) + load(mid + d))
    return total


def odd_sum(load, taps, mid):
    total = taps[1] * (load(mid + 1) - load(mid - 1))
    for d in range(2, len(taps)):
        total = total + (d * taps[d]) * (load(mid + d) - load(mid - d))
    return total


def kernel_pass(plan, taps, quad_ref, in_ref, zb_ref, rows, emit):
    R, X = plan.R, plan.X

    def z_step(x, carry):
        zb_ref[R + x, :rows, :] = even_sum(lambda j: in_ref[x, j : j + rows, :], taps, R)
        return carry

    lax.fori_loop(0, X, z_step, 0, unroll=4)
    many = 8

    def x_step(k, carry):
        base = k * many
        parts = [
            even_sum(lambda j: zb_ref[base + q + j, :rows, :], taps, R) for q in range(many)
        ]
        out = lanes_times(jnp.concatenate(parts, axis=0), quad_ref)
        for q in range(many):
            emit(base + q, out[q * rows : (q + 1) * rows])
        return carry

    for k in range(X // many):
        x_step(k, 0)


def inside(plan, at, off, rows):
    z = lax.broadcasted_iota(jnp.int32, (rows, LANES), 0) + (at * plan.S - plan.H + off)
    return (z >= 0) & (z < plan.Z)


def half_steps(plan, at, taps, quad_ref, sw, tw, bufs, prev_ref, p_ref, last):
    R, S, H = plan.R, plan.S, plan.H
    u, v, zb, kb = bufs["u"], bufs["v"], bufs["zb"], bufs["kb"]
    width = S + 2 * H

    off = R
    for stage in range(2):
        rows = width - 2 * off
        mask = inside(plan, at, off, rows)

        def emit_v(x, ku, rows=rows, off=off, mask=mask, stage=stage):
            kb[:rows, :] = ku
            mine = kb[H - off : H - off + S, :]
            if stage == 0:
                p_ref[0, x] = mine if prev_ref is None else prev_ref[x] * mine
            else:
                p_ref[1, x] = v[x, H - R : H - R + S, :] * mine
            fresh = jnp.where(mask, tw[x, off : off + rows, :] / ku, 0.0)
            if stage == 0:
                v[x, :rows, :] = fresh
            else:
                bufs["v2"][x, :rows, :] = fresh

        kernel_pass(plan, taps, quad_ref, u, zb, rows, emit_v)
        off += R
        if stage == 1 and last is None:
            return
        rows = width - 2 * off
        mask = inside(plan, at, off, rows)

        def emit_u(x, kv, rows=rows, off=off, mask=mask, stage=stage):
            fresh = jnp.where(mask, sw[x, off : off + rows, :] / kv, 0.0)
            if stage == 0:
                u[x, :rows, :] = fresh
            else:
                last[x] = fresh

        kernel_pass(plan, taps, quad_ref, v if stage == 0 else bufs["v2"], zb, rows, emit_u)
        off += R


def clear_edges(ref, edge, size):
    blank = jnp.zeros((edge,) + ref.shape[1:], jnp.float32)
    ref[:edge] = blank
    ref[edge + size :] = blank


def prep_kernel(plan, k_ref, s_ref, own, taps_ref, quad_ref, slope_ref, smooth_ref, high_ref, low_ref):
    del own
    R, Q = plan.R, plan.Q
    taps = [k_ref[d] for d in range(R + 1)]
    stap = smooth_taps(s_ref, Q)
    for d in range(R + 1):
        taps_ref[d] = jnp.zeros((8, LANES), jnp.float32) + taps[d]
    for d in range(Q + 1):
        taps_ref[R + 1 + d] = jnp.broadcast_to(stap[d], (8, LANES))
    quad_ref[...] = quad(banded(taps, LANES, False))
    slope_ref[...] = quad(banded(taps, LANES, True))
    smooth_ref[...] = quad(banded(stap, LANES, False))
    wide = [jnp.concatenate([t] * (plan.Z // LANES), axis=1) for t in stap]
    high_ref[...], low_ref[...] = halves(banded(wide, plan.Z, False))


def kernel_taps(plan, taps_ref):
    return [taps_ref[d, :1, :] for d in range(plan.R + 1)]


def gaps_of(plan, tot, tw, refs):
    S, H = plan.S, plan.H
    first_half = lane_at() < LANES // 2
    both = tot[:1, :]
    sum_s = jnp.sum(jnp.where(first_half, both, 0.0), axis=1, keepdims=True)
    sum_t = jnp.sum(jnp.where(first_half, 0.0, both), axis=1, keepdims=True)
    scale_s = plan.cells / jnp.broadcast_to(sum_s, (1, LANES))
    scale_t = plan.cells / jnp.broadcast_to(sum_t, (1, LANES))

    def p_step(x, carry):
        want = scale_t * tw[x, H : H + S, :]
        new = []
        for t, part in enumerate(carry):
            gap = jnp.abs(scale_s * refs[t // 2][t % 2, x] - want)
            for r in range(0, S, 8):
                part = part + gap[r : r + 8]
            new.append(part)
        return tuple(new)

    zero = jnp.zeros((8, LANES), jnp.float32)
    gaps = lax.fori_loop(0, plan.X, p_step, (zero,) * (2 * len(refs)), unroll=4)
    return [jnp.sum(g, keepdims=True) for g in gaps]


def in_lanes(values, first=0):
    row = jnp.zeros((1, LANES), jnp.float32)
    for t, value in enumerate(values):
        row = jnp.where(lane_at() == first + t, value, row)
    return row


def gaps_kernel(plan, tot, tw, p12, p34, out_ref):
    rows = gaps_of(plan, tot, tw, (p12, p34))
    out_ref[...] = in_lanes(rows)


def first_kernel(plan, taps_ref, quad_ref, own, even, odd, own2, even2, odd2,
                 sw, tw, u_out, p_out, v_out, tot, u, v, v2, zb, kb):
    R, S, H, X, XH, gs = plan.R, plan.S, plan.H, plan.X, plan.XH, plan.gs
    c = lax.axis_index("gz")
    at = place_of(plan)
    taps = kernel_taps(plan, taps_ref)
    clear_edges(zb, R, X)
    tot[...] = own[2 * XH, :8, :] + own2[2 * XH, :8, :]

    def spread(low, high):
        for refs, core in (((own, low[0], high[0]), c), ((own2, low[1], high[1]), 1 - c)):
            for i in range(plan.nx):
                x = plan.bx * i + gs * core
                for st, win in ((0, sw), (1, tw)):
                    here = pl.ds(st * XH + i * gs, gs)
                    win[pl.ds(x, gs), H : H + S, :] = refs[0][here]
                    win[pl.ds(x, gs), :H, :] = refs[1][here]
                    win[pl.ds(x, gs), H + S :, :] = refs[2][here]

    @pl.when(at % 2 == 0)
    def _():
        spread((odd, odd2), (even, even2))

    @pl.when(at % 2 == 1)
    def _():
        spread((even, even2), (odd, odd2))

    def reach_sum(place, size):
        total = jnp.zeros(place.shape, jnp.float32) + taps[0]
        for d in range(1, R + 1):
            total = total + jnp.where(place - d >= 0, taps[d], 0.0)
            total = total + jnp.where(place + d < size, taps[d], 0.0)
        return total

    rows = S + 2 * H
    mask = inside(plan, at, 0, rows)
    y_at = lax.broadcasted_iota(jnp.int32, (rows, LANES), 1)
    z_at = lax.broadcasted_iota(jnp.int32, (rows, LANES), 0) + (at * S - H)
    plane = reach_sum(z_at, plan.Z) * reach_sum(y_at, plan.Y)

    def u_step(x, carry):
        cx = taps[0]
        for d in range(1, R + 1):
            cx = cx + jnp.where(x - d >= 0, taps[d], 0.0) + jnp.where(x + d < X, taps[d], 0.0)
        u[x] = jnp.where(mask, sw[x] / (plane * cx), 0.0)
        return carry

    lax.fori_loop(0, X, u_step, 0, unroll=2)
    bufs = {"u": u, "v": v, "v2": v2, "zb": zb, "kb": kb}
    half_steps(plan, at, taps, quad_ref, sw, tw, bufs, None, p_out, u_out)
    v_out[...] = v2[:, R : R + S, :]


def gather_u(plan, at, mine, side, other, u):
    c = lax.axis_index("gz")
    S, H = plan.S, plan.H
    u[:, H : H + S, :] = mine[...]
    low = jnp.where(at > 0, 1.0, 0.0)
    high = jnp.where(at < plan.P - 1, 1.0, 0.0)

    @pl.when(c == 0)
    def _():
        u[:, :H, :] = side[...] * low
        u[:, H + S :, :] = other[...] * high

    @pl.when(c == 1)
    def _():
        u[:, :H, :] = other[...] * low
        u[:, H + S :, :] = side[...] * high


def next_kernel(plan, taps_ref, quad_ref, mine, side, other, sw, tw, prev, u_out, p_out, v_out,
                u, v, v2, zb, kb):
    R, S = plan.R, plan.S
    at = place_of(plan)
    taps = kernel_taps(plan, taps_ref)
    clear_edges(zb, R, plan.X)
    gather_u(plan, at, mine, side, other, u)
    bufs = {"u": u, "v": v, "v2": v2, "zb": zb, "kb": kb}
    half_steps(plan, at, taps, quad_ref, sw, tw, bufs, prev, p_out, u_out)
    v_out[...] = v2[:, R : R + S, :]


def smooth_taps(s_ref, reach):
    total = s_ref[0]
    tail = s_ref[1]
    for d in range(2, reach + 1):
        tail = tail + s_ref[d]
    scale = 1.0 / (jnp.zeros((1, LANES), jnp.float32) + (total + 2.0 * tail))
    return [scale * s_ref[d] for d in range(reach + 1)]


def last_kernel(plan, taps_ref, quad_ref, slope_ref, smooth_ref, mine, side, other, sw, tw, prev,
                gaps, tot, out_ref, u, v, v2, zb, zg, kb, raw, p56):
    R, S, H, X, gs, Q = plan.R, plan.S, plan.H, plan.X, plan.gs, plan.Q
    size = 3 * S + 1
    c = lax.axis_index("gz")
    at = place_of(plan)
    taps = kernel_taps(plan, taps_ref)
    stap = [taps_ref[R + 1 + d, :1, :] for d in range(Q + 1)]
    clear_edges(zb, R, X)
    clear_edges(zg, R, X)
    for comp in range(3):
        clear_edges(raw.at[comp], Q, X)
    gather_u(plan, at, mine, side, other, u)
    bufs = {"u": u, "v": v, "v2": v2, "zb": zb, "kb": kb}
    half_steps(plan, at, taps, quad_ref, sw, tw, bufs, prev, p56, None)

    def z_step(x, carry):
        load = lambda j: v2[x, j : j + S, :]
        zb[R + x, :S, :] = even_sum(load, taps, R)
        zg[R + x, :S, :] = odd_sum(load, taps, R)
        return carry

    lax.fori_loop(0, X, z_step, 0, unroll=4)
    many = 8

    def x_step(k, carry):
        base = k * many
        kk, gk, kg = [], [], []
        for q in range(many):
            flat = lambda j: zb[base + q + j, :S, :]
            kk.append(even_sum(flat, taps, R))
            gk.append(odd_sum(flat, taps, R))
            kg.append(even_sum(lambda j: zg[base + q + j, :S, :], taps, R))
        kk = jnp.concatenate(kk, axis=0)
        kvol = lanes_times(kk, quad_ref)
        nums = (
            lanes_times(jnp.concatenate(gk, axis=0), quad_ref),
            lanes_times(kk, slope_ref),
            lanes_times(jnp.concatenate(kg, axis=0), quad_ref),
        )
        for comp, num in enumerate(nums):
            value = num / kvol
            for q in range(many):
                raw[comp, Q + base + q] = value[q * S : (q + 1) * S]
        return carry

    for k in range(X // many):
        x_step(k, 0)

    for i in range(plan.nx):
        x = plan.bx * i + gs * c
        for comp in range(3):
            parts = []
            for xx in range(gs):
                parts.append(even_sum(lambda j: raw[comp, x + xx + j], stap, Q))
            flat = lanes_times(jnp.concatenate(parts, axis=0), smooth_ref)
            turned = turn_groups(plan, [flat[xx * S : (xx + 1) * S] for xx in range(gs)])
            for j in range(plan.ny):
                base = size * (i * plan.ny + j) + comp * S
                out_ref[base : base + S, :] = turned[j]

    rows = gaps_of(plan, tot, tw, (p56,))
    stat = gaps[...] + in_lanes(rows, ITERS - 2)
    for p in range(plan.P):
        out_ref[size * p + 3 * S : size * (p + 1), :] = stat


def finish_kernel(plan, high_ref, low_ref, in_ref, keep_ref, send_ref, mis_ref, data, out):
    S = plan.S
    c = lax.axis_index("gz")
    size = 3 * S + 1
    gone = sum_rows(plan, in_ref, size) / plan.cells
    for t in range(ITERS):
        mis_ref[t] = jnp.sum(jnp.where(lane_at() == t, gone, 0.0))
    for place in range(plan.P):
        for comp in range(3):
            base = size * plan.chip(place) + comp * S
            data[S * place : S * place + S, comp * LANES : (comp + 1) * LANES] = in_ref[
                base : base + S, :
            ]
    m_high, m_low = high_ref[...], low_ref[...]
    d_high, d_low = halves(data[...])
    dot = functools.partial(jnp.dot, preferred_element_type=jnp.float32)
    out[...] = dot(m_high, d_high) + (dot(m_high, d_low) + dot(m_low, d_high))
    for comp in range(3):
        lanes = slice(comp * LANES, (comp + 1) * LANES)
        keep_ref[comp] = out[pl.ds(c * LANES, LANES), lanes].T
        send_ref[comp] = out[pl.ds((1 - c) * LANES, LANES), lanes].T


def place_kernel(plan, keep_ref, recv_ref, out_ref):
    c = lax.axis_index("gz")
    gs = plan.gs
    for comp in range(3):
        out_ref[comp, pl.ds(gs * c, gs)] = keep_ref[comp].reshape(gs, plan.by, LANES)
        out_ref[comp, pl.ds(gs * (1 - c), gs)] = recv_ref[comp].reshape(gs, plan.by, LANES)


def slab_shards(plan, source, target, kernel_half, smooth_half):
    R, S, H, X, XH, Pn, Z = plan.R, plan.S, plan.H, plan.X, plan.XH, plan.P, plan.Z
    bind = lambda kernel: functools.partial(kernel, plan)
    half = f32(2, LANES, LANES)
    vm = lambda *shape: pltpu.VMEM(shape, jnp.float32)
    keep, send, stat = call(
        bind(pack_kernel), [half, half, f32(1, LANES)], 0, 0,
        [vm(*source.shape), vm(*source.shape), pltpu.SemaphoreType.DMA((2,))], n_any=2, name="pack",
    )(*(pltpu.with_memory_space_constraint(a, pltpu.HBM) for a in (source, target)))
    recv = swap_cores(plan, send)
    (chunks,) = call(bind(chunk_kernel), [f32(Pn * (2 * S + 1), LANES)], 0, 3, name="chunks")(
        keep, recv, stat
    )
    spread = trade_chunks(chunks)
    (own,) = call(bind(unpack_kernel), [f32(2 * XH + 1, S, LANES)], 0, 1, name="unpack")(spread)
    square = jax.ShapeDtypeStruct((2 * LANES, 2 * LANES), jnp.bfloat16)
    table = jax.ShapeDtypeStruct((Z, Z), jnp.bfloat16)
    taps, quad_k, quad_g, quad_s, high, low = call(
        bind(prep_kernel), [f32(plan.R + plan.Q + 2, 8, LANES), square, square, square, table, table],
        2, 0, n_any=1, name="prep",
    )(kernel_half, smooth_half, own)
    even, odd = swap_even(plan, own), swap_odd(plan, own)
    own2 = swap_cores(plan, own)
    even, odd, taps = lax.optimization_barrier((even, odd, taps))
    even2, odd2 = swap_cores(plan, even), swap_cores(plan, odd)

    wide, slab, pair = f32(X, S + 2 * H, LANES), f32(X, S, LANES), f32(2, X, S, LANES)
    width = S + 2 * H
    work = [vm(X, width, LANES), vm(X, width - 2 * R, LANES), vm(X, width - 6 * R, LANES)]
    zb = vm(X + 2 * R, width - 2 * R, LANES)
    kb = vm(width - 2 * R, LANES)
    sw, tw, u, p12, v, tot = call(
        bind(first_kernel), [wide, wide, slab, pair, slab, f32(8, LANES)], 0, 8,
        [*work, zb, kb], name="first",
    )(taps, quad_k, own, even, odd, own2, even2, odd2)
    side = swap_sides(plan, u)
    other = swap_cores(plan, side)
    u2, p34, v = call(
        bind(next_kernel), [slab, pair, slab], 0, 8, [*work, zb, kb], name="next"
    )(taps, quad_k, u, side, other, sw, tw, v)
    side = swap_sides(plan, u2)
    (gaps,) = call(bind(gaps_kernel), [f32(1, LANES)], 0, 4, name="gaps")(tot, tw, p12, p34)
    side, gaps = lax.optimization_barrier((side, gaps))
    other = swap_cores(plan, side)
    (chunks,) = call(
        bind(last_kernel), [f32(Pn * (3 * S + 1), LANES)], 0, 12,
        [*work, zb, vm(X + 2 * R, S, LANES), kb,
         vm(3, X + 2 * plan.Q, S, LANES), vm(2, X, S, LANES)],
        name="last",
    )(taps, quad_k, quad_g, quad_s, u2, side, other, sw, tw, v, gaps, tot)
    spread = trade_chunks(chunks)
    three = f32(3, LANES, LANES)
    keep, send, mismatch = call(
        bind(finish_kernel), [three, three, f32(ITERS)], 0, 3,
        [vm(Z, 3 * LANES), vm(Z, 3 * LANES)], smem_out=1, name="finish",
    )(high, low, spread)
    recv = swap_cores(plan, send)
    (displacement,) = call(
        bind(place_kernel), [f32(3, plan.bx, plan.by, LANES)], 0, 2, name="place"
    )(keep, recv)
    return displacement, mismatch


def shards(sizes, source, target, kernel_half, smooth_half):
    plan = Plan(sizes, *source.shape, kernel_half.shape[0] - 1, smooth_half.shape[0] - 1)
    if plan.fits():
        return slab_shards(plan, source, target, kernel_half, smooth_half)
    return block_shards(source, target, kernel_half, smooth_half)


def solution(mesh):
    in_specs = (P("gx", "gy", "gz"), P("gx", "gy", "gz"), P(), P())
    out_specs = (P(None, "gx", "gy", "gz"), P())
    body = functools.partial(shards, dict(mesh.shape))
    return jax.shard_map(body, mesh=mesh, in_specs=in_specs, out_specs=out_specs, check_vma=False)
```

```python
import functools

import jax
import jax.numpy as jnp
from jax import lax
from jax.experimental import pallas as pl
from jax.experimental.pallas import tpu as pltpu
from jax.sharding import PartitionSpec as P

ITERS = 6
LANES = 128
AXES = ("gx", "gy", "gz")


def padded_2(block, sides, width):
    for axis, dim in sides:
        count = lax.axis_size(axis)
        forward = [(i, i + 1) for i in range(count - 1)]
        backward = [(target, source) for source, target in forward]
        low = lax.ppermute(
            lax.slice_in_dim(block, block.shape[dim] - width, None, axis=dim), axis, forward
        )
        high = lax.ppermute(lax.slice_in_dim(block, 0, width, axis=dim), axis, backward)
        block = jnp.concatenate([low, block, high], axis=dim)
    return block


def full_taps(half):
    return jnp.concatenate([half[:0:-1], half])


def along(padded, taps, axis, count):
    width = taps.shape[0]
    total = taps[0] * lax.slice_in_dim(padded, 0, count, axis=axis)
    for j in range(1, width):
        total = total + taps[j] * lax.slice_in_dim(padded, j, j + count, axis=axis)
    return total


def three_passes(padded, taps, size_x, size_y, size_z):
    padded = along(padded, taps, 0, size_x)
    padded = along(padded, taps, 1, size_y)
    return along(padded, taps, 2, size_z)


def block_shards(source, target, kernel_half, smooth_half):
    kern = full_taps(kernel_half)
    radius = kernel_half.shape[0] - 1
    reach = smooth_half.shape[0] - 1
    offsets = jnp.arange(-radius, radius + 1).astype(jnp.float32)
    slope = offsets * kern
    norm_total = smooth_half[0] + 2.0 * jnp.sum(smooth_half[1:])
    smooth = full_taps(smooth_half) / norm_total
    size_x, size_y, size_z = source.shape
    cells = float(source.size * lax.axis_size("gx") * lax.axis_size("gy") * lax.axis_size("gz"))
    totals = lax.psum((jnp.sum(source), jnp.sum(target)), AXES)
    first = source * (cells / totals[0])
    second = target * (cells / totals[1])
    first_wide = padded_2(first, (("gx", 0), ("gy", 1), ("gz", 2)), radius)
    scaling_v = jnp.ones_like(source)
    errors = []
    for step in range(ITERS):
        padded = padded_2(scaling_v, (("gx", 0), ("gy", 1), ("gz", 2)), 2 * radius)
        kv_wide = three_passes(
            padded, kern, size_x + 2 * radius, size_y + 2 * radius, size_z + 2 * radius
        )
        u_wide = first_wide / kv_wide
        ku = three_passes(u_wide, kern, size_x, size_y, size_z)
        local_err = jnp.sum(jnp.abs(scaling_v * ku - second))
        errors.append(lax.psum(local_err, AXES) / cells)
        scaling_v = second / ku
    mismatch = jnp.stack(errors)
    padded = padded_2(scaling_v, (("gx", 0), ("gy", 1), ("gz", 2)), radius)
    pass_k = along(padded, kern, 0, size_x)
    pass_g = along(padded, slope, 0, size_x)
    kk = along(pass_k, kern, 1, size_y)
    kg = along(pass_k, slope, 1, size_y)
    gk = along(pass_g, kern, 1, size_y)
    kvol = along(kk, kern, 2, size_z)
    znum = along(kk, slope, 2, size_z)
    ynum = along(kg, kern, 2, size_z)
    xnum = along(gk, kern, 2, size_z)
    raw = jnp.stack([xnum, ynum, znum]) / kvol
    padded = padded_2(raw, (("gx", 1), ("gy", 2), ("gz", 3)), reach)
    padded = along(padded, smooth, 1, size_x)
    padded = along(padded, smooth, 2, size_y)
    displacement = along(padded, smooth, 3, size_z)
    return (displacement, mismatch)


class Plan:
    def __init__(self, mesh, bx, by, bz, radius, reach):
        self.nx, self.ny, self.nc = mesh["gx"], mesh["gy"], mesh["gz"]
        self.bx, self.by, self.bz = bx, by, bz
        self.R, self.Q = radius, reach
        self.P = self.nx * self.ny
        self.X, self.Y, self.Z = bx * self.nx, by * self.ny, bz * self.nc
        self.S = self.Z // self.P
        self.H = 4 * radius
        self.gs = LANES // by if by <= LANES else 0
        self.XH = self.X // 2
        self.cells = float(self.X * self.Y * self.Z)

    def fits(self):
        return (
            self.nc == 2
            and self.ny >= 2
            and self.ny & (self.ny - 1) == 0
            and self.nx >= 2
            and self.bz == LANES
            and self.Y == LANES
            and self.gs == self.ny
            and self.bx == 2 * self.gs
            and self.Z == self.P * self.S
            and self.S == self.H
            and self.S % 8 == 0
            and self.R % 4 == 0
            and ITERS == 6
        )

    def spot(self, at):
        at %= self.P
        col, q = divmod(at, self.nx)
        return (q if col % 2 == 0 else self.nx - 1 - q), col ^ (col >> 1)

    def chip(self, at):
        i, j = self.spot(at)
        return i * self.ny + j

    def device(self, at, core):
        return self.chip(at) * self.nc + core


def swap_cores(plan, value):
    pairs = [(plan.device(at, c), plan.device(at, 1 - c)) for at in range(plan.P) for c in range(2)]
    return lax.ppermute(value, AXES, pairs)


def swap_even(plan, value):
    pairs = [(plan.device(at, c), plan.device(at ^ 1, c)) for at in range(plan.P) for c in range(2)]
    return lax.ppermute(value, AXES, pairs)


def swap_odd(plan, value):
    pairs = [
        (plan.device(at, c), plan.device(((at + 1) ^ 1) - 1, c))
        for at in range(plan.P)
        for c in range(2)
    ]
    return lax.ppermute(value, AXES, pairs)


def swap_sides(plan, value):
    pairs = [(plan.device(at, 0), plan.device(at - 1, 1)) for at in range(plan.P)]
    pairs += [(plan.device(at, 1), plan.device(at + 1, 0)) for at in range(plan.P)]
    return lax.ppermute(value, AXES, pairs)


def trade_chunks(value):
    rows, lanes = value.shape
    out = lax.all_to_all(value.reshape(rows, 1, lanes), ("gx", "gy"), 0, 0, tiled=True)
    return out.reshape(rows, lanes)


def place_of(plan):
    i, j = lax.axis_index("gx"), lax.axis_index("gy")
    at = jnp.int32(0)
    for place in range(plan.P):
        a, b = plan.spot(place)
        at = at + jnp.where((i == a) & (j == b), place, 0)
    return at.astype(jnp.int32)


def call(kernel, out_shape, n_smem, n_vmem, scratch=(), smem_out=0, n_any=0, any_out=0, aliases=None, name=None):
    vm, sm = pl.BlockSpec(memory_space=pltpu.VMEM), pl.BlockSpec(memory_space=pltpu.SMEM)
    hbm = pl.BlockSpec(memory_space=pltpu.HBM)
    out_specs = [vm] * (len(out_shape) - smem_out - any_out) + [sm] * smem_out + [hbm] * any_out
    return pl.pallas_call(
        kernel,
        out_shape=out_shape,
        in_specs=[sm] * n_smem + [vm] * n_vmem + [hbm] * n_any,
        out_specs=out_specs,
        scratch_shapes=list(scratch),
        input_output_aliases=aliases or {},
        compiler_params=pltpu.CompilerParams(vmem_limit_bytes=48 << 20),
        name=name,
    )


def f32(*shape):
    return jax.ShapeDtypeStruct(shape, jnp.float32)


def turn_groups(plan, parts):
    n, w = plan.gs, plan.by
    group = lax.broadcasted_iota(jnp.int32, parts[0].shape, 1) // w
    outs = []
    for a in range(n):
        total = parts[a]
        for b in range(n):
            if b != a:
                moved = pltpu.roll(parts[b], (w * (b - a)) % LANES, 1)
                total = jnp.where(group == b, moved, total)
        outs.append(total)
    return outs


def pack_kernel(plan, src_hbm, tgt_hbm, keep_ref, send_ref, stat_ref, src_ref, tgt_ref, sems):
    c = lax.axis_index("gz")
    gs = plan.gs
    copies = [
        pltpu.make_async_copy(src_hbm, src_ref, sems.at[0]),
        pltpu.make_async_copy(tgt_hbm, tgt_ref, sems.at[1]),
    ]
    for copy in copies:
        copy.start()
    sums = []
    for st, ref in enumerate((src_ref, tgt_ref)):
        copies[st].wait()
        for out, xg in ((keep_ref, c), (send_ref, 1 - c)):
            out[st] = ref[pl.ds(gs * xg, gs)].reshape(LANES, LANES).T
        row = jnp.sum(ref[...].reshape(plan.bx * plan.by, LANES), axis=0, keepdims=True)
        sums.append(row + pltpu.roll(row, LANES // 2, 1))
    stat_ref[...] = jnp.where(lane_at() < LANES // 2, *sums)


def lane_at():
    return lax.broadcasted_iota(jnp.int32, (1, LANES), 1)


def chunk_kernel(plan, keep_ref, recv_ref, stat_ref, out_ref):
    c = lax.axis_index("gz")
    half, S = plan.P // 2, plan.S
    size = 2 * S + 1

    def write(low_ref, high_ref):
        stat = stat_ref[...]
        for place in range(plan.P):
            ref, part = (low_ref, place) if place < half else (high_ref, place - half)
            base = size * plan.chip(place)
            for st in range(2):
                out_ref[base + S * st : base + S * st + S, :] = ref[st, S * part : S * part + S, :]
            out_ref[base + 2 * S : base + size, :] = stat

    pl.when(c == 0)(lambda: write(keep_ref, recv_ref))
    pl.when(c == 1)(lambda: write(recv_ref, keep_ref))


def unpack_kernel(plan, in_ref, s_ref, t_ref):
    S, gs, XH = plan.S, plan.gs, plan.XH
    size = 2 * S + 1
    for st, out_ref in enumerate((s_ref, t_ref)):
        for i in range(plan.nx):
            bases = [size * (i * plan.ny + j) + S * st for j in range(plan.ny)]
            parts = [in_ref[base : base + S, :] for base in bases]
            for xx, value in enumerate(turn_groups(plan, parts)):
                out_ref[i * gs + xx] = value
    t_ref[XH] = jnp.zeros((S, LANES), jnp.float32)
    t_ref[XH, :1, :] = sum_rows(plan, in_ref, size)


def sum_rows(plan, ref, size):
    total = ref[size - 1 : size, :]
    for p in range(1, plan.P):
        total = total + ref[size * p + size - 1 : size * p + size, :]
    return total


def banded(taps, n, odd):
    row = lax.broadcasted_iota(jnp.int32, (n, n), 0)
    col = lax.broadcasted_iota(jnp.int32, (n, n), 1)
    gap = row - col
    total = jnp.zeros((n, n), jnp.float32)
    for d, tap in enumerate(taps):
        if odd:
            if d:
                total = jnp.where(gap == d, d * tap, total)
                total = jnp.where(gap == -d, -(d * tap), total)
        else:
            total = jnp.where(jnp.abs(gap) == d, tap, total)
    return total


def halves(value):
    high = value.astype(jnp.bfloat16)
    return high, (value - high.astype(jnp.float32)).astype(jnp.bfloat16)


def quad(matrix):
    high, low = halves(matrix)
    row = jnp.concatenate([high, low], axis=1)
    return jnp.concatenate([row, row], axis=0)


def lanes_times(value, quad_ref):
    high, low = halves(value)
    both = jnp.concatenate([high, low], axis=1)
    out = jnp.dot(both, quad_ref[...], preferred_element_type=jnp.float32)
    return out[:, :LANES] + out[:, LANES:]


def even_sum(load, taps, mid):
    total = taps[0] * load(mid)
    for d in range(1, len(taps)):
        total = total + taps[d] * (load(mid - d) + load(mid + d))
    return total


def unit_sum(load, taps, mid):
    total = load(mid)
    for d in range(1, len(taps)):
        total = total + taps[d] * (load(mid - d) + load(mid + d))
    return total


def odd_sum(load, taps, mid):
    total = taps[1] * (load(mid + 1) - load(mid - 1))
    for d in range(2, len(taps)):
        total = total + (d * taps[d]) * (load(mid + d) - load(mid - d))
    return total


def kernel_pass(plan, taps, quad_ref, in_ref, zb_ref, rows, emit):
    R, X = plan.R, plan.X

    def z_step(x, carry):
        zb_ref[R + x, :rows, :] = unit_sum(lambda j: in_ref[x, j : j + rows, :], taps, R)
        return carry

    lax.fori_loop(0, X, z_step, 0, unroll=4)
    many = 8
    for base in range(0, X, many):
        parts = [
            unit_sum(lambda j: zb_ref[base + q + j, :rows, :], taps, R) for q in range(many)
        ]
        out = lanes_times(jnp.concatenate(parts, axis=0), quad_ref)
        for q in range(many):
            emit(base + q, out[q * rows : (q + 1) * rows])


def inside(plan, at, off, rows):
    z = lax.broadcasted_iota(jnp.int32, (rows, LANES), 0) + (at * plan.S - plan.H + off)
    return (z >= 0) & (z < plan.Z)


def scale_step(plan, at, taps, quad_ref, zb, src, top, dst, over, off, start, rows):
    mask = inside(plan, at, off + start, rows)
    src = src.at[:, pl.ds(top, rows + 2 * plan.R), :]
    lead = (off + 7) // 8 * 8
    over = over.at[:, pl.ds(start, rows + lead), :]

    def emit(x, value):
        dst[x, pl.ds(start, rows), :] = jnp.where(mask, over[x, off : off + rows, :] / value, 0.0)

    kernel_pass(plan, taps, quad_ref, src, zb, rows, emit)


def clear_edges(ref, edge, size):
    blank = jnp.zeros((edge,) + ref.shape[1:], jnp.float32)
    ref[:edge] = blank
    ref[edge + size :] = blank


def prep_kernel(plan, k_ref, s_ref, own, taps_ref, quad_ref, slope_ref, smooth_ref, high_ref, low_ref):
    del own
    R, Q = plan.R, plan.Q
    taps = [jnp.zeros((1, LANES), jnp.float32) + k_ref[d] for d in range(R + 1)]
    taps = [jnp.ones((1, LANES), jnp.float32)] + [tap / taps[0] for tap in taps[1:]]
    stap = smooth_taps(s_ref, Q)
    for d in range(R + 1):
        taps_ref[d] = jnp.broadcast_to(taps[d], (8, LANES))
    for d in range(Q + 1):
        taps_ref[R + 1 + d] = jnp.broadcast_to(stap[d], (8, LANES))
    quad_ref[...] = quad(banded(taps, LANES, False))
    slope_ref[...] = quad(banded(taps, LANES, True))
    smooth_ref[...] = quad(banded(stap, LANES, False))
    wide = [jnp.concatenate([t] * (plan.Z // LANES), axis=1) for t in stap]
    high_ref[...], low_ref[...] = halves(banded(wide, plan.Z, False))


def kernel_taps(plan, taps_ref):
    return [taps_ref[d, :1, :] for d in range(plan.R + 1)]


def gaps_of(plan, tot, tw, olds, news):
    S, H = plan.S, plan.H
    first_half = lane_at() < LANES // 2
    both = tot[:1, :]
    sum_s = jnp.sum(jnp.where(first_half, both, 0.0), axis=1, keepdims=True)
    sum_t = jnp.sum(jnp.where(first_half, 0.0, both), axis=1, keepdims=True)
    scale_s = plan.cells / jnp.broadcast_to(sum_s, (1, LANES))
    scale_t = plan.cells / jnp.broadcast_to(sum_t, (1, LANES))

    def mid(ref, x):
        edge = (ref.shape[1] - S) // 2
        return ref[x, edge : edge + S, :]

    def p_step(x, carry):
        t = mid(tw, x)
        want = scale_t * t
        have = scale_s * t
        result = []
        for part, old, new in zip(carry, olds, news):
            value = have / mid(new, x)
            if old is not None:
                value = value * mid(old, x)
            gap = jnp.abs(value - want)
            for r in range(0, S, 8):
                part = part + gap[r : r + 8]
            result.append(part)
        return tuple(result)

    zero = jnp.zeros((8, LANES), jnp.float32)
    gaps = lax.fori_loop(0, plan.X, p_step, (zero,) * len(news), unroll=4)
    return [jnp.sum(g, keepdims=True) for g in gaps]


def in_lanes(values, first=0):
    row = jnp.zeros((1, LANES), jnp.float32)
    for t, value in enumerate(values):
        row = jnp.where(lane_at() == first + t, value, row)
    return row


def gaps_kernel(plan, tot, tw, v1, v2, v3, v4, out_ref):
    out_ref[...] = in_lanes(gaps_of(plan, tot, tw, (None, v1, v2, v3), (v1, v2, v3, v4)))


def spread_halves(plan, at, own, even, odd, own2, even2, odd2, win):
    S, H, gs = plan.S, plan.H, plan.gs
    c = lax.axis_index("gz")

    def spread(low, high):
        for k, (mid, core) in enumerate(((own, c), (own2, 1 - c))):
            for i in range(plan.nx):
                x, here = plan.bx * i + gs * core, pl.ds(i * gs, gs)
                win[pl.ds(x, gs), H : H + S, :] = mid[here]
                win[pl.ds(x, gs), :H, :] = low[k][here]
                win[pl.ds(x, gs), H + S :, :] = high[k][here]

    pl.when(at % 2 == 0)(lambda: spread((odd, odd2), (even, even2)))
    pl.when(at % 2 == 1)(lambda: spread((even, even2), (odd, odd2)))


def open_kernel(plan, taps_ref, quad_ref, own, even, odd, own2, even2, odd2, sw, ku, u, zb):
    R, S, H, X = plan.R, plan.S, plan.H, plan.X
    at = place_of(plan)
    taps = kernel_taps(plan, taps_ref)
    clear_edges(zb, R, X)
    spread_halves(plan, at, own, even, odd, own2, even2, odd2, sw)

    def reach_sum(place, size):
        total = jnp.ones(place.shape, jnp.float32)
        for d in range(1, R + 1):
            total = total + jnp.where(place - d >= 0, taps[d], 0.0)
            total = total + jnp.where(place + d < size, taps[d], 0.0)
        return total

    rows = S + 2 * H
    mask = inside(plan, at, 0, rows)
    y_at = lax.broadcasted_iota(jnp.int32, (rows, LANES), 1)
    z_at = lax.broadcasted_iota(jnp.int32, (rows, LANES), 0) + (at * S - H)
    plane = reach_sum(z_at, plan.Z) * (reach_sum(y_at, plan.Y) * taps_ref[0, :1, :])

    def u_step(x, carry):
        cx = reach_sum(jnp.zeros((1, LANES), jnp.int32) + x, X)
        u[x] = jnp.where(mask, sw[x] / (plane * cx), 0.0)
        return carry

    lax.fori_loop(0, X, u_step, 0, unroll=2)

    def emit(x, value):
        ku[x] = value

    kernel_pass(plan, taps, quad_ref, u, zb, rows - 2 * R, emit)


def first_kernel(plan, taps_ref, quad_ref, own, even, odd, own2, even2, odd2, sw, ku,
                 tw, v, v2, u_out, tot, u, zb):
    R, S, H, X, XH = plan.R, plan.S, plan.H, plan.X, plan.XH
    at = place_of(plan)
    taps = kernel_taps(plan, taps_ref)
    clear_edges(zb, R, X)
    spread_halves(plan, at, own, even, odd, own2, even2, odd2, tw)
    tot[...] = own[XH, :1, :] + own2[XH, :1, :]
    rows = S + 2 * H - 2 * R
    mask = inside(plan, at, R, rows)

    def v_step(x, carry):
        v[x] = jnp.where(mask, tw[x, R : R + rows, :] / ku[x], 0.0)
        return carry

    lax.fori_loop(0, X, v_step, 0, unroll=4)
    step = functools.partial(scale_step, plan, at, taps, quad_ref, zb)
    step(v, 0, u, sw, 2 * R, 0, rows - 2 * R)
    step(u, 0, v2, tw, 3 * R, 0, rows - 4 * R)
    step(v2, 0, u_out, sw, 4 * R, 0, rows - 6 * R)


def early_kernel(plan, taps_ref, quad_ref, mine, side, sw, tw, v, u, v2, win, zb):
    R, S, H = plan.R, plan.S, plan.H
    c = lax.axis_index("gz")
    at = place_of(plan)
    taps = kernel_taps(plan, taps_ref)
    clear_edges(zb, R, plan.X)
    real = jnp.where(jnp.where(c == 0, at > 0, at < plan.P - 1), 1.0, 0.0)
    win[:, pl.ds(pl.multiple_of(H * c, 8), H), :] = side[...] * real
    win[:, pl.ds(pl.multiple_of(H * (1 - c), 8), S), :] = mine[...]
    step = functools.partial(scale_step, plan, at, taps, quad_ref, zb)
    from_ = pl.multiple_of(S * c, 8)
    step(win, 0, v, tw, R, from_, S + H - 2 * R)
    step(v, from_, u, sw, 2 * R, from_, S + H - 4 * R)
    step(u, from_, v2, tw, 3 * R, from_, S + H - 6 * R)


def late_rows(plan, at, taps, quad_ref, mine, other, sw, tw, v, u, v2, win, zb):
    R, S, H = plan.R, plan.S, plan.H
    c = lax.axis_index("gz")
    real = jnp.where(jnp.where(c == 1, at > 0, at < plan.P - 1), 1.0, 0.0)
    half = S // 2

    def lay(other_at, mine_at, mine_from):
        win[:, other_at : other_at + H, :] = other[...] * real
        win[:, mine_at : mine_at + half, :] = mine[:, mine_from : mine_from + half, :]

    pl.when(c == 0)(lambda: lay(half, 0, half))
    pl.when(c == 1)(lambda: lay(0, H, 0))
    step = functools.partial(scale_step, plan, at, taps, quad_ref, zb)
    first = pl.multiple_of((S + H - 2 * R) * (1 - c), 8)
    step(win, 0, v, tw, R, first, S)
    second = pl.multiple_of((S + H - 4 * R) * (1 - c), 8)
    step(v, second, u, sw, 2 * R, second, S)
    third = pl.multiple_of((S + H - 6 * R) * (1 - c), 8)
    step(u, third, v2, tw, 3 * R, third, S)


def late_kernel(plan, taps_ref, quad_ref, mine, other, sw, tw, v_in, u_in, v2_in,
                v, u, v2, u_out, win, zb):
    del v_in, u_in, v2_in
    R, S = plan.R, plan.S
    at = place_of(plan)
    taps = kernel_taps(plan, taps_ref)
    clear_edges(zb, R, plan.X)
    late_rows(plan, at, taps, quad_ref, mine, other, sw, tw, v, u, v2, win, zb)
    scale_step(plan, at, taps, quad_ref, zb, v2, 0, u_out, sw, 4 * R, 0, S)


def smooth_taps(s_ref, reach):
    total = s_ref[0]
    tail = s_ref[1]
    for d in range(2, reach + 1):
        tail = tail + s_ref[d]
    scale = 1.0 / (jnp.zeros((1, LANES), jnp.float32) + (total + 2.0 * tail))
    return [scale * s_ref[d] for d in range(reach + 1)]


def last_kernel(plan, taps_ref, quad_ref, slope_ref, smooth_ref, mine, other, sw, tw, prev,
                gaps, tot, v_in, u_in, v2_in, v, u, v2, out_ref, win, zb, zg, raw):
    del v_in, u_in, v2_in
    R, S, X, gs, Q = plan.R, plan.S, plan.X, plan.gs, plan.Q
    size = 3 * S + 1
    c = lax.axis_index("gz")
    at = place_of(plan)
    taps = kernel_taps(plan, taps_ref)
    stap = [taps_ref[R + 1 + d, :1, :] for d in range(Q + 1)]
    clear_edges(zb, R, X)
    clear_edges(zg, R, X)
    for comp in range(3):
        clear_edges(raw.at[comp], Q, X)
    late_rows(plan, at, taps, quad_ref, mine, other, sw, tw, v, u, v2, win, zb)

    def z_step(x, carry):
        load = lambda j: v2[x, j : j + S, :]
        zb[R + x, :S, :] = unit_sum(load, taps, R)
        zg[R + x, :S, :] = odd_sum(load, taps, R)
        return carry

    lax.fori_loop(0, X, z_step, 0, unroll=4)
    many = 8

    def x_step(k, carry):
        base = k * many
        kk, gk, kg = [], [], []
        for q in range(many):
            flat = lambda j: zb[base + q + j, :S, :]
            kk.append(unit_sum(flat, taps, R))
            gk.append(odd_sum(flat, taps, R))
            kg.append(unit_sum(lambda j: zg[base + q + j, :S, :], taps, R))
        kk = jnp.concatenate(kk, axis=0)
        kvol = lanes_times(kk, quad_ref)
        nums = (
            lanes_times(jnp.concatenate(gk, axis=0), quad_ref),
            lanes_times(kk, slope_ref),
            lanes_times(jnp.concatenate(kg, axis=0), quad_ref),
        )
        for comp, num in enumerate(nums):
            value = num / kvol
            for q in range(many):
                raw[comp, Q + base + q] = value[q * S : (q + 1) * S]
        return carry

    for k in range(X // many):
        x_step(k, 0)

    for i in range(plan.nx):
        x = plan.bx * i + gs * c
        for comp in range(3):
            parts = []
            for xx in range(gs):
                parts.append(even_sum(lambda j: raw[comp, x + xx + j], stap, Q))
            flat = lanes_times(jnp.concatenate(parts, axis=0), smooth_ref)
            turned = turn_groups(plan, [flat[xx * S : (xx + 1) * S] for xx in range(gs)])
            for j in range(plan.ny):
                base = size * (i * plan.ny + j) + comp * S
                out_ref[base : base + S, :] = turned[j]

    rows = gaps_of(plan, tot, tw, (prev, v), (v, v2))
    stat = gaps[...] + in_lanes(rows, ITERS - 2)
    for p in range(plan.P):
        out_ref[size * p + 3 * S : size * (p + 1), :] = stat


def smooth_z(plan, core, high_ref, low_ref, in_ref, data, emit):
    S = plan.S
    size = 3 * S + 1
    for place in range(plan.P):
        for comp in range(3):
            base = size * plan.chip(place) + comp * S
            data[S * place : S * place + S, comp * LANES : (comp + 1) * LANES] = in_ref[
                base : base + S, :
            ]
    rows = pl.ds(pl.multiple_of(core * LANES, LANES), LANES)
    m_high, m_low = high_ref[rows, :], low_ref[rows, :]
    d_high, d_low = halves(data[...])
    dot = functools.partial(jnp.dot, preferred_element_type=jnp.float32)
    out = dot(m_high, d_high) + (dot(m_high, d_low) + dot(m_low, d_high))
    for comp in range(3):
        emit(comp, out[:, comp * LANES : (comp + 1) * LANES].T)


def away_kernel(plan, high_ref, low_ref, in_ref, send_ref, data):
    def emit(comp, value):
        send_ref[comp] = value

    smooth_z(plan, 1 - lax.axis_index("gz"), high_ref, low_ref, in_ref, data, emit)


def home_kernel(plan, high_ref, low_ref, in_ref, mis_ref, out_hbm, data, keep, sem):
    c = lax.axis_index("gz")
    gs = plan.gs

    def emit(comp, value):
        keep[comp] = value.reshape(gs, plan.by, LANES)

    smooth_z(plan, c, high_ref, low_ref, in_ref, data, emit)
    copy = pltpu.make_async_copy(keep, out_hbm.at[:, pl.ds(gs * c, gs)], sem)
    copy.start()
    gone = sum_rows(plan, in_ref, 3 * plan.S + 1) / plan.cells
    for t in range(ITERS):
        mis_ref[t] = jnp.sum(jnp.where(lane_at() == t, gone, 0.0))
    copy.wait()


def place_kernel(plan, recv_ref, in_hbm, out_hbm, sem):
    del in_hbm
    c = lax.axis_index("gz")
    copy = pltpu.make_async_copy(recv_ref, out_hbm.at[:, pl.ds(plan.gs * (1 - c), plan.gs)], sem)
    copy.start()
    copy.wait()


def slab_shards(plan, source, target, kernel_half, smooth_half):
    R, S, H, X, XH, Pn, Z = plan.R, plan.S, plan.H, plan.X, plan.XH, plan.P, plan.Z
    bind = lambda kernel: functools.partial(kernel, plan)
    half = f32(2, LANES, LANES)
    vm = lambda *shape: pltpu.VMEM(shape, jnp.float32)
    keep, send, stat = call(
        bind(pack_kernel), [half, half, f32(1, LANES)], 0, 0,
        [vm(*source.shape), vm(*source.shape), pltpu.SemaphoreType.DMA((2,))], n_any=2, name="pack",
    )(*(pltpu.with_memory_space_constraint(a, pltpu.HBM) for a in (source, target)))
    recv = swap_cores(plan, send)
    (chunks,) = call(bind(chunk_kernel), [f32(Pn * (2 * S + 1), LANES)], 0, 3, name="chunks")(
        keep, recv, stat
    )
    spread = trade_chunks(chunks)
    own_s, own_t = call(
        bind(unpack_kernel), [f32(XH, S, LANES), f32(XH + 1, S, LANES)], 0, 1, name="unpack"
    )(spread)
    square = jax.ShapeDtypeStruct((2 * LANES, 2 * LANES), jnp.bfloat16)
    table = jax.ShapeDtypeStruct((Z, Z), jnp.bfloat16)
    taps, quad_k, quad_g, quad_s, high, low = call(
        bind(prep_kernel), [f32(plan.R + plan.Q + 2, 8, LANES), square, square, square, table, table],
        2, 0, n_any=1, name="prep",
    )(kernel_half, smooth_half, own_s)
    even_s, odd_s = swap_even(plan, own_s), swap_odd(plan, own_s)
    even_t, odd_t = swap_even(plan, own_t), swap_odd(plan, own_t)
    own2_s, own2_t = swap_cores(plan, own_s), swap_cores(plan, own_t)
    even_s, odd_s, taps = lax.optimization_barrier((even_s, odd_s, taps))
    halos_s = swap_cores(plan, even_s), swap_cores(plan, odd_s)

    slab = f32(X, S, LANES)
    width = S + 2 * H
    wide, v_shape, u_shape, v2_shape = (f32(X, width - 2 * k * R, LANES) for k in (0, 1, 2, 3))
    zb = vm(X + 2 * R, width - 2 * R, LANES)
    sw, ku = call(
        bind(open_kernel), [wide, v_shape], 0, 8, [vm(*wide.shape), zb], name="open"
    )(taps, quad_k, own_s, even_s, odd_s, own2_s, *halos_s)
    even_t, odd_t, ku = lax.optimization_barrier((even_t, odd_t, ku))
    halos_t = swap_cores(plan, even_t), swap_cores(plan, odd_t)
    tw, v1, v2, u, tot = call(
        bind(first_kernel), [wide, v_shape, v2_shape, slab, f32(1, LANES)], 0, 10,
        [vm(*u_shape.shape), zb], name="first",
    )(taps, quad_k, own_t, even_t, odd_t, own2_t, *halos_t, sw, ku)

    def early(u, side):
        return call(
            bind(early_kernel), [v_shape, u_shape, v2_shape], 0, 6,
            [vm(X, S + H, LANES), zb], name="early",
        )(taps, quad_k, u, side, sw, tw)

    rest = vm(X, H + S // 2, LANES)
    side = swap_sides(plan, u)
    other = swap_cores(plan, side)
    v3, u4, v4 = early(u, side)
    v3, _, v4, u = call(
        bind(late_kernel), [v_shape, u_shape, v2_shape, slab], 0, 9, [rest, zb],
        aliases={6: 0, 7: 1, 8: 2}, name="late",
    )(taps, quad_k, u, other, sw, tw, v3, u4, v4)
    side = swap_sides(plan, u)
    (gaps,) = call(bind(gaps_kernel), [f32(1, LANES)], 0, 6, name="gaps")(tot, tw, v1, v2, v3, v4)
    side, gaps = lax.optimization_barrier((side, gaps))
    other = swap_cores(plan, side)
    v5, u6, v6 = early(u, side)
    *_, chunks = call(
        bind(last_kernel), [v_shape, u_shape, v2_shape, f32(Pn * (3 * S + 1), LANES)], 0, 14,
        [rest, zb, vm(X + 2 * R, S, LANES), vm(3, X + 2 * plan.Q, S, LANES)],
        aliases={11: 0, 12: 1, 13: 2}, name="last",
    )(taps, quad_k, quad_g, quad_s, u, other, sw, tw, v4, gaps, tot, v5, u6, v6)
    spread = trade_chunks(chunks)
    data = vm(Z, 3 * LANES)
    (send,) = call(bind(away_kernel), [f32(3, LANES, LANES)], 0, 3, [data], name="away")(
        high, low, spread
    )
    half = (3, plan.gs, plan.by, LANES)
    recv = swap_cores(plan, send.reshape(half))
    whole = f32(3, plan.bx, plan.by, LANES)
    mismatch, displacement = call(
        bind(home_kernel), [f32(ITERS), whole], 0, 3, [data, vm(*half), pltpu.SemaphoreType.DMA(())],
        smem_out=1, any_out=1, name="home",
    )(high, low, spread)
    (displacement,) = call(
        bind(place_kernel), [whole], 0, 1, [pltpu.SemaphoreType.DMA(())], n_any=1, any_out=1,
        aliases={1: 0}, name="place",
    )(recv, displacement)
    return displacement, mismatch


def shards(sizes, source, target, kernel_half, smooth_half):
    plan = Plan(sizes, *source.shape, kernel_half.shape[0] - 1, smooth_half.shape[0] - 1)
    if plan.fits():
        return slab_shards(plan, source, target, kernel_half, smooth_half)
    return block_shards(source, target, kernel_half, smooth_half)


def solution(mesh):
    in_specs = (P("gx", "gy", "gz"), P("gx", "gy", "gz"), P(), P())
    out_specs = (P(None, "gx", "gy", "gz"), P())
    body = functools.partial(shards, dict(mesh.shape))
    return jax.shard_map(body, mesh=mesh, in_specs=in_specs, out_specs=out_specs, check_vma=False)
```

```python
import functools

import jax
import jax.numpy as jnp
from jax import lax
from jax.experimental import pallas as pl
from jax.experimental.pallas import tpu as pltpu
from jax.sharding import PartitionSpec as P

ITERS = 6
LANES = 128
AXES = ("gx", "gy", "gz")


def padded_2(block, sides, width):
    for axis, dim in sides:
        count = lax.axis_size(axis)
        forward = [(i, i + 1) for i in range(count - 1)]
        backward = [(target, source) for source, target in forward]
        low = lax.ppermute(
            lax.slice_in_dim(block, block.shape[dim] - width, None, axis=dim), axis, forward
        )
        high = lax.ppermute(lax.slice_in_dim(block, 0, width, axis=dim), axis, backward)
        block = jnp.concatenate([low, block, high], axis=dim)
    return block


def full_taps(half):
    return jnp.concatenate([half[:0:-1], half])


def along(padded, taps, axis, count):
    width = taps.shape[0]
    total = taps[0] * lax.slice_in_dim(padded, 0, count, axis=axis)
    for j in range(1, width):
        total = total + taps[j] * lax.slice_in_dim(padded, j, j + count, axis=axis)
    return total


def three_passes(padded, taps, size_x, size_y, size_z):
    padded = along(padded, taps, 0, size_x)
    padded = along(padded, taps, 1, size_y)
    return along(padded, taps, 2, size_z)


def block_shards(source, target, kernel_half, smooth_half):
    kern = full_taps(kernel_half)
    radius = kernel_half.shape[0] - 1
    reach = smooth_half.shape[0] - 1
    offsets = jnp.arange(-radius, radius + 1).astype(jnp.float32)
    slope = offsets * kern
    norm_total = smooth_half[0] + 2.0 * jnp.sum(smooth_half[1:])
    smooth = full_taps(smooth_half) / norm_total
    size_x, size_y, size_z = source.shape
    cells = float(source.size * lax.axis_size("gx") * lax.axis_size("gy") * lax.axis_size("gz"))
    totals = lax.psum((jnp.sum(source), jnp.sum(target)), AXES)
    first = source * (cells / totals[0])
    second = target * (cells / totals[1])
    first_wide = padded_2(first, (("gx", 0), ("gy", 1), ("gz", 2)), radius)
    scaling_v = jnp.ones_like(source)
    errors = []
    for step in range(ITERS):
        padded = padded_2(scaling_v, (("gx", 0), ("gy", 1), ("gz", 2)), 2 * radius)
        kv_wide = three_passes(
            padded, kern, size_x + 2 * radius, size_y + 2 * radius, size_z + 2 * radius
        )
        u_wide = first_wide / kv_wide
        ku = three_passes(u_wide, kern, size_x, size_y, size_z)
        local_err = jnp.sum(jnp.abs(scaling_v * ku - second))
        errors.append(lax.psum(local_err, AXES) / cells)
        scaling_v = second / ku
    mismatch = jnp.stack(errors)
    padded = padded_2(scaling_v, (("gx", 0), ("gy", 1), ("gz", 2)), radius)
    pass_k = along(padded, kern, 0, size_x)
    pass_g = along(padded, slope, 0, size_x)
    kk = along(pass_k, kern, 1, size_y)
    kg = along(pass_k, slope, 1, size_y)
    gk = along(pass_g, kern, 1, size_y)
    kvol = along(kk, kern, 2, size_z)
    znum = along(kk, slope, 2, size_z)
    ynum = along(kg, kern, 2, size_z)
    xnum = along(gk, kern, 2, size_z)
    raw = jnp.stack([xnum, ynum, znum]) / kvol
    padded = padded_2(raw, (("gx", 1), ("gy", 2), ("gz", 3)), reach)
    padded = along(padded, smooth, 1, size_x)
    padded = along(padded, smooth, 2, size_y)
    displacement = along(padded, smooth, 3, size_z)
    return (displacement, mismatch)


class Plan:
    def __init__(self, mesh, bx, by, bz, radius, reach):
        self.nx, self.ny, self.nc = mesh["gx"], mesh["gy"], mesh["gz"]
        self.bx, self.by, self.bz = bx, by, bz
        self.R, self.Q = radius, reach
        self.P = self.nx * self.ny
        self.X, self.Y, self.Z = bx * self.nx, by * self.ny, bz * self.nc
        self.S = self.Z // self.P
        self.H = 4 * radius
        self.gs = LANES // by if by <= LANES else 0
        self.XH = self.X // 2
        self.cells = float(self.X * self.Y * self.Z)

    def fits(self):
        return (
            self.nc == 2
            and self.ny >= 2
            and self.ny & (self.ny - 1) == 0
            and self.nx >= 2
            and self.bz == LANES
            and self.Y == LANES
            and self.gs == self.ny
            and self.bx == 2 * self.gs
            and self.Z == self.P * self.S
            and self.S == self.H
            and self.S % 8 == 0
            and self.R % 4 == 0
            and ITERS == 6
        )

    def spot(self, at):
        at %= self.P
        col, q = divmod(at, self.nx)
        return (q if col % 2 == 0 else self.nx - 1 - q), col ^ (col >> 1)

    def chip(self, at):
        i, j = self.spot(at)
        return i * self.ny + j

    def device(self, at, core):
        return self.chip(at) * self.nc + core


def swap_cores(plan, value):
    pairs = [(plan.device(at, c), plan.device(at, 1 - c)) for at in range(plan.P) for c in range(2)]
    return lax.ppermute(value, AXES, pairs)


def swap_even(plan, value):
    pairs = [(plan.device(at, c), plan.device(at ^ 1, c)) for at in range(plan.P) for c in range(2)]
    return lax.ppermute(value, AXES, pairs)


def swap_odd(plan, value):
    pairs = [
        (plan.device(at, c), plan.device(((at + 1) ^ 1) - 1, c))
        for at in range(plan.P)
        for c in range(2)
    ]
    return lax.ppermute(value, AXES, pairs)


def swap_sides(plan, value):
    pairs = [(plan.device(at, 0), plan.device(at - 1, 1)) for at in range(plan.P)]
    pairs += [(plan.device(at, 1), plan.device(at + 1, 0)) for at in range(plan.P)]
    return lax.ppermute(value, AXES, pairs)


def trade_chunks(value):
    rows, lanes = value.shape
    out = lax.all_to_all(value.reshape(rows, 1, lanes), ("gx", "gy"), 0, 0, tiled=True)
    return out.reshape(rows, lanes)


def place_of(plan):
    i, j = lax.axis_index("gx"), lax.axis_index("gy")
    at = jnp.int32(0)
    for place in range(plan.P):
        a, b = plan.spot(place)
        at = at + jnp.where((i == a) & (j == b), place, 0)
    return at.astype(jnp.int32)


def call(kernel, out_shape, n_smem, n_vmem, scratch=(), smem_out=0, n_any=0, any_out=0, aliases=None, name=None):
    vm, sm = pl.BlockSpec(memory_space=pltpu.VMEM), pl.BlockSpec(memory_space=pltpu.SMEM)
    hbm = pl.BlockSpec(memory_space=pltpu.HBM)
    out_specs = [vm] * (len(out_shape) - smem_out - any_out) + [sm] * smem_out + [hbm] * any_out
    return pl.pallas_call(
        kernel,
        out_shape=out_shape,
        in_specs=[sm] * n_smem + [vm] * n_vmem + [hbm] * n_any,
        out_specs=out_specs,
        scratch_shapes=list(scratch),
        input_output_aliases=aliases or {},
        compiler_params=pltpu.CompilerParams(vmem_limit_bytes=48 << 20),
        name=name,
    )


def f32(*shape):
    return jax.ShapeDtypeStruct(shape, jnp.float32)


def turn_groups(plan, parts):
    n, w = plan.gs, plan.by
    group = lax.broadcasted_iota(jnp.int32, parts[0].shape, 1) // w
    outs = []
    for a in range(n):
        total = parts[a]
        for b in range(n):
            if b != a:
                moved = pltpu.roll(parts[b], (w * (b - a)) % LANES, 1)
                total = jnp.where(group == b, moved, total)
        outs.append(total)
    return outs


def pack_kernel(plan, src_hbm, tgt_hbm, keep_ref, send_ref, stat_ref, src_ref, tgt_ref, sems):
    c = lax.axis_index("gz")
    gs = plan.gs
    copies = [
        pltpu.make_async_copy(src_hbm, src_ref, sems.at[0]),
        pltpu.make_async_copy(tgt_hbm, tgt_ref, sems.at[1]),
    ]
    for copy in copies:
        copy.start()
    sums = []
    for st, ref in enumerate((src_ref, tgt_ref)):
        copies[st].wait()
        for out, xg in ((keep_ref, c), (send_ref, 1 - c)):
            out[st] = ref[pl.ds(gs * xg, gs)].reshape(LANES, LANES).T
        row = jnp.sum(ref[...].reshape(plan.bx * plan.by, LANES), axis=0, keepdims=True)
        sums.append(row + pltpu.roll(row, LANES // 2, 1))
    stat_ref[...] = jnp.where(lane_at() < LANES // 2, *sums)


def lane_at():
    return lax.broadcasted_iota(jnp.int32, (1, LANES), 1)


def chunk_kernel(plan, keep_ref, recv_ref, stat_ref, out_ref):
    c = lax.axis_index("gz")
    half, S = plan.P // 2, plan.S
    size = 2 * S + 1

    def write(low_ref, high_ref):
        stat = stat_ref[...]
        for place in range(plan.P):
            ref, part = (low_ref, place) if place < half else (high_ref, place - half)
            base = size * plan.chip(place)
            for st in range(2):
                out_ref[base + S * st : base + S * st + S, :] = ref[st, S * part : S * part + S, :]
            out_ref[base + 2 * S : base + size, :] = stat

    pl.when(c == 0)(lambda: write(keep_ref, recv_ref))
    pl.when(c == 1)(lambda: write(recv_ref, keep_ref))


def unpack_kernel(plan, in_ref, s_ref, t_ref):
    S, gs, XH = plan.S, plan.gs, plan.XH
    size = 2 * S + 1
    for st, out_ref in enumerate((s_ref, t_ref)):
        for i in range(plan.nx):
            bases = [size * (i * plan.ny + j) + S * st for j in range(plan.ny)]
            parts = [in_ref[base : base + S, :] for base in bases]
            for xx, value in enumerate(turn_groups(plan, parts)):
                out_ref[i * gs + xx] = value
    t_ref[XH] = jnp.zeros((S, LANES), jnp.float32)
    t_ref[XH, :1, :] = sum_rows(plan, in_ref, size)


def sum_rows(plan, ref, size):
    total = ref[size - 1 : size, :]
    for p in range(1, plan.P):
        total = total + ref[size * p + size - 1 : size * p + size, :]
    return total


def banded(taps, n, odd):
    row = lax.broadcasted_iota(jnp.int32, (n, n), 0)
    col = lax.broadcasted_iota(jnp.int32, (n, n), 1)
    gap = row - col
    total = jnp.zeros((n, n), jnp.float32)
    for d, tap in enumerate(taps):
        if odd:
            if d:
                total = jnp.where(gap == d, d * tap, total)
                total = jnp.where(gap == -d, -(d * tap), total)
        else:
            total = jnp.where(jnp.abs(gap) == d, tap, total)
    return total


def halves(value):
    high = value.astype(jnp.bfloat16)
    return high, (value - high.astype(jnp.float32)).astype(jnp.bfloat16)


def quad(matrix):
    high, low = halves(matrix)
    row = jnp.concatenate([high, low], axis=1)
    return jnp.concatenate([row, row], axis=0)


def lanes_times(value, quad_ref):
    high, low = halves(value)
    both = jnp.concatenate([high, low], axis=1)
    out = jnp.dot(both, quad_ref[...], preferred_element_type=jnp.float32)
    return out[:, :LANES] + out[:, LANES:]


def even_sum(load, taps, mid):
    total = taps[0] * load(mid)
    for d in range(1, len(taps)):
        total = total + taps[d] * (load(mid - d) + load(mid + d))
    return total


def unit_sum(load, taps, mid):
    total = load(mid)
    for d in range(1, len(taps)):
        total = total + taps[d] * (load(mid - d) + load(mid + d))
    return total


def odd_sum(load, taps, mid):
    total = taps[1] * (load(mid + 1) - load(mid - 1))
    for d in range(2, len(taps)):
        total = total + (d * taps[d]) * (load(mid + d) - load(mid - d))
    return total


MANY = 8


def run_passes(plan, passes):
    chunks = range(0, plan.X, MANY)
    for base in chunks:
        passes[0][0](base)
    for (_, matmul_part, emit_part), after in zip(passes, passes[1:] + [None]):
        done = None

        def close(pair):
            emit_part(*pair)
            if after is not None:
                after[0](pair[0])

        for base in chunks:
            out = matmul_part(base)
            if done is not None:
                close(done)
            done = (base, out)
        close(done)


def kernel_pass(plan, taps, quad_ref, in_ref, zb_ref, rows, emit):
    R = plan.R

    def z_part(base):
        for x in range(base, base + MANY):
            zb_ref[R + x, :rows, :] = unit_sum(lambda j: in_ref[x, j : j + rows, :], taps, R)

    def matmul_part(base):
        parts = [
            unit_sum(lambda j: zb_ref[base + q + j, :rows, :], taps, R) for q in range(MANY)
        ]
        return lanes_times(jnp.concatenate(parts, axis=0), quad_ref)

    def emit_part(base, out):
        for q in range(MANY):
            emit(base + q, out[q * rows : (q + 1) * rows])

    return z_part, matmul_part, emit_part


def inside(plan, at, off, rows):
    z = lax.broadcasted_iota(jnp.int32, (rows, LANES), 0) + (at * plan.S - plan.H + off)
    return (z >= 0) & (z < plan.Z)


def scale_step(plan, at, taps, quad_ref, zb, src, top, dst, over, off, start, rows):
    mask = inside(plan, at, off + start, rows)
    src = src.at[:, pl.ds(top, rows + 2 * plan.R), :]
    lead = (off + 7) // 8 * 8
    over = over.at[:, pl.ds(start, rows + lead), :]

    def emit(x, value):
        dst[x, pl.ds(start, rows), :] = jnp.where(mask, over[x, off : off + rows, :] / value, 0.0)

    return kernel_pass(plan, taps, quad_ref, src, zb, rows, emit)


def clear_edges(ref, edge, size):
    blank = jnp.zeros((edge,) + ref.shape[1:], jnp.float32)
    ref[:edge] = blank
    ref[edge + size :] = blank


def prep_kernel(plan, k_ref, s_ref, own, taps_ref, quad_ref, slope_ref, smooth_ref, high_ref, low_ref):
    del own
    R, Q = plan.R, plan.Q
    taps = [jnp.zeros((1, LANES), jnp.float32) + k_ref[d] for d in range(R + 1)]
    taps = [jnp.ones((1, LANES), jnp.float32)] + [tap / taps[0] for tap in taps[1:]]
    stap = smooth_taps(s_ref, Q)
    for d in range(R + 1):
        taps_ref[d] = jnp.broadcast_to(taps[d], (8, LANES))
    for d in range(Q + 1):
        taps_ref[R + 1 + d] = jnp.broadcast_to(stap[d], (8, LANES))
    quad_ref[...] = quad(banded(taps, LANES, False))
    slope_ref[...] = quad(banded(taps, LANES, True))
    smooth_ref[...] = quad(banded(stap, LANES, False))
    wide = [jnp.concatenate([t] * (plan.Z // LANES), axis=1) for t in stap]
    high_ref[...], low_ref[...] = halves(banded(wide, plan.Z, False))


def kernel_taps(plan, taps_ref):
    return [taps_ref[d, :1, :] for d in range(plan.R + 1)]


def gaps_of(plan, tot, tw, olds, news):
    S, H = plan.S, plan.H
    first_half = lane_at() < LANES // 2
    both = tot[:1, :]
    sum_s = jnp.sum(jnp.where(first_half, both, 0.0), axis=1, keepdims=True)
    sum_t = jnp.sum(jnp.where(first_half, 0.0, both), axis=1, keepdims=True)
    scale_s = plan.cells / jnp.broadcast_to(sum_s, (1, LANES))
    scale_t = plan.cells / jnp.broadcast_to(sum_t, (1, LANES))

    def mid(ref, x):
        edge = (ref.shape[1] - S) // 2
        return ref[x, edge : edge + S, :]

    def p_step(x, carry):
        t = mid(tw, x)
        want = scale_t * t
        have = scale_s * t
        result = []
        for part, old, new in zip(carry, olds, news):
            value = have / mid(new, x)
            if old is not None:
                value = value * mid(old, x)
            gap = jnp.abs(value - want)
            for r in range(0, S, 8):
                part = part + gap[r : r + 8]
            result.append(part)
        return tuple(result)

    zero = jnp.zeros((8, LANES), jnp.float32)
    gaps = lax.fori_loop(0, plan.X, p_step, (zero,) * len(news), unroll=4)
    return [jnp.sum(g, keepdims=True) for g in gaps]


def in_lanes(values, first=0):
    row = jnp.zeros((1, LANES), jnp.float32)
    for t, value in enumerate(values):
        row = jnp.where(lane_at() == first + t, value, row)
    return row


def gaps_kernel(plan, tot, tw, v1, v2, v3, v4, out_ref):
    out_ref[...] = in_lanes(gaps_of(plan, tot, tw, (None, v1, v2, v3), (v1, v2, v3, v4)))


def spread_halves(plan, at, own, even, odd, own2, even2, odd2, win):
    S, H, gs = plan.S, plan.H, plan.gs
    c = lax.axis_index("gz")

    def spread(low, high):
        for k, (mid, core) in enumerate(((own, c), (own2, 1 - c))):
            for i in range(plan.nx):
                x, here = plan.bx * i + gs * core, pl.ds(i * gs, gs)
                win[pl.ds(x, gs), H : H + S, :] = mid[here]
                win[pl.ds(x, gs), :H, :] = low[k][here]
                win[pl.ds(x, gs), H + S :, :] = high[k][here]

    pl.when(at % 2 == 0)(lambda: spread((odd, odd2), (even, even2)))
    pl.when(at % 2 == 1)(lambda: spread((even, even2), (odd, odd2)))


def open_kernel(plan, taps_ref, quad_ref, own, even, odd, own2, even2, odd2, sw, ku, u, zb):
    R, S, H, X = plan.R, plan.S, plan.H, plan.X
    at = place_of(plan)
    taps = kernel_taps(plan, taps_ref)
    clear_edges(zb, R, X)
    spread_halves(plan, at, own, even, odd, own2, even2, odd2, sw)

    def reach_sum(place, size):
        total = jnp.ones(place.shape, jnp.float32)
        for d in range(1, R + 1):
            total = total + jnp.where(place - d >= 0, taps[d], 0.0)
            total = total + jnp.where(place + d < size, taps[d], 0.0)
        return total

    rows = S + 2 * H
    mask = inside(plan, at, 0, rows)
    y_at = lax.broadcasted_iota(jnp.int32, (rows, LANES), 1)
    z_at = lax.broadcasted_iota(jnp.int32, (rows, LANES), 0) + (at * S - H)
    plane = reach_sum(z_at, plan.Z) * (reach_sum(y_at, plan.Y) * taps_ref[0, :1, :])

    def u_step(x, carry):
        cx = reach_sum(jnp.zeros((1, LANES), jnp.int32) + x, X)
        u[x] = jnp.where(mask, sw[x] / (plane * cx), 0.0)
        return carry

    lax.fori_loop(0, X, u_step, 0, unroll=2)

    def emit(x, value):
        ku[x] = value

    run_passes(plan, [kernel_pass(plan, taps, quad_ref, u, zb, rows - 2 * R, emit)])


def first_kernel(plan, taps_ref, quad_ref, own, even, odd, own2, even2, odd2, sw, ku,
                 tw, v, v2, u_out, tot, u, zb, zc):
    R, S, H, X, XH = plan.R, plan.S, plan.H, plan.X, plan.XH
    at = place_of(plan)
    taps = kernel_taps(plan, taps_ref)
    clear_edges(zb, R, X)
    clear_edges(zc, R, X)
    spread_halves(plan, at, own, even, odd, own2, even2, odd2, tw)
    tot[...] = own[XH, :1, :] + own2[XH, :1, :]
    rows = S + 2 * H - 2 * R
    mask = inside(plan, at, R, rows)

    def v_step(x, carry):
        v[x] = jnp.where(mask, tw[x, R : R + rows, :] / ku[x], 0.0)
        return carry

    lax.fori_loop(0, X, v_step, 0, unroll=4)
    step = functools.partial(scale_step, plan, at, taps, quad_ref)
    run_passes(plan, [
        step(zb, v, 0, u, sw, 2 * R, 0, rows - 2 * R),
        step(zc, u, 0, v2, tw, 3 * R, 0, rows - 4 * R),
        step(zb, v2, 0, u_out, sw, 4 * R, 0, rows - 6 * R),
    ])


def early_kernel(plan, taps_ref, quad_ref, mine, side, sw, tw, v, u, v2, win, zb, zc):
    R, S, H = plan.R, plan.S, plan.H
    c = lax.axis_index("gz")
    at = place_of(plan)
    taps = kernel_taps(plan, taps_ref)
    clear_edges(zb, R, plan.X)
    clear_edges(zc, R, plan.X)
    real = jnp.where(jnp.where(c == 0, at > 0, at < plan.P - 1), 1.0, 0.0)
    win[:, pl.ds(pl.multiple_of(H * c, 8), H), :] = side[...] * real
    win[:, pl.ds(pl.multiple_of(H * (1 - c), 8), S), :] = mine[...]
    step = functools.partial(scale_step, plan, at, taps, quad_ref)
    from_ = pl.multiple_of(S * c, 8)
    run_passes(plan, [
        step(zb, win, 0, v, tw, R, from_, S + H - 2 * R),
        step(zc, v, from_, u, sw, 2 * R, from_, S + H - 4 * R),
        step(zb, u, from_, v2, tw, 3 * R, from_, S + H - 6 * R),
    ])


def late_rows(plan, at, taps, quad_ref, mine, other, sw, tw, v, u, v2, win, zb, zc):
    R, S, H = plan.R, plan.S, plan.H
    c = lax.axis_index("gz")
    real = jnp.where(jnp.where(c == 1, at > 0, at < plan.P - 1), 1.0, 0.0)
    half = S // 2

    def lay(other_at, mine_at, mine_from):
        win[:, other_at : other_at + H, :] = other[...] * real
        win[:, mine_at : mine_at + half, :] = mine[:, mine_from : mine_from + half, :]

    pl.when(c == 0)(lambda: lay(half, 0, half))
    pl.when(c == 1)(lambda: lay(0, H, 0))
    step = functools.partial(scale_step, plan, at, taps, quad_ref)
    first = pl.multiple_of((S + H - 2 * R) * (1 - c), 8)
    second = pl.multiple_of((S + H - 4 * R) * (1 - c), 8)
    third = pl.multiple_of((S + H - 6 * R) * (1 - c), 8)
    return [
        step(zb, win, 0, v, tw, R, first, S),
        step(zc, v, second, u, sw, 2 * R, second, S),
        step(zb, u, third, v2, tw, 3 * R, third, S),
    ]


def late_kernel(plan, taps_ref, quad_ref, mine, other, sw, tw, v_in, u_in, v2_in,
                v, u, v2, u_out, win, zb, zc):
    del v_in, u_in, v2_in
    R, S = plan.R, plan.S
    at = place_of(plan)
    taps = kernel_taps(plan, taps_ref)
    clear_edges(zb, R, plan.X)
    clear_edges(zc, R, plan.X)
    passes = late_rows(plan, at, taps, quad_ref, mine, other, sw, tw, v, u, v2, win, zb, zc)
    passes.append(scale_step(plan, at, taps, quad_ref, zc, v2, 0, u_out, sw, 4 * R, 0, S))
    run_passes(plan, passes)


def smooth_taps(s_ref, reach):
    total = s_ref[0]
    tail = s_ref[1]
    for d in range(2, reach + 1):
        tail = tail + s_ref[d]
    scale = 1.0 / (jnp.zeros((1, LANES), jnp.float32) + (total + 2.0 * tail))
    return [scale * s_ref[d] for d in range(reach + 1)]


def last_kernel(plan, taps_ref, quad_ref, slope_ref, smooth_ref, mine, other, sw, tw, prev,
                gaps, tot, v_in, u_in, v2_in, v, u, v2, out_ref, win, zb, zc, zg, raw):
    del v_in, u_in, v2_in
    R, S, X, gs, Q = plan.R, plan.S, plan.X, plan.gs, plan.Q
    size = 3 * S + 1
    c = lax.axis_index("gz")
    at = place_of(plan)
    taps = kernel_taps(plan, taps_ref)
    stap = [taps_ref[R + 1 + d, :1, :] for d in range(Q + 1)]
    clear_edges(zb, R, X)
    clear_edges(zc, R, X)
    clear_edges(zg, R, X)
    for comp in range(3):
        clear_edges(raw.at[comp], Q, X)
    passes = late_rows(plan, at, taps, quad_ref, mine, other, sw, tw, v, u, v2, win, zb, zc)

    def z_part(base):
        for x in range(base, base + MANY):
            load = lambda j: v2[x, j : j + S, :]
            zc[R + x, :S, :] = unit_sum(load, taps, R)
            zg[R + x, :S, :] = odd_sum(load, taps, R)

    def matmul_part(base):
        kk, gk, kg = [], [], []
        for q in range(MANY):
            flat = lambda j: zc[base + q + j, :S, :]
            kk.append(unit_sum(flat, taps, R))
            gk.append(odd_sum(flat, taps, R))
            kg.append(unit_sum(lambda j: zg[base + q + j, :S, :], taps, R))
        kk, gk, kg = (jnp.concatenate(part, axis=0) for part in (kk, gk, kg))
        nums = lanes_times(gk, quad_ref), lanes_times(kk, slope_ref), lanes_times(kg, quad_ref)
        return lanes_times(kk, quad_ref), nums

    def emit_part(base, out):
        kvol, nums = out
        for comp, num in enumerate(nums):
            value = num / kvol
            for q in range(MANY):
                raw[comp, Q + base + q] = value[q * S : (q + 1) * S]

    run_passes(plan, passes + [(z_part, matmul_part, emit_part)])

    for i in range(plan.nx):
        x = plan.bx * i + gs * c
        for comp in range(3):
            parts = []
            for xx in range(gs):
                parts.append(even_sum(lambda j: raw[comp, x + xx + j], stap, Q))
            flat = lanes_times(jnp.concatenate(parts, axis=0), smooth_ref)
            turned = turn_groups(plan, [flat[xx * S : (xx + 1) * S] for xx in range(gs)])
            for j in range(plan.ny):
                base = size * (i * plan.ny + j) + comp * S
                out_ref[base : base + S, :] = turned[j]

    rows = gaps_of(plan, tot, tw, (prev, v), (v, v2))
    stat = gaps[...] + in_lanes(rows, ITERS - 2)
    for p in range(plan.P):
        out_ref[size * p + 3 * S : size * (p + 1), :] = stat


def smooth_z(plan, core, high_ref, low_ref, in_ref, data, emit):
    S = plan.S
    size = 3 * S + 1
    for place in range(plan.P):
        for comp in range(3):
            base = size * plan.chip(place) + comp * S
            data[S * place : S * place + S, comp * LANES : (comp + 1) * LANES] = in_ref[
                base : base + S, :
            ]
    rows = pl.ds(pl.multiple_of(core * LANES, LANES), LANES)
    m_high, m_low = high_ref[rows, :], low_ref[rows, :]
    d_high, d_low = halves(data[...])
    dot = functools.partial(jnp.dot, preferred_element_type=jnp.float32)
    out = dot(m_high, d_high) + (dot(m_high, d_low) + dot(m_low, d_high))
    for comp in range(3):
        emit(comp, out[:, comp * LANES : (comp + 1) * LANES].T)


def away_kernel(plan, high_ref, low_ref, in_ref, send_ref, data):
    def emit(comp, value):
        send_ref[comp] = value

    smooth_z(plan, 1 - lax.axis_index("gz"), high_ref, low_ref, in_ref, data, emit)


def home_kernel(plan, high_ref, low_ref, in_ref, mis_ref, out_hbm, data, keep, sem):
    c = lax.axis_index("gz")
    gs = plan.gs

    def emit(comp, value):
        keep[comp] = value.reshape(gs, plan.by, LANES)

    smooth_z(plan, c, high_ref, low_ref, in_ref, data, emit)
    copy = pltpu.make_async_copy(keep, out_hbm.at[:, pl.ds(gs * c, gs)], sem)
    copy.start()
    gone = sum_rows(plan, in_ref, 3 * plan.S + 1) / plan.cells
    for t in range(ITERS):
        mis_ref[t] = jnp.sum(jnp.where(lane_at() == t, gone, 0.0))
    copy.wait()


def place_kernel(plan, recv_ref, in_hbm, out_hbm, sem):
    del in_hbm
    c = lax.axis_index("gz")
    copy = pltpu.make_async_copy(recv_ref, out_hbm.at[:, pl.ds(plan.gs * (1 - c), plan.gs)], sem)
    copy.start()
    copy.wait()


def slab_shards(plan, source, target, kernel_half, smooth_half):
    R, S, H, X, XH, Pn, Z = plan.R, plan.S, plan.H, plan.X, plan.XH, plan.P, plan.Z
    bind = lambda kernel: functools.partial(kernel, plan)
    half = f32(2, LANES, LANES)
    vm = lambda *shape: pltpu.VMEM(shape, jnp.float32)
    keep, send, stat = call(
        bind(pack_kernel), [half, half, f32(1, LANES)], 0, 0,
        [vm(*source.shape), vm(*source.shape), pltpu.SemaphoreType.DMA((2,))], n_any=2, name="pack",
    )(*(pltpu.with_memory_space_constraint(a, pltpu.HBM) for a in (source, target)))
    recv = swap_cores(plan, send)
    (chunks,) = call(bind(chunk_kernel), [f32(Pn * (2 * S + 1), LANES)], 0, 3, name="chunks")(
        keep, recv, stat
    )
    spread = trade_chunks(chunks)
    own_s, own_t = call(
        bind(unpack_kernel), [f32(XH, S, LANES), f32(XH + 1, S, LANES)], 0, 1, name="unpack"
    )(spread)
    square = jax.ShapeDtypeStruct((2 * LANES, 2 * LANES), jnp.bfloat16)
    table = jax.ShapeDtypeStruct((Z, Z), jnp.bfloat16)
    taps, quad_k, quad_g, quad_s, high, low = call(
        bind(prep_kernel), [f32(plan.R + plan.Q + 2, 8, LANES), square, square, square, table, table],
        2, 0, n_any=1, name="prep",
    )(kernel_half, smooth_half, own_s)
    even_s, odd_s = swap_even(plan, own_s), swap_odd(plan, own_s)
    far_t, taps = lax.optimization_barrier((own_t, taps))
    even_t, odd_t = swap_even(plan, far_t), swap_odd(plan, far_t)
    own2_s, own2_t = swap_cores(plan, own_s), swap_cores(plan, own_t)
    even_s, odd_s, taps = lax.optimization_barrier((even_s, odd_s, taps))
    halos_s = swap_cores(plan, even_s), swap_cores(plan, odd_s)

    slab = f32(X, S, LANES)
    width = S + 2 * H
    wide, v_shape, u_shape, v2_shape = (f32(X, width - 2 * k * R, LANES) for k in (0, 1, 2, 3))
    zb = vm(X + 2 * R, width - 2 * R, LANES)
    sw, ku = call(
        bind(open_kernel), [wide, v_shape], 0, 8, [vm(*wide.shape), zb], name="open"
    )(taps, quad_k, own_s, even_s, odd_s, own2_s, *halos_s)
    even_t, odd_t, ku = lax.optimization_barrier((even_t, odd_t, ku))
    halos_t = swap_cores(plan, even_t), swap_cores(plan, odd_t)
    tw, v1, v2, u, tot = call(
        bind(first_kernel), [wide, v_shape, v2_shape, slab, f32(1, LANES)], 0, 10,
        [vm(*u_shape.shape), zb, zb], name="first",
    )(taps, quad_k, own_t, even_t, odd_t, own2_t, *halos_t, sw, ku)

    def early(u, side):
        return call(
            bind(early_kernel), [v_shape, u_shape, v2_shape], 0, 6,
            [vm(X, S + H, LANES), zb, zb], name="early",
        )(taps, quad_k, u, side, sw, tw)

    rest = vm(X, H + S // 2, LANES)
    side = swap_sides(plan, u)
    other = swap_cores(plan, side)
    v3, u4, v4 = early(u, side)
    v3, _, v4, u = call(
        bind(late_kernel), [v_shape, u_shape, v2_shape, slab], 0, 9, [rest, zb, zb],
        aliases={6: 0, 7: 1, 8: 2}, name="late",
    )(taps, quad_k, u, other, sw, tw, v3, u4, v4)
    side = swap_sides(plan, u)
    (gaps,) = call(bind(gaps_kernel), [f32(1, LANES)], 0, 6, name="gaps")(tot, tw, v1, v2, v3, v4)
    side, gaps = lax.optimization_barrier((side, gaps))
    other = swap_cores(plan, side)
    v5, u6, v6 = early(u, side)
    *_, chunks = call(
        bind(last_kernel), [v_shape, u_shape, v2_shape, f32(Pn * (3 * S + 1), LANES)], 0, 14,
        [rest, zb, zb, vm(X + 2 * R, S, LANES), vm(3, X + 2 * plan.Q, S, LANES)],
        aliases={11: 0, 12: 1, 13: 2}, name="last",
    )(taps, quad_k, quad_g, quad_s, u, other, sw, tw, v4, gaps, tot, v5, u6, v6)
    spread = trade_chunks(chunks)
    data = vm(Z, 3 * LANES)
    (send,) = call(bind(away_kernel), [f32(3, LANES, LANES)], 0, 3, [data], name="away")(
        high, low, spread
    )
    half = (3, plan.gs, plan.by, LANES)
    recv = swap_cores(plan, send.reshape(half))
    whole = f32(3, plan.bx, plan.by, LANES)
    mismatch, displacement = call(
        bind(home_kernel), [f32(ITERS), whole], 0, 3, [data, vm(*half), pltpu.SemaphoreType.DMA(())],
        smem_out=1, any_out=1, name="home",
    )(high, low, spread)
    (displacement,) = call(
        bind(place_kernel), [whole], 0, 1, [pltpu.SemaphoreType.DMA(())], n_any=1, any_out=1,
        aliases={1: 0}, name="place",
    )(recv, displacement)
    return displacement, mismatch


def shards(sizes, source, target, kernel_half, smooth_half):
    plan = Plan(sizes, *source.shape, kernel_half.shape[0] - 1, smooth_half.shape[0] - 1)
    if plan.fits():
        return slab_shards(plan, source, target, kernel_half, smooth_half)
    return block_shards(source, target, kernel_half, smooth_half)


def solution(mesh):
    in_specs = (P("gx", "gy", "gz"), P("gx", "gy", "gz"), P(), P())
    out_specs = (P(None, "gx", "gy", "gz"), P())
    body = functools.partial(shards, dict(mesh.shape))
    return jax.shard_map(body, mesh=mesh, in_specs=in_specs, out_specs=out_specs, check_vma=False)
```

```python
import functools

import jax
import jax.numpy as jnp
from jax import lax
from jax.experimental import pallas as pl
from jax.experimental.pallas import tpu as pltpu
from jax.sharding import PartitionSpec as P


ITERS = 6
LANES = 128
AXES = ("gx", "gy", "gz")


def padded_2(block, sides, width):
    for axis, dim in sides:
        count = lax.axis_size(axis)
        forward = [(i, i + 1) for i in range(count - 1)]
        backward = [(target, source) for source, target in forward]
        low = lax.ppermute(
            lax.slice_in_dim(block, block.shape[dim] - width, None, axis=dim), axis, forward
        )
        high = lax.ppermute(lax.slice_in_dim(block, 0, width, axis=dim), axis, backward)
        block = jnp.concatenate([low, block, high], axis=dim)
    return block


def full_taps(half):
    return jnp.concatenate([half[:0:-1], half])


def along(padded, taps, axis, count):
    width = taps.shape[0]
    total = taps[0] * lax.slice_in_dim(padded, 0, count, axis=axis)
    for j in range(1, width):
        total = total + taps[j] * lax.slice_in_dim(padded, j, j + count, axis=axis)
    return total


def three_passes(padded, taps, size_x, size_y, size_z):
    padded = along(padded, taps, 0, size_x)
    padded = along(padded, taps, 1, size_y)
    return along(padded, taps, 2, size_z)


def block_shards(source, target, kernel_half, smooth_half):
    kern = full_taps(kernel_half)
    radius = kernel_half.shape[0] - 1
    reach = smooth_half.shape[0] - 1
    offsets = jnp.arange(-radius, radius + 1).astype(jnp.float32)
    slope = offsets * kern
    norm_total = smooth_half[0] + 2.0 * jnp.sum(smooth_half[1:])
    smooth = full_taps(smooth_half) / norm_total
    size_x, size_y, size_z = source.shape
    cells = float(source.size * lax.axis_size("gx") * lax.axis_size("gy") * lax.axis_size("gz"))
    totals = lax.psum((jnp.sum(source), jnp.sum(target)), AXES)
    first = source * (cells / totals[0])
    second = target * (cells / totals[1])
    first_wide = padded_2(first, (("gx", 0), ("gy", 1), ("gz", 2)), radius)
    scaling_v = jnp.ones_like(source)
    errors = []
    for _ in range(ITERS):
        padded = padded_2(scaling_v, (("gx", 0), ("gy", 1), ("gz", 2)), 2 * radius)
        kv_wide = three_passes(
            padded, kern, size_x + 2 * radius, size_y + 2 * radius, size_z + 2 * radius
        )
        u_wide = first_wide / kv_wide
        ku = three_passes(u_wide, kern, size_x, size_y, size_z)
        local_err = jnp.sum(jnp.abs(scaling_v * ku - second))
        errors.append(lax.psum(local_err, AXES) / cells)
        scaling_v = second / ku
    mismatch = jnp.stack(errors)
    padded = padded_2(scaling_v, (("gx", 0), ("gy", 1), ("gz", 2)), radius)
    pass_k = along(padded, kern, 0, size_x)
    pass_g = along(padded, slope, 0, size_x)
    kk = along(pass_k, kern, 1, size_y)
    kg = along(pass_k, slope, 1, size_y)
    gk = along(pass_g, kern, 1, size_y)
    kvol = along(kk, kern, 2, size_z)
    znum = along(kk, slope, 2, size_z)
    ynum = along(kg, kern, 2, size_z)
    xnum = along(gk, kern, 2, size_z)
    raw = jnp.stack([xnum, ynum, znum]) / kvol
    padded = padded_2(raw, (("gx", 1), ("gy", 2), ("gz", 3)), reach)
    padded = along(padded, smooth, 1, size_x)
    padded = along(padded, smooth, 2, size_y)
    displacement = along(padded, smooth, 3, size_z)
    return (displacement, mismatch)


class Plan:
    def __init__(self, mesh, bx, by, bz, radius, reach):
        self.nx, self.ny, self.nc = mesh["gx"], mesh["gy"], mesh["gz"]
        self.bx, self.by, self.bz = bx, by, bz
        self.R, self.Q = radius, reach
        self.P = self.nx * self.ny
        self.X, self.Y, self.Z = bx * self.nx, by * self.ny, bz * self.nc
        self.S = self.Z // self.P
        self.H = 4 * radius
        self.gs = LANES // by if by <= LANES else 0
        self.XH = self.X // 2
        self.cells = float(self.X * self.Y * self.Z)

    def fits(self):
        return (
            self.nc == 2
            and self.ny >= 2
            and self.ny & (self.ny - 1) == 0
            and self.nx >= 2
            and self.bz == LANES
            and self.Y == LANES
            and self.gs == self.ny
            and self.bx == 2 * self.gs
            and self.Z == self.P * self.S
            and self.S == self.H
            and self.S % 8 == 0
            and self.R % 4 == 0
            and ITERS == 6
        )

    def spot(self, at):
        at %= self.P
        col, q = divmod(at, self.nx)
        return (q if col % 2 == 0 else self.nx - 1 - q), col ^ (col >> 1)

    def chip(self, at):
        i, j = self.spot(at)
        return i * self.ny + j

    def device(self, at, core):
        return self.chip(at) * self.nc + core


def swap_cores(plan, value):
    pairs = [(plan.device(at, c), plan.device(at, 1 - c)) for at in range(plan.P) for c in range(2)]
    return lax.ppermute(value, AXES, pairs)


def swap_even(plan, value):
    pairs = [(plan.device(at, c), plan.device(at ^ 1, c)) for at in range(plan.P) for c in range(2)]
    return lax.ppermute(value, AXES, pairs)


def swap_odd(plan, value):
    pairs = [
        (plan.device(at, c), plan.device(((at + 1) ^ 1) - 1, c))
        for at in range(plan.P)
        for c in range(2)
    ]
    return lax.ppermute(value, AXES, pairs)


def swap_sides(plan, value):
    pairs = [(plan.device(at, 0), plan.device(at - 1, 1)) for at in range(plan.P)]
    pairs += [(plan.device(at, 1), plan.device(at + 1, 0)) for at in range(plan.P)]
    return lax.ppermute(value, AXES, pairs)


def trade_chunks(value):
    rows, lanes = value.shape
    out = lax.all_to_all(value.reshape(rows, 1, lanes), ("gx", "gy"), 0, 0, tiled=True)
    return out.reshape(rows, lanes)


def place_of(plan):
    i, j = lax.axis_index("gx"), lax.axis_index("gy")
    at = jnp.int32(0)
    for place in range(plan.P):
        a, b = plan.spot(place)
        at = at + jnp.where((i == a) & (j == b), place, 0)
    return at.astype(jnp.int32)


def call(kernel, out_shape, n_smem, n_vmem, scratch=(), smem_out=0, n_any=0, any_out=0, aliases=None):
    vm, sm = pl.BlockSpec(memory_space=pltpu.VMEM), pl.BlockSpec(memory_space=pltpu.SMEM)
    hbm = pl.BlockSpec(memory_space=pltpu.HBM)
    out_specs = [vm] * (len(out_shape) - smem_out - any_out) + [sm] * smem_out + [hbm] * any_out
    return pl.pallas_call(
        kernel,
        out_shape=out_shape,
        in_specs=[sm] * n_smem + [vm] * n_vmem + [hbm] * n_any,
        out_specs=out_specs,
        scratch_shapes=list(scratch),
        input_output_aliases=aliases or {},
        compiler_params=pltpu.CompilerParams(vmem_limit_bytes=48 << 20),
    )


def f32(*shape):
    return jax.ShapeDtypeStruct(shape, jnp.float32)


def turn_groups(plan, parts):
    n, w = plan.gs, plan.by
    group = lax.broadcasted_iota(jnp.int32, parts[0].shape, 1) // w
    outs = []
    for a in range(n):
        total = parts[a]
        for b in range(n):
            if b != a:
                moved = pltpu.roll(parts[b], (w * (b - a)) % LANES, 1)
                total = jnp.where(group == b, moved, total)
        outs.append(total)
    return outs


def pack_kernel(plan, src_hbm, tgt_hbm, keep_ref, stat_ref, src_ref, tgt_ref, sems):
    c = lax.axis_index("gz")
    copies = [
        pltpu.make_async_copy(src_hbm, src_ref, sems.at[0]),
        pltpu.make_async_copy(tgt_hbm, tgt_ref, sems.at[1]),
    ]
    for copy in copies:
        copy.start()
    sums = []
    for st, ref in enumerate((src_ref, tgt_ref)):
        copies[st].wait()
        keep_ref[st] = ref[pl.ds(plan.gs * c, plan.gs)].reshape(LANES, LANES).T
        row = jnp.sum(ref[...].reshape(plan.bx * plan.by, LANES), axis=0, keepdims=True)
        sums.append(row + pltpu.roll(row, LANES // 2, 1))
    stat_ref[...] = jnp.where(lane_at() < LANES // 2, *sums)


def lane_at():
    return lax.broadcasted_iota(jnp.int32, (1, LANES), 1)


def chunk_kernel(plan, keep_ref, src_ref, tgt_ref, stat_ref, out_ref, recv_ref):
    c = lax.axis_index("gz")
    half, S = plan.P // 2, plan.S
    size = 2 * S + 1
    for st, ref in enumerate((src_ref, tgt_ref)):
        recv_ref[st] = ref[pl.ds(plan.gs * c, plan.gs)].reshape(LANES, LANES).T

    def write(low_ref, high_ref):
        stat = stat_ref[...]
        for place in range(plan.P):
            ref, part = (low_ref, place) if place < half else (high_ref, place - half)
            base = size * plan.chip(place)
            for st in range(2):
                out_ref[base + S * st : base + S * st + S, :] = ref[st, S * part : S * part + S, :]
            out_ref[base + 2 * S : base + size, :] = stat

    pl.when(c == 0)(lambda: write(keep_ref, recv_ref))
    pl.when(c == 1)(lambda: write(recv_ref, keep_ref))


def unpack_kernel(plan, in_ref, s_ref, t_ref):
    S, gs, XH = plan.S, plan.gs, plan.XH
    size = 2 * S + 1
    for st, out_ref in enumerate((s_ref, t_ref)):
        for i in range(plan.nx):
            bases = [size * (i * plan.ny + j) + S * st for j in range(plan.ny)]
            parts = [in_ref[base : base + S, :] for base in bases]
            for xx, value in enumerate(turn_groups(plan, parts)):
                out_ref[i * gs + xx] = value
    t_ref[XH] = jnp.zeros((S, LANES), jnp.float32)
    t_ref[XH, :1, :] = sum_rows(plan, in_ref, size)


def sum_rows(plan, ref, size):
    total = ref[size - 1 : size, :]
    for p in range(1, plan.P):
        total = total + ref[size * p + size - 1 : size * p + size, :]
    return total


def banded(taps, n, odd):
    row = lax.broadcasted_iota(jnp.int32, (n, n), 0)
    col = lax.broadcasted_iota(jnp.int32, (n, n), 1)
    gap = row - col
    total = jnp.zeros((n, n), jnp.float32)
    for d, tap in enumerate(taps):
        if odd:
            if d:
                total = jnp.where(gap == d, d * tap, total)
                total = jnp.where(gap == -d, -(d * tap), total)
        else:
            total = jnp.where(jnp.abs(gap) == d, tap, total)
    return total


def halves(value):
    high = value.astype(jnp.bfloat16)
    return high, (value - high.astype(jnp.float32)).astype(jnp.bfloat16)


def quad(matrix):
    high, low = halves(matrix)
    row = jnp.concatenate([high, low], axis=1)
    return jnp.concatenate([row, row], axis=0)


def lanes_times(value, quad_ref):
    high, low = halves(value)
    both = jnp.concatenate([high, low], axis=1)
    out = jnp.dot(both, quad_ref[...], preferred_element_type=jnp.float32)
    return out[:, :LANES] + out[:, LANES:]


def even_sum(load, taps, mid):
    total = taps[0] * load(mid)
    for d in range(1, len(taps)):
        total = total + taps[d] * (load(mid - d) + load(mid + d))
    return total


def unit_sum(load, taps, mid):
    total = load(mid)
    for d in range(1, len(taps)):
        total = total + taps[d] * (load(mid - d) + load(mid + d))
    return total


def odd_sum(load, taps, mid):
    total = taps[1] * (load(mid + 1) - load(mid - 1))
    for d in range(2, len(taps)):
        total = total + (d * taps[d]) * (load(mid + d) - load(mid - d))
    return total


MANY = 8


def run_passes(plan, passes):
    chunks = range(0, plan.X, MANY)
    for base in chunks:
        passes[0][0](base)
    for (_, matmul_part, emit_part), after in zip(passes, passes[1:] + [None]):
        done = None

        def close(pair):
            emit_part(*pair)
            if after is not None:
                after[0](pair[0])

        for base in chunks:
            out = matmul_part(base)
            if done is not None:
                close(done)
            done = (base, out)
        close(done)


def kernel_pass(plan, taps, quad_ref, in_ref, zb_ref, rows, emit):
    R = plan.R

    def z_part(base):
        for x in range(base, base + MANY):
            zb_ref[R + x, :rows, :] = unit_sum(lambda j: in_ref[x, j : j + rows, :], taps, R)

    def matmul_part(base):
        parts = [
            unit_sum(lambda j: zb_ref[base + q + j, :rows, :], taps, R) for q in range(MANY)
        ]
        return lanes_times(jnp.concatenate(parts, axis=0), quad_ref)

    def emit_part(base, out):
        for q in range(MANY):
            emit(base + q, out[q * rows : (q + 1) * rows])

    return z_part, matmul_part, emit_part


def inside(plan, at, off, rows):
    z = lax.broadcasted_iota(jnp.int32, (rows, LANES), 0) + (at * plan.S - plan.H + off)
    return (z >= 0) & (z < plan.Z)


def scale_step(plan, at, taps, quad_ref, zb, src, top, dst, over, off, start, rows):
    mask = inside(plan, at, off + start, rows)
    src = src.at[:, pl.ds(top, rows + 2 * plan.R), :]
    lead = (off + 7) // 8 * 8
    over = over.at[:, pl.ds(start, rows + lead), :]

    def emit(x, value):
        dst[x, pl.ds(start, rows), :] = jnp.where(mask, over[x, off : off + rows, :] / value, 0.0)

    return kernel_pass(plan, taps, quad_ref, src, zb, rows, emit)


def clear_edges(ref, edge, size):
    blank = jnp.zeros((edge,) + ref.shape[1:], jnp.float32)
    ref[:edge] = blank
    ref[edge + size :] = blank


def prep_kernel(plan, k_ref, s_ref, own, taps_ref, quad_ref, slope_ref, smooth_ref, high_ref, low_ref):
    del own
    R, Q = plan.R, plan.Q
    taps = [jnp.zeros((1, LANES), jnp.float32) + k_ref[d] for d in range(R + 1)]
    taps = [jnp.ones((1, LANES), jnp.float32)] + [tap / taps[0] for tap in taps[1:]]
    stap = smooth_taps(s_ref, Q)
    for d in range(R + 1):
        taps_ref[d] = jnp.broadcast_to(taps[d], (8, LANES))
    for d in range(Q + 1):
        taps_ref[R + 1 + d] = jnp.broadcast_to(stap[d], (8, LANES))
    quad_ref[...] = quad(banded(taps, LANES, False))
    slope_ref[...] = quad(banded(taps, LANES, True))
    smooth_ref[...] = quad(banded(stap, LANES, False))
    wide = [jnp.concatenate([t] * (plan.Z // LANES), axis=1) for t in stap]
    high_ref[...], low_ref[...] = halves(banded(wide, plan.Z, False))


def kernel_taps(plan, taps_ref):
    return [taps_ref[d, :1, :] for d in range(plan.R + 1)]


def gaps_of(plan, tot, tw, olds, news):
    S = plan.S
    first_half = lane_at() < LANES // 2
    both = tot[:1, :]
    sum_s = jnp.sum(jnp.where(first_half, both, 0.0), axis=1, keepdims=True)
    sum_t = jnp.sum(jnp.where(first_half, 0.0, both), axis=1, keepdims=True)
    scale_s = plan.cells / jnp.broadcast_to(sum_s, (1, LANES))
    scale_t = plan.cells / jnp.broadcast_to(sum_t, (1, LANES))

    def mid(ref, x):
        edge = (ref.shape[1] - S) // 2
        return ref[x, edge : edge + S, :]

    def p_step(x, carry):
        t = mid(tw, x)
        want = scale_t * t
        have = scale_s * t
        result = []
        for part, old, new in zip(carry, olds, news):
            value = have / mid(new, x)
            if old is not None:
                value = value * mid(old, x)
            gap = jnp.abs(value - want)
            for r in range(0, S, 8):
                part = part + gap[r : r + 8]
            result.append(part)
        return tuple(result)

    zero = jnp.zeros((8, LANES), jnp.float32)
    gaps = lax.fori_loop(0, plan.X, p_step, (zero,) * len(news), unroll=4)
    return [jnp.sum(g, keepdims=True) for g in gaps]


def in_lanes(values, first=0):
    row = jnp.zeros((1, LANES), jnp.float32)
    for t, value in enumerate(values):
        row = jnp.where(lane_at() == first + t, value, row)
    return row


def gaps_kernel(plan, tot, tw, v1, v2, v3, v4, out_ref):
    out_ref[...] = in_lanes(gaps_of(plan, tot, tw, (None, v1, v2, v3), (v1, v2, v3, v4)))


def spread_halves(plan, at, own, even, odd, own2, even2, odd2, win):
    S, H, gs = plan.S, plan.H, plan.gs
    c = lax.axis_index("gz")

    def spread(low, high):
        for k, (mid, core) in enumerate(((own, c), (own2, 1 - c))):
            for i in range(plan.nx):
                x, here = plan.bx * i + gs * core, pl.ds(i * gs, gs)
                win[pl.ds(x, gs), H : H + S, :] = mid[here]
                win[pl.ds(x, gs), :H, :] = low[k][here]
                win[pl.ds(x, gs), H + S :, :] = high[k][here]

    pl.when(at % 2 == 0)(lambda: spread((odd, odd2), (even, even2)))
    pl.when(at % 2 == 1)(lambda: spread((even, even2), (odd, odd2)))


def open_kernel(plan, taps_ref, quad_ref, own, even, odd, own2, even2, odd2, sw, ku, u, zb):
    R, S, H, X = plan.R, plan.S, plan.H, plan.X
    at = place_of(plan)
    taps = kernel_taps(plan, taps_ref)
    clear_edges(zb, R, X)
    spread_halves(plan, at, own, even, odd, own2, even2, odd2, sw)

    def reach_sum(place, size):
        total = jnp.ones(place.shape, jnp.float32)
        for d in range(1, R + 1):
            total = total + jnp.where(place - d >= 0, taps[d], 0.0)
            total = total + jnp.where(place + d < size, taps[d], 0.0)
        return total

    rows = S + 2 * H
    mask = inside(plan, at, 0, rows)
    y_at = lax.broadcasted_iota(jnp.int32, (rows, LANES), 1)
    z_at = lax.broadcasted_iota(jnp.int32, (rows, LANES), 0) + (at * S - H)
    plane = reach_sum(z_at, plan.Z) * (reach_sum(y_at, plan.Y) * taps_ref[0, :1, :])

    def u_step(x, carry):
        cx = reach_sum(jnp.zeros((1, LANES), jnp.int32) + x, X)
        u[x] = jnp.where(mask, sw[x] / (plane * cx), 0.0)
        return carry

    lax.fori_loop(0, X, u_step, 0, unroll=2)

    def emit(x, value):
        ku[x] = value

    run_passes(plan, [kernel_pass(plan, taps, quad_ref, u, zb, rows - 2 * R, emit)])


def first_kernel(plan, taps_ref, quad_ref, own, even, odd, own2, even2, odd2, sw, ku,
                 tw, v, v2, u_out, tot, u, zb, zc):
    R, S, H, X, XH = plan.R, plan.S, plan.H, plan.X, plan.XH
    at = place_of(plan)
    taps = kernel_taps(plan, taps_ref)
    clear_edges(zb, R, X)
    clear_edges(zc, R, X)
    spread_halves(plan, at, own, even, odd, own2, even2, odd2, tw)
    tot[...] = own[XH, :1, :] + own2[XH, :1, :]
    rows = S + 2 * H - 2 * R
    mask = inside(plan, at, R, rows)

    def v_step(x, carry):
        v[x] = jnp.where(mask, tw[x, R : R + rows, :] / ku[x], 0.0)
        return carry

    lax.fori_loop(0, X, v_step, 0, unroll=4)
    step = functools.partial(scale_step, plan, at, taps, quad_ref)
    run_passes(plan, [
        step(zb, v, 0, u, sw, 2 * R, 0, rows - 2 * R),
        step(zc, u, 0, v2, tw, 3 * R, 0, rows - 4 * R),
        step(zb, v2, 0, u_out, sw, 4 * R, 0, rows - 6 * R),
    ])


def early_kernel(plan, taps_ref, quad_ref, mine, side, sw, tw, v, u, v2, win, zb, zc):
    R, S, H = plan.R, plan.S, plan.H
    c = lax.axis_index("gz")
    at = place_of(plan)
    taps = kernel_taps(plan, taps_ref)
    clear_edges(zb, R, plan.X)
    clear_edges(zc, R, plan.X)
    real = jnp.where(jnp.where(c == 0, at > 0, at < plan.P - 1), 1.0, 0.0)
    win[:, pl.ds(pl.multiple_of(H * c, 8), H), :] = side[...] * real
    win[:, pl.ds(pl.multiple_of(H * (1 - c), 8), S), :] = mine[...]
    step = functools.partial(scale_step, plan, at, taps, quad_ref)
    from_ = pl.multiple_of(S * c, 8)
    run_passes(plan, [
        step(zb, win, 0, v, tw, R, from_, S + H - 2 * R),
        step(zc, v, from_, u, sw, 2 * R, from_, S + H - 4 * R),
        step(zb, u, from_, v2, tw, 3 * R, from_, S + H - 6 * R),
    ])


def late_rows(plan, at, taps, quad_ref, mine, other, sw, tw, v, u, v2, win, zb, zc):
    R, S, H = plan.R, plan.S, plan.H
    c = lax.axis_index("gz")
    real = jnp.where(jnp.where(c == 1, at > 0, at < plan.P - 1), 1.0, 0.0)
    half = S // 2

    def lay(other_at, mine_at, mine_from):
        win[:, other_at : other_at + H, :] = other[...] * real
        win[:, mine_at : mine_at + half, :] = mine[:, mine_from : mine_from + half, :]

    pl.when(c == 0)(lambda: lay(half, 0, half))
    pl.when(c == 1)(lambda: lay(0, H, 0))
    step = functools.partial(scale_step, plan, at, taps, quad_ref)
    first = pl.multiple_of((S + H - 2 * R) * (1 - c), 8)
    second = pl.multiple_of((S + H - 4 * R) * (1 - c), 8)
    third = pl.multiple_of((S + H - 6 * R) * (1 - c), 8)
    return [
        step(zb, win, 0, v, tw, R, first, S),
        step(zc, v, second, u, sw, 2 * R, second, S),
        step(zb, u, third, v2, tw, 3 * R, third, S),
    ]


def late_kernel(plan, taps_ref, quad_ref, mine, other, sw, tw, v_in, u_in, v2_in,
                v, u, v2, u_out, win, zb, zc):
    del v_in, u_in, v2_in
    R, S = plan.R, plan.S
    at = place_of(plan)
    taps = kernel_taps(plan, taps_ref)
    clear_edges(zb, R, plan.X)
    clear_edges(zc, R, plan.X)
    passes = late_rows(plan, at, taps, quad_ref, mine, other, sw, tw, v, u, v2, win, zb, zc)
    passes.append(scale_step(plan, at, taps, quad_ref, zc, v2, 0, u_out, sw, 4 * R, 0, S))
    run_passes(plan, passes)


def smooth_taps(s_ref, reach):
    total = s_ref[0]
    tail = s_ref[1]
    for d in range(2, reach + 1):
        tail = tail + s_ref[d]
    scale = 1.0 / (jnp.zeros((1, LANES), jnp.float32) + (total + 2.0 * tail))
    return [scale * s_ref[d] for d in range(reach + 1)]


def last_kernel(plan, taps_ref, quad_ref, slope_ref, smooth_ref, mine, other, sw, tw, prev,
                gaps, tot, v_in, u_in, v2_in, v, u, v2, out_ref, win, zb, zc, zg, raw):
    del v_in, u_in, v2_in
    R, S, X, gs, Q = plan.R, plan.S, plan.X, plan.gs, plan.Q
    size = 3 * S + 1
    c = lax.axis_index("gz")
    at = place_of(plan)
    taps = kernel_taps(plan, taps_ref)
    stap = [taps_ref[R + 1 + d, :1, :] for d in range(Q + 1)]
    clear_edges(zb, R, X)
    clear_edges(zc, R, X)
    clear_edges(zg, R, X)
    for comp in range(3):
        clear_edges(raw.at[comp], Q, X)
    passes = late_rows(plan, at, taps, quad_ref, mine, other, sw, tw, v, u, v2, win, zb, zc)

    def z_part(base):
        for x in range(base, base + MANY):
            load = lambda j: v2[x, j : j + S, :]
            zc[R + x, :S, :] = unit_sum(load, taps, R)
            zg[R + x, :S, :] = odd_sum(load, taps, R)

    def matmul_part(base):
        kk, gk, kg = [], [], []
        for q in range(MANY):
            flat = lambda j: zc[base + q + j, :S, :]
            kk.append(unit_sum(flat, taps, R))
            gk.append(odd_sum(flat, taps, R))
            kg.append(unit_sum(lambda j: zg[base + q + j, :S, :], taps, R))
        kk, gk, kg = (jnp.concatenate(part, axis=0) for part in (kk, gk, kg))
        nums = lanes_times(gk, quad_ref), lanes_times(kk, slope_ref), lanes_times(kg, quad_ref)
        return lanes_times(kk, quad_ref), nums

    def emit_part(base, out):
        kvol, nums = out
        for comp, num in enumerate(nums):
            value = num / kvol
            for q in range(MANY):
                raw[comp, Q + base + q] = value[q * S : (q + 1) * S]

    run_passes(plan, passes + [(z_part, matmul_part, emit_part)])

    for i in range(plan.nx):
        x = plan.bx * i + gs * c
        for comp in range(3):
            parts = []
            for xx in range(gs):
                parts.append(even_sum(lambda j: raw[comp, x + xx + j], stap, Q))
            flat = lanes_times(jnp.concatenate(parts, axis=0), smooth_ref)
            turned = turn_groups(plan, [flat[xx * S : (xx + 1) * S] for xx in range(gs)])
            for j in range(plan.ny):
                base = size * (i * plan.ny + j) + comp * S
                out_ref[base : base + S, :] = turned[j]

    rows = gaps_of(plan, tot, tw, (prev, v), (v, v2))
    stat = gaps[...] + in_lanes(rows, ITERS - 2)
    for p in range(plan.P):
        out_ref[size * p + 3 * S : size * (p + 1), :] = stat


def smooth_z(plan, core, high_ref, low_ref, in_ref, data, emit):
    S = plan.S
    size = 3 * S + 1
    for place in range(plan.P):
        for comp in range(3):
            base = size * plan.chip(place) + comp * S
            data[S * place : S * place + S, comp * LANES : (comp + 1) * LANES] = in_ref[
                base : base + S, :
            ]
    rows = pl.ds(pl.multiple_of(core * LANES, LANES), LANES)
    m_high, m_low = high_ref[rows, :], low_ref[rows, :]
    d_high, d_low = halves(data[...])
    dot = functools.partial(jnp.dot, preferred_element_type=jnp.float32)
    out = dot(m_high, d_high) + (dot(m_high, d_low) + dot(m_low, d_high))
    for comp in range(3):
        emit(comp, out[:, comp * LANES : (comp + 1) * LANES].T)


def away_kernel(plan, high_ref, low_ref, in_ref, send_ref, data):
    def emit(comp, value):
        send_ref[comp] = value

    smooth_z(plan, 1 - lax.axis_index("gz"), high_ref, low_ref, in_ref, data, emit)


def home_kernel(plan, high_ref, low_ref, in_ref, mis_ref, out_hbm, data, keep, sem):
    c = lax.axis_index("gz")
    gs = plan.gs

    def emit(comp, value):
        keep[comp] = value.reshape(gs, plan.by, LANES)

    smooth_z(plan, c, high_ref, low_ref, in_ref, data, emit)
    copy = pltpu.make_async_copy(keep, out_hbm.at[:, pl.ds(gs * c, gs)], sem)
    copy.start()
    gone = sum_rows(plan, in_ref, 3 * plan.S + 1) / plan.cells
    for t in range(ITERS):
        mis_ref[t] = jnp.sum(jnp.where(lane_at() == t, gone, 0.0))
    copy.wait()


def place_kernel(plan, recv_ref, in_hbm, out_hbm, sem):
    del in_hbm
    c = lax.axis_index("gz")
    copy = pltpu.make_async_copy(recv_ref, out_hbm.at[:, pl.ds(plan.gs * (1 - c), plan.gs)], sem)
    copy.start()
    copy.wait()


def slab_shards(plan, source, target, kernel_half, smooth_half):
    R, S, H, X, XH, Pn, Z = plan.R, plan.S, plan.H, plan.X, plan.XH, plan.P, plan.Z
    bind = lambda kernel: functools.partial(kernel, plan)
    half = f32(2, LANES, LANES)
    vm = lambda *shape: pltpu.VMEM(shape, jnp.float32)
    keep, stat = call(
        bind(pack_kernel), [half, f32(1, LANES)], 0, 0,
        [vm(*source.shape), vm(*source.shape), pltpu.SemaphoreType.DMA((2,))], n_any=2,
    )(*(pltpu.with_memory_space_constraint(a, pltpu.HBM) for a in (source, target)))
    (chunks,) = call(
        bind(chunk_kernel), [f32(Pn * (2 * S + 1), LANES)], 0, 4, [vm(*half.shape)]
    )(keep, swap_cores(plan, source), swap_cores(plan, target), stat)
    spread = trade_chunks(chunks)
    own_s, own_t = call(
        bind(unpack_kernel), [f32(XH, S, LANES), f32(XH + 1, S, LANES)], 0, 1
    )(spread)
    square = jax.ShapeDtypeStruct((2 * LANES, 2 * LANES), jnp.bfloat16)
    table = jax.ShapeDtypeStruct((Z, Z), jnp.bfloat16)
    taps, quad_k, quad_g, quad_s, high, low = call(
        bind(prep_kernel), [f32(plan.R + plan.Q + 2, 8, LANES), square, square, square, table, table],
        2, 0, n_any=1,
    )(kernel_half, smooth_half, own_s)
    even_s, odd_s = swap_even(plan, own_s), swap_odd(plan, own_s)
    even_t, odd_t = swap_even(plan, own_t), swap_odd(plan, own_t)
    own2_s, own2_t = swap_cores(plan, own_s), swap_cores(plan, own_t)
    even_s, odd_s, taps = lax.optimization_barrier((even_s, odd_s, taps))
    halos_s = swap_cores(plan, even_s), swap_cores(plan, odd_s)
    even_t, odd_t, own2_s = lax.optimization_barrier((even_t, odd_t, own2_s))
    halos_t = swap_cores(plan, even_t), swap_cores(plan, odd_t)

    slab = f32(X, S, LANES)
    width = S + 2 * H
    wide, v_shape, u_shape, v2_shape = (f32(X, width - 2 * k * R, LANES) for k in (0, 1, 2, 3))
    zb = vm(X + 2 * R, width - 2 * R, LANES)
    sw, ku = call(
        bind(open_kernel), [wide, v_shape], 0, 8, [vm(*wide.shape), zb]
    )(taps, quad_k, own_s, even_s, odd_s, own2_s, *halos_s)
    tw, v1, v2, u, tot = call(
        bind(first_kernel), [wide, v_shape, v2_shape, slab, f32(1, LANES)], 0, 10,
        [vm(*u_shape.shape), zb, zb],
    )(taps, quad_k, own_t, even_t, odd_t, own2_t, *halos_t, sw, ku)

    def early(u, side):
        return call(
            bind(early_kernel), [v_shape, u_shape, v2_shape], 0, 6,
            [vm(X, S + H, LANES), zb, zb],
        )(taps, quad_k, u, side, sw, tw)

    rest = vm(X, H + S // 2, LANES)
    side = swap_sides(plan, u)
    other = swap_cores(plan, side)
    v3, u4, v4 = early(u, side)
    v3, _, v4, u = call(
        bind(late_kernel), [v_shape, u_shape, v2_shape, slab], 0, 9, [rest, zb, zb],
        aliases={6: 0, 7: 1, 8: 2},
    )(taps, quad_k, u, other, sw, tw, v3, u4, v4)
    side = swap_sides(plan, u)
    (gaps,) = call(bind(gaps_kernel), [f32(1, LANES)], 0, 6)(tot, tw, v1, v2, v3, v4)
    side, gaps = lax.optimization_barrier((side, gaps))
    other = swap_cores(plan, side)
    v5, u6, v6 = early(u, side)
    *_, chunks = call(
        bind(last_kernel), [v_shape, u_shape, v2_shape, f32(Pn * (3 * S + 1), LANES)], 0, 14,
        [rest, zb, zb, vm(X + 2 * R, S, LANES), vm(3, X + 2 * plan.Q, S, LANES)],
        aliases={11: 0, 12: 1, 13: 2},
    )(taps, quad_k, quad_g, quad_s, u, other, sw, tw, v4, gaps, tot, v5, u6, v6)
    spread = trade_chunks(chunks)
    data = vm(Z, 3 * LANES)
    (send,) = call(bind(away_kernel), [f32(3, LANES, LANES)], 0, 3, [data])(high, low, spread)
    half = (3, plan.gs, plan.by, LANES)
    recv = swap_cores(plan, send.reshape(half))
    whole = f32(3, plan.bx, plan.by, LANES)
    mismatch, displacement = call(
        bind(home_kernel), [f32(ITERS), whole], 0, 3, [data, vm(*half), pltpu.SemaphoreType.DMA(())],
        smem_out=1, any_out=1,
    )(high, low, spread)
    (displacement,) = call(
        bind(place_kernel), [whole], 0, 1, [pltpu.SemaphoreType.DMA(())], n_any=1, any_out=1,
        aliases={1: 0},
    )(recv, displacement)
    return displacement, mismatch


def shards(sizes, source, target, kernel_half, smooth_half):
    plan = Plan(sizes, *source.shape, kernel_half.shape[0] - 1, smooth_half.shape[0] - 1)
    if plan.fits():
        return slab_shards(plan, source, target, kernel_half, smooth_half)
    return block_shards(source, target, kernel_half, smooth_half)


def solution(mesh):
    in_specs = (P("gx", "gy", "gz"), P("gx", "gy", "gz"), P(), P())
    out_specs = (P(None, "gx", "gy", "gz"), P())
    body = functools.partial(shards, dict(mesh.shape))
    return jax.shard_map(body, mesh=mesh, in_specs=in_specs, out_specs=out_specs, check_vma=False)
```

```python
import functools

import jax
import jax.numpy as jnp
from jax import lax
from jax.experimental import pallas as pl
from jax.experimental.pallas import tpu as pltpu
from jax.sharding import PartitionSpec as P


ITERS = 6
LANES = 128
AXES = ("gx", "gy", "gz")


def padded_2(block, sides, width):
    for axis, dim in sides:
        count = lax.axis_size(axis)
        forward = [(i, i + 1) for i in range(count - 1)]
        backward = [(target, source) for source, target in forward]
        low = lax.ppermute(
            lax.slice_in_dim(block, block.shape[dim] - width, None, axis=dim), axis, forward
        )
        high = lax.ppermute(lax.slice_in_dim(block, 0, width, axis=dim), axis, backward)
        block = jnp.concatenate([low, block, high], axis=dim)
    return block


def full_taps(half):
    return jnp.concatenate([half[:0:-1], half])


def along(padded, taps, axis, count):
    width = taps.shape[0]
    total = taps[0] * lax.slice_in_dim(padded, 0, count, axis=axis)
    for j in range(1, width):
        total = total + taps[j] * lax.slice_in_dim(padded, j, j + count, axis=axis)
    return total


def three_passes(padded, taps, size_x, size_y, size_z):
    padded = along(padded, taps, 0, size_x)
    padded = along(padded, taps, 1, size_y)
    return along(padded, taps, 2, size_z)


def block_shards(source, target, kernel_half, smooth_half):
    kern = full_taps(kernel_half)
    radius = kernel_half.shape[0] - 1
    reach = smooth_half.shape[0] - 1
    offsets = jnp.arange(-radius, radius + 1).astype(jnp.float32)
    slope = offsets * kern
    norm_total = smooth_half[0] + 2.0 * jnp.sum(smooth_half[1:])
    smooth = full_taps(smooth_half) / norm_total
    size_x, size_y, size_z = source.shape
    cells = float(source.size * lax.axis_size("gx") * lax.axis_size("gy") * lax.axis_size("gz"))
    totals = lax.psum((jnp.sum(source), jnp.sum(target)), AXES)
    first = source * (cells / totals[0])
    second = target * (cells / totals[1])
    first_wide = padded_2(first, (("gx", 0), ("gy", 1), ("gz", 2)), radius)
    scaling_v = jnp.ones_like(source)
    errors = []
    for _ in range(ITERS):
        padded = padded_2(scaling_v, (("gx", 0), ("gy", 1), ("gz", 2)), 2 * radius)
        kv_wide = three_passes(
            padded, kern, size_x + 2 * radius, size_y + 2 * radius, size_z + 2 * radius
        )
        u_wide = first_wide / kv_wide
        ku = three_passes(u_wide, kern, size_x, size_y, size_z)
        local_err = jnp.sum(jnp.abs(scaling_v * ku - second))
        errors.append(lax.psum(local_err, AXES) / cells)
        scaling_v = second / ku
    mismatch = jnp.stack(errors)
    padded = padded_2(scaling_v, (("gx", 0), ("gy", 1), ("gz", 2)), radius)
    pass_k = along(padded, kern, 0, size_x)
    pass_g = along(padded, slope, 0, size_x)
    kk = along(pass_k, kern, 1, size_y)
    kg = along(pass_k, slope, 1, size_y)
    gk = along(pass_g, kern, 1, size_y)
    kvol = along(kk, kern, 2, size_z)
    znum = along(kk, slope, 2, size_z)
    ynum = along(kg, kern, 2, size_z)
    xnum = along(gk, kern, 2, size_z)
    raw = jnp.stack([xnum, ynum, znum]) / kvol
    padded = padded_2(raw, (("gx", 1), ("gy", 2), ("gz", 3)), reach)
    padded = along(padded, smooth, 1, size_x)
    padded = along(padded, smooth, 2, size_y)
    displacement = along(padded, smooth, 3, size_z)
    return (displacement, mismatch)


class Plan:
    def __init__(self, mesh, bx, by, bz, radius, reach):
        self.nx, self.ny, self.nc = mesh["gx"], mesh["gy"], mesh["gz"]
        self.bx, self.by, self.bz = bx, by, bz
        self.R, self.Q = radius, reach
        self.P = self.nx * self.ny
        self.X, self.Y, self.Z = bx * self.nx, by * self.ny, bz * self.nc
        self.S = self.Z // self.P
        self.H = 4 * radius
        self.gs = LANES // by if by <= LANES else 0
        self.XH = self.X // 2
        self.cells = float(self.X * self.Y * self.Z)

    def fits(self):
        return (
            self.nc == 2
            and self.ny >= 2
            and self.ny & (self.ny - 1) == 0
            and self.nx >= 2
            and self.bz == LANES
            and self.Y == LANES
            and self.gs == self.ny
            and self.bx == 2 * self.gs
            and self.Z == self.P * self.S
            and self.S == self.H
            and self.S % 16 == 0
            and self.R % 4 == 0
            and ITERS == 6
        )

    def spot(self, at):
        at %= self.P
        col, q = divmod(at, self.nx)
        return (q if col % 2 == 0 else self.nx - 1 - q), col ^ (col >> 1)

    def chip(self, at):
        i, j = self.spot(at)
        return i * self.ny + j

    def device(self, at, core):
        return self.chip(at) * self.nc + core


def swap_cores(plan, value):
    pairs = [(plan.device(at, c), plan.device(at, 1 - c)) for at in range(plan.P) for c in range(2)]
    return lax.ppermute(value, AXES, pairs)


def swap_even(plan, value):
    pairs = [(plan.device(at, c), plan.device(at ^ 1, c)) for at in range(plan.P) for c in range(2)]
    return lax.ppermute(value, AXES, pairs)


def swap_odd(plan, value):
    pairs = [
        (plan.device(at, c), plan.device(((at + 1) ^ 1) - 1, c))
        for at in range(plan.P)
        for c in range(2)
    ]
    return lax.ppermute(value, AXES, pairs)


def swap_sides(plan, value):
    pairs = [(plan.device(at, 0), plan.device(at - 1, 1)) for at in range(plan.P)]
    pairs += [(plan.device(at, 1), plan.device(at + 1, 0)) for at in range(plan.P)]
    return lax.ppermute(value, AXES, pairs)


def trade_chunks(value, axes):
    rows, lanes = value.shape
    out = lax.all_to_all(value.reshape(rows, 1, lanes), axes, 0, 0, tiled=True)
    return out.reshape(rows, lanes)


def place_of(plan):
    i, j = lax.axis_index("gx"), lax.axis_index("gy")
    at = jnp.int32(0)
    for place in range(plan.P):
        a, b = plan.spot(place)
        at = at + jnp.where((i == a) & (j == b), place, 0)
    return at.astype(jnp.int32)


def call(kernel, out_shape, n_smem, n_vmem, scratch=(), smem_out=0, n_any=0, any_out=0, aliases=None):
    vm, sm = pl.BlockSpec(memory_space=pltpu.VMEM), pl.BlockSpec(memory_space=pltpu.SMEM)
    hbm = pl.BlockSpec(memory_space=pltpu.HBM)
    out_specs = [vm] * (len(out_shape) - smem_out - any_out) + [sm] * smem_out + [hbm] * any_out
    return pl.pallas_call(
        kernel,
        out_shape=out_shape,
        in_specs=[sm] * n_smem + [vm] * n_vmem + [hbm] * n_any,
        out_specs=out_specs,
        scratch_shapes=list(scratch),
        input_output_aliases=aliases or {},
        compiler_params=pltpu.CompilerParams(vmem_limit_bytes=48 << 20),
    )


def f32(*shape):
    return jax.ShapeDtypeStruct(shape, jnp.float32)


def turn_groups(plan, parts):
    n, w = plan.gs, plan.by
    group = lax.broadcasted_iota(jnp.int32, parts[0].shape, 1) // w
    outs = []
    for a in range(n):
        total = parts[a]
        for b in range(n):
            if b != a:
                moved = pltpu.roll(parts[b], (w * (b - a)) % LANES, 1)
                total = jnp.where(group == b, moved, total)
        outs.append(total)
    return outs


def pack_kernel(plan, src_hbm, tgt_hbm, keep_ref, stat_ref, src_ref, tgt_ref, sems):
    c = lax.axis_index("gz")
    copies = [
        pltpu.make_async_copy(src_hbm, src_ref, sems.at[0]),
        pltpu.make_async_copy(tgt_hbm, tgt_ref, sems.at[1]),
    ]
    for copy in copies:
        copy.start()
    sums = []
    for st, ref in enumerate((src_ref, tgt_ref)):
        copies[st].wait()
        keep_ref[st] = ref[pl.ds(plan.gs * c, plan.gs)].reshape(LANES, LANES).T
        row = jnp.sum(ref[...].reshape(plan.bx * plan.by, LANES), axis=0, keepdims=True)
        sums.append(row + pltpu.roll(row, LANES // 2, 1))
    stat_ref[...] = jnp.where(lane_at() < LANES // 2, *sums)


def lane_at():
    return lax.broadcasted_iota(jnp.int32, (1, LANES), 1)


def chunk_kernel(plan, keep_ref, src_ref, tgt_ref, stat_ref, out_ref, recv_ref):
    c = lax.axis_index("gz")
    half, S = plan.P // 2, plan.S
    size = 2 * S + 1
    for st, ref in enumerate((src_ref, tgt_ref)):
        recv_ref[st] = ref[pl.ds(plan.gs * c, plan.gs)].reshape(LANES, LANES).T

    def write(low_ref, high_ref):
        stat = stat_ref[...]
        for place in range(plan.P):
            ref, part = (low_ref, place) if place < half else (high_ref, place - half)
            base = size * plan.chip(place)
            for st in range(2):
                out_ref[base + S * st : base + S * st + S, :] = ref[st, S * part : S * part + S, :]
            out_ref[base + 2 * S : base + size, :] = stat

    pl.when(c == 0)(lambda: write(keep_ref, recv_ref))
    pl.when(c == 1)(lambda: write(recv_ref, keep_ref))


def unpack_kernel(plan, in_ref, s_ref, t_ref):
    S, gs, XH = plan.S, plan.gs, plan.XH
    size = 2 * S + 1
    for st, out_ref in enumerate((s_ref, t_ref)):
        for i in range(plan.nx):
            bases = [size * (i * plan.ny + j) + S * st for j in range(plan.ny)]
            parts = [in_ref[base : base + S, :] for base in bases]
            for xx, value in enumerate(turn_groups(plan, parts)):
                out_ref[i * gs + xx] = value
    t_ref[XH] = jnp.zeros((S, LANES), jnp.float32)
    t_ref[XH, :1, :] = sum_rows(in_ref, size)


def sum_rows(ref, size):
    total = ref[size - 1 : size, :]
    for p in range(1, ref.shape[0] // size):
        total = total + ref[size * p + size - 1 : size * p + size, :]
    return total


def banded(taps, n, odd):
    row = lax.broadcasted_iota(jnp.int32, (n, n), 0)
    col = lax.broadcasted_iota(jnp.int32, (n, n), 1)
    gap = row - col
    total = jnp.zeros((n, n), jnp.float32)
    for d, tap in enumerate(taps):
        if odd:
            if d:
                total = jnp.where(gap == d, d * tap, total)
                total = jnp.where(gap == -d, -(d * tap), total)
        else:
            total = jnp.where(jnp.abs(gap) == d, tap, total)
    return total


def halves(value):
    high = value.astype(jnp.bfloat16)
    return high, (value - high.astype(jnp.float32)).astype(jnp.bfloat16)


def quad(matrix):
    high, low = halves(matrix)
    row = jnp.concatenate([high, low], axis=1)
    return jnp.concatenate([row, row], axis=0)


def lanes_times(value, quad_ref):
    high, low = halves(value)
    both = jnp.concatenate([high, low], axis=1)
    out = jnp.dot(both, quad_ref[...], preferred_element_type=jnp.float32)
    return out[:, :LANES] + out[:, LANES:]


def even_sum(load, taps, mid):
    total = taps[0] * load(mid)
    for d in range(1, len(taps)):
        total = total + taps[d] * (load(mid - d) + load(mid + d))
    return total


def unit_sum(load, taps, mid):
    total = load(mid)
    for d in range(1, len(taps)):
        total = total + taps[d] * (load(mid - d) + load(mid + d))
    return total


def odd_sum(load, taps, mid):
    total = taps[1] * (load(mid + 1) - load(mid - 1))
    for d in range(2, len(taps)):
        total = total + (d * taps[d]) * (load(mid + d) - load(mid - d))
    return total


MANY = 16


def run_passes(plan, passes):
    chunks = range(0, plan.X, MANY)
    for base in chunks:
        passes[0][0](base)
    for (_, matmul_part, emit_part), after in zip(passes, passes[1:] + [None]):
        done = None

        def close(pair):
            emit_part(*pair)
            if after is not None:
                after[0](pair[0])

        for base in chunks:
            out = matmul_part(base)
            if done is not None:
                close(done)
            done = (base, out)
        close(done)


def kernel_pass(plan, taps, quad_ref, in_ref, zb_ref, rows, emit):
    R = plan.R

    def z_part(base):
        for x in range(base, base + MANY):
            zb_ref[R + x, :rows, :] = unit_sum(lambda j: in_ref[x, j : j + rows, :], taps, R)

    def matmul_part(base):
        parts = [
            unit_sum(lambda j: zb_ref[base + q + j, :rows, :], taps, R) for q in range(MANY)
        ]
        return lanes_times(jnp.concatenate(parts, axis=0), quad_ref)

    def emit_part(base, out):
        for q in range(MANY):
            emit(base + q, out[q * rows : (q + 1) * rows])

    return z_part, matmul_part, emit_part


def inside(plan, at, off, rows):
    z = lax.broadcasted_iota(jnp.int32, (rows, LANES), 0) + (at * plan.S - plan.H + off)
    return (z >= 0) & (z < plan.Z)


def scale_step(plan, at, taps, quad_ref, zb, src, top, dst, over, off, start, rows):
    mask = inside(plan, at, off + start, rows)
    src = src.at[:, pl.ds(top, rows + 2 * plan.R), :]
    lead = (off + 7) // 8 * 8
    over = over.at[:, pl.ds(start, rows + lead), :]

    def emit(x, value):
        dst[x, pl.ds(start, rows), :] = jnp.where(mask, over[x, off : off + rows, :] / value, 0.0)

    return kernel_pass(plan, taps, quad_ref, src, zb, rows, emit)


def clear_edges(ref, edge, size):
    blank = jnp.zeros((edge,) + ref.shape[1:], jnp.float32)
    ref[:edge] = blank
    ref[edge + size :] = blank


def prep_kernel(plan, k_ref, s_ref, own, taps_ref, quad_ref, slope_ref, smooth_ref, high_ref, low_ref):
    del own
    R, Q = plan.R, plan.Q
    taps = [jnp.zeros((1, LANES), jnp.float32) + k_ref[d] for d in range(R + 1)]
    taps = [jnp.ones((1, LANES), jnp.float32)] + [tap / taps[0] for tap in taps[1:]]
    stap = smooth_taps(s_ref, Q)
    for d in range(R + 1):
        taps_ref[d] = jnp.broadcast_to(taps[d], (8, LANES))
    for d in range(Q + 1):
        taps_ref[R + 1 + d] = jnp.broadcast_to(stap[d], (8, LANES))
    quad_ref[...] = quad(banded(taps, LANES, False))
    slope_ref[...] = quad(banded(taps, LANES, True))
    smooth_ref[...] = quad(banded(stap, LANES, False))
    wide = [jnp.concatenate([t] * (plan.Z // LANES), axis=1) for t in stap]
    high_ref[...], low_ref[...] = halves(banded(wide, plan.Z, False))


def kernel_taps(plan, taps_ref):
    return [taps_ref[d, :1, :] for d in range(plan.R + 1)]


def gaps_of(plan, tot, tw, olds, news):
    S = plan.S
    half = S // 2
    mine = pl.multiple_of(half * lax.axis_index("gz"), 8)
    first_half = lane_at() < LANES // 2
    both = tot[:1, :]
    sum_s = jnp.sum(jnp.where(first_half, both, 0.0), axis=1, keepdims=True)
    sum_t = jnp.sum(jnp.where(first_half, 0.0, both), axis=1, keepdims=True)
    scale_s = plan.cells / jnp.broadcast_to(sum_s, (1, LANES))
    scale_t = plan.cells / jnp.broadcast_to(sum_t, (1, LANES))

    def mid(ref):
        edge = (ref.shape[1] - S) // 2
        ref = ref.at[:, pl.ds(mine, ref.shape[1] - half), :]
        return lambda x: ref[x, edge : edge + half, :]

    t_at = mid(tw)
    olds = [old if old is None else mid(old) for old in olds]
    news = [mid(new) for new in news]

    def p_step(x, carry):
        t = t_at(x)
        want = scale_t * t
        have = scale_s * t
        result = []
        for part, old, new in zip(carry, olds, news):
            value = have / new(x)
            if old is not None:
                value = value * old(x)
            gap = jnp.abs(value - want)
            for r in range(0, half, 8):
                part = part + gap[r : r + 8]
            result.append(part)
        return tuple(result)

    zero = jnp.zeros((8, LANES), jnp.float32)
    gaps = lax.fori_loop(0, plan.X, p_step, (zero,) * len(news), unroll=4)
    return [jnp.sum(g, keepdims=True) for g in gaps]


def in_lanes(values, first=0):
    row = jnp.zeros((1, LANES), jnp.float32)
    for t, value in enumerate(values):
        row = jnp.where(lane_at() == first + t, value, row)
    return row


def gaps_kernel(plan, tot, tw, v1, v2, v3, v4, out_ref):
    out_ref[...] = in_lanes(gaps_of(plan, tot, tw, (None, v1, v2, v3), (v1, v2, v3, v4)))


def spread_halves(plan, at, own, even, odd, own2, even2, odd2, win):
    S, H, gs = plan.S, plan.H, plan.gs
    c = lax.axis_index("gz")

    def spread(low, high):
        for k, (mid, core) in enumerate(((own, c), (own2, 1 - c))):
            for i in range(plan.nx):
                x, here = plan.bx * i + gs * core, pl.ds(i * gs, gs)
                win[pl.ds(x, gs), H : H + S, :] = mid[here]
                win[pl.ds(x, gs), :H, :] = low[k][here]
                win[pl.ds(x, gs), H + S :, :] = high[k][here]

    pl.when(at % 2 == 0)(lambda: spread((odd, odd2), (even, even2)))
    pl.when(at % 2 == 1)(lambda: spread((even, even2), (odd, odd2)))


def open_kernel(plan, taps_ref, quad_ref, own, even, odd, own2, even2, odd2, sw, ku, u, zb):
    R, S, H, X = plan.R, plan.S, plan.H, plan.X
    at = place_of(plan)
    taps = kernel_taps(plan, taps_ref)
    clear_edges(zb, R, X)
    spread_halves(plan, at, own, even, odd, own2, even2, odd2, sw)

    def reach_sum(place, size):
        total = jnp.ones(place.shape, jnp.float32)
        for d in range(1, R + 1):
            total = total + jnp.where(place - d >= 0, taps[d], 0.0)
            total = total + jnp.where(place + d < size, taps[d], 0.0)
        return total

    rows = S + 2 * H
    mask = inside(plan, at, 0, rows)
    y_at = lax.broadcasted_iota(jnp.int32, (rows, LANES), 1)
    z_at = lax.broadcasted_iota(jnp.int32, (rows, LANES), 0) + (at * S - H)
    plane = reach_sum(z_at, plan.Z) * (reach_sum(y_at, plan.Y) * taps_ref[0, :1, :])

    def u_step(x, carry):
        cx = reach_sum(jnp.zeros((1, LANES), jnp.int32) + x, X)
        u[x] = jnp.where(mask, sw[x] / (plane * cx), 0.0)
        return carry

    lax.fori_loop(0, X, u_step, 0, unroll=2)

    def emit(x, value):
        ku[x] = value

    run_passes(plan, [kernel_pass(plan, taps, quad_ref, u, zb, rows - 2 * R, emit)])


def first_kernel(plan, taps_ref, quad_ref, own, even, odd, own2, even2, odd2, sw, ku,
                 tw, v, v2, u_out, tot, u, zb, zc):
    R, S, H, X, XH = plan.R, plan.S, plan.H, plan.X, plan.XH
    at = place_of(plan)
    taps = kernel_taps(plan, taps_ref)
    clear_edges(zb, R, X)
    clear_edges(zc, R, X)
    spread_halves(plan, at, own, even, odd, own2, even2, odd2, tw)
    tot[...] = own[XH, :1, :] + own2[XH, :1, :]
    rows = S + 2 * H - 2 * R
    mask = inside(plan, at, R, rows)

    def v_step(x, carry):
        v[x] = jnp.where(mask, tw[x, R : R + rows, :] / ku[x], 0.0)
        return carry

    lax.fori_loop(0, X, v_step, 0, unroll=4)
    step = functools.partial(scale_step, plan, at, taps, quad_ref)
    run_passes(plan, [
        step(zb, v, 0, u, sw, 2 * R, 0, rows - 2 * R),
        step(zc, u, 0, v2, tw, 3 * R, 0, rows - 4 * R),
        step(zb, v2, 0, u_out, sw, 4 * R, 0, rows - 6 * R),
    ])


def early_kernel(plan, taps_ref, quad_ref, mine, side, sw, tw, v, u, v2, win, zb, zc):
    R, S, H = plan.R, plan.S, plan.H
    c = lax.axis_index("gz")
    at = place_of(plan)
    taps = kernel_taps(plan, taps_ref)
    clear_edges(zb, R, plan.X)
    clear_edges(zc, R, plan.X)
    real = jnp.where(jnp.where(c == 0, at > 0, at < plan.P - 1), 1.0, 0.0)
    win[:, pl.ds(pl.multiple_of(H * c, 8), H), :] = side[...] * real
    win[:, pl.ds(pl.multiple_of(H * (1 - c), 8), S), :] = mine[...]
    step = functools.partial(scale_step, plan, at, taps, quad_ref)
    from_ = pl.multiple_of(S * c, 8)
    run_passes(plan, [
        step(zb, win, 0, v, tw, R, from_, S + H - 2 * R),
        step(zc, v, from_, u, sw, 2 * R, from_, S + H - 4 * R),
        step(zb, u, from_, v2, tw, 3 * R, from_, S + H - 6 * R),
    ])


def late_rows(plan, at, taps, quad_ref, mine, other, sw, tw, v, u, v2, win, zb, zc):
    R, S, H = plan.R, plan.S, plan.H
    c = lax.axis_index("gz")
    real = jnp.where(jnp.where(c == 1, at > 0, at < plan.P - 1), 1.0, 0.0)
    half = S // 2

    def lay(other_at, mine_at, mine_from):
        win[:, other_at : other_at + H, :] = other[...] * real
        win[:, mine_at : mine_at + half, :] = mine[:, mine_from : mine_from + half, :]

    pl.when(c == 0)(lambda: lay(half, 0, half))
    pl.when(c == 1)(lambda: lay(0, H, 0))
    step = functools.partial(scale_step, plan, at, taps, quad_ref)
    first = pl.multiple_of((S + H - 2 * R) * (1 - c), 8)
    second = pl.multiple_of((S + H - 4 * R) * (1 - c), 8)
    third = pl.multiple_of((S + H - 6 * R) * (1 - c), 8)
    return [
        step(zb, win, 0, v, tw, R, first, S),
        step(zc, v, second, u, sw, 2 * R, second, S),
        step(zb, u, third, v2, tw, 3 * R, third, S),
    ]


def late_kernel(plan, taps_ref, quad_ref, mine, other, sw, tw, v_in, u_in, v2_in,
                v, u, v2, u_out, win, zb, zc):
    del v_in, u_in, v2_in
    R, S = plan.R, plan.S
    at = place_of(plan)
    taps = kernel_taps(plan, taps_ref)
    clear_edges(zb, R, plan.X)
    clear_edges(zc, R, plan.X)
    passes = late_rows(plan, at, taps, quad_ref, mine, other, sw, tw, v, u, v2, win, zb, zc)
    passes.append(scale_step(plan, at, taps, quad_ref, zc, v2, 0, u_out, sw, 4 * R, 0, S))
    run_passes(plan, passes)


def smooth_taps(s_ref, reach):
    total = s_ref[0]
    tail = s_ref[1]
    for d in range(2, reach + 1):
        tail = tail + s_ref[d]
    scale = 1.0 / (jnp.zeros((1, LANES), jnp.float32) + (total + 2.0 * tail))
    return [scale * s_ref[d] for d in range(reach + 1)]


def last_kernel(plan, taps_ref, quad_ref, slope_ref, smooth_ref, mine, other, sw, tw, prev,
                gaps, tot, v_in, u_in, v2_in, v, u, v2, out_ref, win, zb, zc, zg, raw):
    del v_in, u_in, v2_in
    R, S, H, X, gs, Q = plan.R, plan.S, plan.H, plan.X, plan.gs, plan.Q
    half = S // 2
    size = 3 * half + 1
    c = lax.axis_index("gz")
    at = place_of(plan)
    taps = kernel_taps(plan, taps_ref)
    stap = [taps_ref[R + 1 + d, :1, :] for d in range(Q + 1)]
    clear_edges(zb, R, X)
    clear_edges(zc, R, X)
    clear_edges(zg, R, X)
    for comp in range(3):
        clear_edges(raw.at[comp], Q, X)
    real = jnp.where(jnp.where(c == 1, at > 0, at < plan.P - 1), 1.0, 0.0)

    @pl.when(c == 0)
    def _():
        win[:, :half, :] = mine[:, half:, :]
        win[:, half:, :] = other[:, :half, :] * real

    @pl.when(c == 1)
    def _():
        win[:, :half, :] = other[:, H - half :, :] * real
        win[:, half:, :] = mine[:, :half, :]

    step = functools.partial(scale_step, plan, at, taps, quad_ref)
    own = pl.multiple_of(half * c, 8)
    first = pl.multiple_of(S + half - S * c, 8)
    second = pl.multiple_of(S - half * c, 8)
    passes = [
        step(zb, win, 0, v, tw, R, first, half),
        step(zc, v, second, u, sw, 2 * R, second, half),
        step(zb, u, half, v2, tw, 3 * R, half, half),
    ]
    near = v2.at[:, pl.ds(own, S), :]

    def z_part(base):
        for x in range(base, base + MANY):
            load = lambda j: near[x, j : j + half, :]
            zc[R + x, :half, :] = unit_sum(load, taps, R)
            zg[R + x] = odd_sum(load, taps, R)

    def matmul_part(base):
        kk, gk, kg = [], [], []
        for q in range(MANY):
            flat = lambda j: zc[base + q + j, :half, :]
            kk.append(unit_sum(flat, taps, R))
            gk.append(odd_sum(flat, taps, R))
            kg.append(unit_sum(lambda j: zg[base + q + j], taps, R))
        kk, gk, kg = (jnp.concatenate(part, axis=0) for part in (kk, gk, kg))
        nums = lanes_times(gk, quad_ref), lanes_times(kk, slope_ref), lanes_times(kg, quad_ref)
        return lanes_times(kk, quad_ref), nums

    def emit_part(base, out):
        kvol, nums = out
        for comp, num in enumerate(nums):
            value = num / kvol
            for q in range(MANY):
                raw[comp, Q + base + q] = value[q * half : (q + 1) * half]

    run_passes(plan, passes + [(z_part, matmul_part, emit_part)])

    for i in range(plan.nx):
        for comp in range(3):
            x = plan.bx * i
            parts = [even_sum(lambda j: raw[comp, x + k + j], stap, Q) for k in range(plan.bx)]
            flat = lanes_times(jnp.concatenate(parts, axis=0), smooth_ref)
            for core in range(2):
                rows = range(gs * core, gs * (core + 1))
                turned = turn_groups(plan, [flat[k * half : (k + 1) * half] for k in rows])
                for j in range(plan.ny):
                    base = size * ((i * plan.ny + j) * 2 + core) + comp * half
                    out_ref[base : base + half, :] = turned[j]

    rows = gaps_of(plan, tot, tw, (prev, v), (v, v2))
    stat = gaps[...] + in_lanes(rows, ITERS - 2)
    for p in range(2 * plan.P):
        out_ref[size * (p + 1) - 1 : size * (p + 1), :] = stat


def smooth_z(plan, core, high_ref, low_ref, in_ref, data, emit):
    half = plan.S // 2
    size = 3 * half + 1
    for part in range(2 * plan.P):
        for comp in range(3):
            base = size * plan.device(part // 2, part % 2) + comp * half
            data[half * part : half * (part + 1), comp * LANES : (comp + 1) * LANES] = in_ref[
                base : base + half, :
            ]
    rows = pl.ds(pl.multiple_of(core * LANES, LANES), LANES)
    m_high, m_low = high_ref[rows, :], low_ref[rows, :]
    d_high, d_low = halves(data[...])
    dot = functools.partial(jnp.dot, preferred_element_type=jnp.float32)
    out = dot(m_high, d_high) + (dot(m_high, d_low) + dot(m_low, d_high))
    for comp in range(3):
        emit(comp, out[:, comp * LANES : (comp + 1) * LANES].T)


def away_kernel(plan, high_ref, low_ref, in_ref, send_ref, data):
    def emit(comp, value):
        send_ref[comp] = value

    smooth_z(plan, 1 - lax.axis_index("gz"), high_ref, low_ref, in_ref, data, emit)


def home_kernel(plan, high_ref, low_ref, in_ref, mis_ref, out_hbm, data, keep, sem):
    c = lax.axis_index("gz")
    gs = plan.gs

    def emit(comp, value):
        keep[comp] = value.reshape(gs, plan.by, LANES)

    smooth_z(plan, c, high_ref, low_ref, in_ref, data, emit)
    copy = pltpu.make_async_copy(keep, out_hbm.at[:, pl.ds(gs * c, gs)], sem)
    copy.start()
    gone = sum_rows(in_ref, 3 * plan.S // 2 + 1) / plan.cells
    for t in range(ITERS):
        mis_ref[t] = jnp.sum(jnp.where(lane_at() == t, gone, 0.0))
    copy.wait()


def place_kernel(plan, recv_ref, in_hbm, out_hbm, sem):
    del in_hbm
    c = lax.axis_index("gz")
    copy = pltpu.make_async_copy(recv_ref, out_hbm.at[:, pl.ds(plan.gs * (1 - c), plan.gs)], sem)
    copy.start()
    copy.wait()


def slab_shards(plan, source, target, kernel_half, smooth_half):
    R, S, H, X, XH, Pn, Z = plan.R, plan.S, plan.H, plan.X, plan.XH, plan.P, plan.Z
    bind = lambda kernel: functools.partial(kernel, plan)
    half = f32(2, LANES, LANES)
    vm = lambda *shape: pltpu.VMEM(shape, jnp.float32)
    keep, stat = call(
        bind(pack_kernel), [half, f32(1, LANES)], 0, 0,
        [vm(*source.shape), vm(*source.shape), pltpu.SemaphoreType.DMA((2,))], n_any=2,
    )(*(pltpu.with_memory_space_constraint(a, pltpu.HBM) for a in (source, target)))
    (chunks,) = call(
        bind(chunk_kernel), [f32(Pn * (2 * S + 1), LANES)], 0, 4, [vm(*half.shape)]
    )(keep, swap_cores(plan, source), swap_cores(plan, target), stat)
    spread = trade_chunks(chunks, ("gx", "gy"))
    own_s, own_t = call(
        bind(unpack_kernel), [f32(XH, S, LANES), f32(XH + 1, S, LANES)], 0, 1
    )(spread)
    square = jax.ShapeDtypeStruct((2 * LANES, 2 * LANES), jnp.bfloat16)
    table = jax.ShapeDtypeStruct((Z, Z), jnp.bfloat16)
    taps, quad_k, quad_g, quad_s, high, low = call(
        bind(prep_kernel), [f32(plan.R + plan.Q + 2, 8, LANES), square, square, square, table, table],
        2, 0, n_any=1,
    )(kernel_half, smooth_half, own_s)
    even_s, odd_s = swap_even(plan, own_s), swap_odd(plan, own_s)
    even_t, odd_t = swap_even(plan, own_t), swap_odd(plan, own_t)
    own2_s, own2_t = swap_cores(plan, own_s), swap_cores(plan, own_t)
    even_s, odd_s, taps = lax.optimization_barrier((even_s, odd_s, taps))
    halos_s = swap_cores(plan, even_s), swap_cores(plan, odd_s)
    even_t, odd_t, own2_s = lax.optimization_barrier((even_t, odd_t, own2_s))
    halos_t = swap_cores(plan, even_t), swap_cores(plan, odd_t)

    slab = f32(X, S, LANES)
    width = S + 2 * H
    wide, v_shape, u_shape, v2_shape = (f32(X, width - 2 * k * R, LANES) for k in (0, 1, 2, 3))
    zb = vm(X + 2 * R, width - 2 * R, LANES)
    sw, ku = call(
        bind(open_kernel), [wide, v_shape], 0, 8, [vm(*wide.shape), zb]
    )(taps, quad_k, own_s, even_s, odd_s, own2_s, *halos_s)
    tw, v1, v2, u, tot = call(
        bind(first_kernel), [wide, v_shape, v2_shape, slab, f32(1, LANES)], 0, 10,
        [vm(*u_shape.shape), zb, zb],
    )(taps, quad_k, own_t, even_t, odd_t, own2_t, *halos_t, sw, ku)

    def early(u, side):
        return call(
            bind(early_kernel), [v_shape, u_shape, v2_shape], 0, 6,
            [vm(X, S + H, LANES), zb, zb],
        )(taps, quad_k, u, side, sw, tw)

    rest = vm(X, H + S // 2, LANES)
    side = swap_sides(plan, u)
    other = swap_cores(plan, side)
    v3, u4, v4 = early(u, side)
    v3, _, v4, u = call(
        bind(late_kernel), [v_shape, u_shape, v2_shape, slab], 0, 9, [rest, zb, zb],
        aliases={6: 0, 7: 1, 8: 2},
    )(taps, quad_k, u, other, sw, tw, v3, u4, v4)
    side = swap_sides(plan, u)
    (gaps,) = call(bind(gaps_kernel), [f32(1, LANES)], 0, 6)(tot, tw, v1, v2, v3, v4)
    side, gaps = lax.optimization_barrier((side, gaps))
    other = swap_cores(plan, side)
    v5, u6, v6 = early(u, side)
    *_, chunks = call(
        bind(last_kernel), [v_shape, u_shape, v2_shape, f32(2 * Pn * (3 * S // 2 + 1), LANES)], 0, 14,
        [vm(X, S, LANES), zb, zb, vm(X + 2 * R, S // 2, LANES), vm(3, X + 2 * plan.Q, S // 2, LANES)],
        aliases={11: 0, 12: 1, 13: 2},
    )(taps, quad_k, quad_g, quad_s, u, other, sw, tw, v4, gaps, tot, v5, u6, v6)
    spread = trade_chunks(chunks, AXES)
    data = vm(Z, 3 * LANES)
    (send,) = call(bind(away_kernel), [f32(3, LANES, LANES)], 0, 3, [data])(high, low, spread)
    half = (3, plan.gs, plan.by, LANES)
    recv = swap_cores(plan, send.reshape(half))
    whole = f32(3, plan.bx, plan.by, LANES)
    mismatch, displacement = call(
        bind(home_kernel), [f32(ITERS), whole], 0, 3, [data, vm(*half), pltpu.SemaphoreType.DMA(())],
        smem_out=1, any_out=1,
    )(high, low, spread)
    (displacement,) = call(
        bind(place_kernel), [whole], 0, 1, [pltpu.SemaphoreType.DMA(())], n_any=1, any_out=1,
        aliases={1: 0},
    )(recv, displacement)
    return displacement, mismatch


def shards(sizes, source, target, kernel_half, smooth_half):
    plan = Plan(sizes, *source.shape, kernel_half.shape[0] - 1, smooth_half.shape[0] - 1)
    if plan.fits():
        return slab_shards(plan, source, target, kernel_half, smooth_half)
    return block_shards(source, target, kernel_half, smooth_half)


def solution(mesh):
    in_specs = (P("gx", "gy", "gz"), P("gx", "gy", "gz"), P(), P())
    out_specs = (P(None, "gx", "gy", "gz"), P())
    body = functools.partial(shards, dict(mesh.shape))
    return jax.shard_map(body, mesh=mesh, in_specs=in_specs, out_specs=out_specs, check_vma=False)
```

```python
import functools

import jax
import jax.numpy as jnp
from jax import lax
from jax.experimental import pallas as pl
from jax.experimental.pallas import tpu as pltpu
from jax.sharding import PartitionSpec as P


ITERS = 6
LANES = 128
AXES = ("gx", "gy", "gz")


def padded_2(block, sides, width):
    for axis, dim in sides:
        count = lax.axis_size(axis)
        forward = [(i, i + 1) for i in range(count - 1)]
        backward = [(target, source) for source, target in forward]
        low = lax.ppermute(
            lax.slice_in_dim(block, block.shape[dim] - width, None, axis=dim), axis, forward
        )
        high = lax.ppermute(lax.slice_in_dim(block, 0, width, axis=dim), axis, backward)
        block = jnp.concatenate([low, block, high], axis=dim)
    return block


def full_taps(half):
    return jnp.concatenate([half[:0:-1], half])


def along(padded, taps, axis, count):
    width = taps.shape[0]
    total = taps[0] * lax.slice_in_dim(padded, 0, count, axis=axis)
    for j in range(1, width):
        total = total + taps[j] * lax.slice_in_dim(padded, j, j + count, axis=axis)
    return total


def three_passes(padded, taps, size_x, size_y, size_z):
    padded = along(padded, taps, 0, size_x)
    padded = along(padded, taps, 1, size_y)
    return along(padded, taps, 2, size_z)


def block_shards(source, target, kernel_half, smooth_half):
    kern = full_taps(kernel_half)
    radius = kernel_half.shape[0] - 1
    reach = smooth_half.shape[0] - 1
    offsets = jnp.arange(-radius, radius + 1).astype(jnp.float32)
    slope = offsets * kern
    norm_total = smooth_half[0] + 2.0 * jnp.sum(smooth_half[1:])
    smooth = full_taps(smooth_half) / norm_total
    size_x, size_y, size_z = source.shape
    cells = float(source.size * lax.axis_size("gx") * lax.axis_size("gy") * lax.axis_size("gz"))
    totals = lax.psum((jnp.sum(source), jnp.sum(target)), AXES)
    first = source * (cells / totals[0])
    second = target * (cells / totals[1])
    first_wide = padded_2(first, (("gx", 0), ("gy", 1), ("gz", 2)), radius)
    scaling_v = jnp.ones_like(source)
    errors = []
    for _ in range(ITERS):
        padded = padded_2(scaling_v, (("gx", 0), ("gy", 1), ("gz", 2)), 2 * radius)
        kv_wide = three_passes(
            padded, kern, size_x + 2 * radius, size_y + 2 * radius, size_z + 2 * radius
        )
        u_wide = first_wide / kv_wide
        ku = three_passes(u_wide, kern, size_x, size_y, size_z)
        local_err = jnp.sum(jnp.abs(scaling_v * ku - second))
        errors.append(lax.psum(local_err, AXES) / cells)
        scaling_v = second / ku
    mismatch = jnp.stack(errors)
    padded = padded_2(scaling_v, (("gx", 0), ("gy", 1), ("gz", 2)), radius)
    pass_k = along(padded, kern, 0, size_x)
    pass_g = along(padded, slope, 0, size_x)
    kk = along(pass_k, kern, 1, size_y)
    kg = along(pass_k, slope, 1, size_y)
    gk = along(pass_g, kern, 1, size_y)
    kvol = along(kk, kern, 2, size_z)
    znum = along(kk, slope, 2, size_z)
    ynum = along(kg, kern, 2, size_z)
    xnum = along(gk, kern, 2, size_z)
    raw = jnp.stack([xnum, ynum, znum]) / kvol
    padded = padded_2(raw, (("gx", 1), ("gy", 2), ("gz", 3)), reach)
    padded = along(padded, smooth, 1, size_x)
    padded = along(padded, smooth, 2, size_y)
    displacement = along(padded, smooth, 3, size_z)
    return (displacement, mismatch)


class Plan:
    def __init__(self, mesh, bx, by, bz, radius, reach):
        self.nx, self.ny, self.nc = mesh["gx"], mesh["gy"], mesh["gz"]
        self.bx, self.by, self.bz = bx, by, bz
        self.R, self.Q = radius, reach
        self.P = self.nx * self.ny
        self.X, self.Y, self.Z = bx * self.nx, by * self.ny, bz * self.nc
        self.S = self.Z // self.P
        self.H = 4 * radius
        self.gs = LANES // by if by <= LANES else 0
        self.XH = self.X // 2
        self.cells = float(self.X * self.Y * self.Z)

    def fits(self):
        return (
            self.nc == 2
            and self.ny >= 2
            and self.ny & (self.ny - 1) == 0
            and self.nx >= 2
            and self.bz == LANES
            and self.Y == LANES
            and self.gs == self.ny
            and self.bx == 2 * self.gs
            and self.Z == self.P * self.S
            and self.S == self.H
            and self.S % 16 == 0
            and self.R % 4 == 0
            and ITERS == 6
        )

    def spot(self, at):
        at %= self.P
        col, q = divmod(at, self.nx)
        return (q if col % 2 == 0 else self.nx - 1 - q), col ^ (col >> 1)

    def chip(self, at):
        i, j = self.spot(at)
        return i * self.ny + j

    def device(self, at, core):
        return self.chip(at) * self.nc + core


def swap_cores(plan, value):
    pairs = [(plan.device(at, c), plan.device(at, 1 - c)) for at in range(plan.P) for c in range(2)]
    return lax.ppermute(value, AXES, pairs)


def swap_even(plan, value):
    pairs = [(plan.device(at, c), plan.device(at ^ 1, c)) for at in range(plan.P) for c in range(2)]
    return lax.ppermute(value, AXES, pairs)


def swap_odd(plan, value):
    pairs = [
        (plan.device(at, c), plan.device(((at + 1) ^ 1) - 1, c))
        for at in range(plan.P)
        for c in range(2)
    ]
    return lax.ppermute(value, AXES, pairs)


def swap_sides(plan, value):
    pairs = [(plan.device(at, 0), plan.device(at - 1, 1)) for at in range(plan.P)]
    pairs += [(plan.device(at, 1), plan.device(at + 1, 0)) for at in range(plan.P)]
    return lax.ppermute(value, AXES, pairs)


def trade_chunks(value, axes):
    rows, lanes = value.shape
    out = lax.all_to_all(value.reshape(rows, 1, lanes), axes, 0, 0, tiled=True)
    return out.reshape(rows, lanes)


def place_of(plan):
    i, j = lax.axis_index("gx"), lax.axis_index("gy")
    at = jnp.int32(0)
    for place in range(plan.P):
        a, b = plan.spot(place)
        at = at + jnp.where((i == a) & (j == b), place, 0)
    return at.astype(jnp.int32)


def call(kernel, out_shape, n_smem, n_vmem, scratch=(), smem_out=0, n_any=0, any_out=0, aliases=None):
    vm, sm = pl.BlockSpec(memory_space=pltpu.VMEM), pl.BlockSpec(memory_space=pltpu.SMEM)
    hbm = pl.BlockSpec(memory_space=pltpu.HBM)
    out_specs = [vm] * (len(out_shape) - smem_out - any_out) + [sm] * smem_out + [hbm] * any_out
    return pl.pallas_call(
        kernel,
        out_shape=out_shape,
        in_specs=[sm] * n_smem + [vm] * n_vmem + [hbm] * n_any,
        out_specs=out_specs,
        scratch_shapes=list(scratch),
        input_output_aliases=aliases or {},
        compiler_params=pltpu.CompilerParams(vmem_limit_bytes=48 << 20),
    )


def f32(*shape):
    return jax.ShapeDtypeStruct(shape, jnp.float32)


def turn_groups(plan, parts):
    n, w = plan.gs, plan.by
    group = lax.broadcasted_iota(jnp.int32, parts[0].shape, 1) // w
    outs = []
    for a in range(n):
        total = parts[a]
        for b in range(n):
            if b != a:
                moved = pltpu.roll(parts[b], (w * (b - a)) % LANES, 1)
                total = jnp.where(group == b, moved, total)
        outs.append(total)
    return outs


def pack_kernel(plan, src_hbm, tgt_hbm, keep_ref, stat_ref, src_ref, tgt_ref, sems):
    c = lax.axis_index("gz")
    copies = [
        pltpu.make_async_copy(src_hbm, src_ref, sems.at[0]),
        pltpu.make_async_copy(tgt_hbm, tgt_ref, sems.at[1]),
    ]
    for copy in copies:
        copy.start()
    sums = []
    for st, ref in enumerate((src_ref, tgt_ref)):
        copies[st].wait()
        keep_ref[st] = ref[pl.ds(plan.gs * c, plan.gs)].reshape(LANES, LANES).T
        row = jnp.sum(ref[...].reshape(plan.bx * plan.by, LANES), axis=0, keepdims=True)
        sums.append(row + pltpu.roll(row, LANES // 2, 1))
    stat_ref[...] = jnp.where(lane_at() < LANES // 2, *sums)


def lane_at():
    return lax.broadcasted_iota(jnp.int32, (1, LANES), 1)


def chunk_kernel(plan, keep_ref, src_ref, tgt_ref, stat_ref, out_ref, recv_ref):
    c = lax.axis_index("gz")
    half, S = plan.P // 2, plan.S
    size = 2 * S + 1
    for st, ref in enumerate((src_ref, tgt_ref)):
        recv_ref[st] = ref[pl.ds(plan.gs * c, plan.gs)].reshape(LANES, LANES).T

    def write(low_ref, high_ref):
        stat = stat_ref[...]
        for place in range(plan.P):
            ref, part = (low_ref, place) if place < half else (high_ref, place - half)
            base = size * plan.chip(place)
            for st in range(2):
                out_ref[base + S * st : base + S * st + S, :] = ref[st, S * part : S * part + S, :]
            out_ref[base + 2 * S : base + size, :] = stat

    pl.when(c == 0)(lambda: write(keep_ref, recv_ref))
    pl.when(c == 1)(lambda: write(recv_ref, keep_ref))


def unpack_kernel(plan, st, in_ref, out_ref):
    S, gs, XH = plan.S, plan.gs, plan.XH
    size = 2 * S + 1
    for i in range(plan.nx):
        bases = [size * (i * plan.ny + j) + S * st for j in range(plan.ny)]
        parts = [in_ref[base : base + S, :] for base in bases]
        for xx, value in enumerate(turn_groups(plan, parts)):
            out_ref[i * gs + xx] = value
    if st:
        out_ref[XH] = jnp.zeros((S, LANES), jnp.float32)
        out_ref[XH, :1, :] = sum_rows(in_ref, size)


def sum_rows(ref, size):
    total = ref[size - 1 : size, :]
    for p in range(1, ref.shape[0] // size):
        total = total + ref[size * p + size - 1 : size * p + size, :]
    return total


def banded(taps, n, odd):
    row = lax.broadcasted_iota(jnp.int32, (n, n), 0)
    col = lax.broadcasted_iota(jnp.int32, (n, n), 1)
    gap = row - col
    total = jnp.zeros((n, n), jnp.float32)
    for d, tap in enumerate(taps):
        if odd:
            if d:
                total = jnp.where(gap == d, d * tap, total)
                total = jnp.where(gap == -d, -(d * tap), total)
        else:
            total = jnp.where(jnp.abs(gap) == d, tap, total)
    return total


def halves(value):
    high = value.astype(jnp.bfloat16)
    return high, (value - high.astype(jnp.float32)).astype(jnp.bfloat16)


def quad(matrix):
    high, low = halves(matrix)
    row = jnp.concatenate([high, low], axis=1)
    return jnp.concatenate([row, row], axis=0)


def lanes_times(value, quad_ref):
    high, low = halves(value)
    both = jnp.concatenate([high, low], axis=1)
    out = jnp.dot(both, quad_ref[...], preferred_element_type=jnp.float32)
    return out[:, :LANES] + out[:, LANES:]


def even_sum(load, taps, mid):
    total = taps[0] * load(mid)
    for d in range(1, len(taps)):
        total = total + taps[d] * (load(mid - d) + load(mid + d))
    return total


def unit_sum(load, taps, mid):
    total = load(mid)
    for d in range(1, len(taps)):
        total = total + taps[d] * (load(mid - d) + load(mid + d))
    return total


def odd_sum(load, taps, mid):
    total = taps[1] * (load(mid + 1) - load(mid - 1))
    for d in range(2, len(taps)):
        total = total + (d * taps[d]) * (load(mid + d) - load(mid - d))
    return total


MANY = 16


def run_passes(plan, passes):
    chunks = range(0, plan.X, MANY)
    for base in chunks:
        passes[0][0](base)
    for (_, matmul_part, emit_part), after in zip(passes, passes[1:] + [None]):
        done = None

        def close(pair):
            emit_part(*pair)
            if after is not None:
                after[0](pair[0])

        for base in chunks:
            out = matmul_part(base)
            if done is not None:
                close(done)
            done = (base, out)
        close(done)


def kernel_pass(plan, taps, quad_ref, in_ref, zb_ref, rows, emit):
    R = plan.R

    def z_part(base):
        for x in range(base, base + MANY):
            zb_ref[R + x, :rows, :] = unit_sum(lambda j: in_ref[x, j : j + rows, :], taps, R)

    def matmul_part(base):
        parts = [
            unit_sum(lambda j: zb_ref[base + q + j, :rows, :], taps, R) for q in range(MANY)
        ]
        return lanes_times(jnp.concatenate(parts, axis=0), quad_ref)

    def emit_part(base, out):
        for q in range(MANY):
            emit(base + q, out[q * rows : (q + 1) * rows])

    return z_part, matmul_part, emit_part


def inside(plan, at, off, rows):
    z = lax.broadcasted_iota(jnp.int32, (rows, LANES), 0) + (at * plan.S - plan.H + off)
    return (z >= 0) & (z < plan.Z)


def scale_step(plan, at, taps, quad_ref, zb, src, top, dst, over, off, start, rows):
    mask = inside(plan, at, off + start, rows)
    src = src.at[:, pl.ds(top, rows + 2 * plan.R), :]
    lead = (off + 7) // 8 * 8
    over = over.at[:, pl.ds(start, rows + lead), :]

    def emit(x, value):
        dst[x, pl.ds(start, rows), :] = jnp.where(mask, over[x, off : off + rows, :] / value, 0.0)

    return kernel_pass(plan, taps, quad_ref, src, zb, rows, emit)


def clear_edges(ref, edge, size):
    blank = jnp.zeros((edge,) + ref.shape[1:], jnp.float32)
    ref[:edge] = blank
    ref[edge + size :] = blank


def prep_kernel(plan, k_ref, s_ref, own, taps_ref, quad_ref, slope_ref, smooth_ref, high_ref,
                low_ref, plane_ref, line_ref):
    del own
    R, Q = plan.R, plan.Q
    taps = [jnp.zeros((1, LANES), jnp.float32) + k_ref[d] for d in range(R + 1)]
    taps = [jnp.ones((1, LANES), jnp.float32)] + [tap / taps[0] for tap in taps[1:]]
    stap = smooth_taps(s_ref, Q)
    for d in range(R + 1):
        taps_ref[d] = jnp.broadcast_to(taps[d], (8, LANES))
    for d in range(Q + 1):
        taps_ref[R + 1 + d] = jnp.broadcast_to(stap[d], (8, LANES))
    quad_ref[...] = quad(banded(taps, LANES, False))
    slope_ref[...] = quad(banded(taps, LANES, True))
    smooth_ref[...] = quad(banded(stap, LANES, False))
    wide = [jnp.concatenate([t] * (plan.Z // LANES), axis=1) for t in stap]
    high_ref[...], low_ref[...] = halves(banded(wide, plan.Z, False))


    def reach_sum(shape, axis, start, size):
        place = lax.broadcasted_iota(jnp.int32, shape, axis) + start
        total = jnp.ones(shape, jnp.float32)
        for d in range(1, R + 1):
            total = total + jnp.where(place - d >= 0, taps[d], 0.0)
            total = total + jnp.where(place + d < size, taps[d], 0.0)
        return total

    at = place_of(plan)
    shape = plane_ref.shape
    over = reach_sum(shape, 0, at * plan.S - plan.H, plan.Z) * reach_sum(shape, 1, 0, plan.Y)
    plane_ref[...] = jnp.where(inside(plan, at, 0, shape[0]), 1.0 / over, 0.0)
    line_ref[...] = 1.0 / reach_sum(line_ref.shape, 0, 0, plan.X)


def kernel_taps(plan, taps_ref):
    return [taps_ref[d, :1, :] for d in range(plan.R + 1)]


def gaps_of(plan, tot, tw, olds, news):
    S = plan.S
    half = S // 2
    mine = pl.multiple_of(half * lax.axis_index("gz"), 8)
    first_half = lane_at() < LANES // 2
    both = tot[:1, :]
    sum_s = jnp.sum(jnp.where(first_half, both, 0.0), axis=1, keepdims=True)
    sum_t = jnp.sum(jnp.where(first_half, 0.0, both), axis=1, keepdims=True)
    scale_s = plan.cells / jnp.broadcast_to(sum_s, (1, LANES))
    scale_t = plan.cells / jnp.broadcast_to(sum_t, (1, LANES))

    def mid(ref):
        edge = (ref.shape[1] - S) // 2
        ref = ref.at[:, pl.ds(mine, ref.shape[1] - half), :]
        return lambda x: ref[x, edge : edge + half, :]

    t_at = mid(tw)
    olds = [old if old is None else mid(old) for old in olds]
    news = [mid(new) for new in news]

    def p_step(x, carry):
        t = t_at(x)
        want = scale_t * t
        have = scale_s * t
        result = []
        for part, old, new in zip(carry, olds, news):
            value = have / new(x)
            if old is not None:
                value = value * old(x)
            gap = jnp.abs(value - want)
            for r in range(0, half, 8):
                part = part + gap[r : r + 8]
            result.append(part)
        return tuple(result)

    zero = jnp.zeros((8, LANES), jnp.float32)
    gaps = lax.fori_loop(0, plan.X, p_step, (zero,) * len(news), unroll=4)
    return [jnp.sum(g, keepdims=True) for g in gaps]


def in_lanes(values, first=0):
    row = jnp.zeros((1, LANES), jnp.float32)
    for t, value in enumerate(values):
        row = jnp.where(lane_at() == first + t, value, row)
    return row


def gaps_kernel(plan, tot, tw, v1, v2, v3, v4, out_ref):
    out_ref[...] = in_lanes(gaps_of(plan, tot, tw, (None, v1, v2, v3), (v1, v2, v3, v4)))


def spread_halves(plan, at, own, even, odd, own2, even2, odd2, win):
    S, H, gs = plan.S, plan.H, plan.gs
    c = lax.axis_index("gz")

    def spread(low, high):
        for k, (mid, core) in enumerate(((own, c), (own2, 1 - c))):
            for i in range(plan.nx):
                x, here = plan.bx * i + gs * core, pl.ds(i * gs, gs)
                win[pl.ds(x, gs), H : H + S, :] = mid[here]
                win[pl.ds(x, gs), :H, :] = low[k][here]
                win[pl.ds(x, gs), H + S :, :] = high[k][here]

    pl.when(at % 2 == 0)(lambda: spread((odd, odd2), (even, even2)))
    pl.when(at % 2 == 1)(lambda: spread((even, even2), (odd, odd2)))


def open_kernel(plan, taps_ref, quad_ref, plane_ref, line_ref, own, even, odd, own2, even2, odd2,
                sw, ku, u, zb):
    R = plan.R
    at = place_of(plan)
    taps = kernel_taps(plan, taps_ref)
    clear_edges(zb, R, plan.X)
    spread_halves(plan, at, own, even, odd, own2, even2, odd2, sw)
    for x in range(plan.X):
        u[x] = sw[x] * (plane_ref[...] * line_ref[x : x + 1, :])

    def emit(x, value):
        ku[x] = value

    rows = ku.shape[1]
    run_passes(plan, [kernel_pass(plan, taps, quad_ref, u, zb, rows, emit)])


def first_kernel(plan, taps_ref, quad_ref, own, even, odd, own2, even2, odd2, sw, ku,
                 tw, v, v2, u_out, tot, u, zb, zc):
    R, S, H, X, XH = plan.R, plan.S, plan.H, plan.X, plan.XH
    at = place_of(plan)
    taps = kernel_taps(plan, taps_ref)
    clear_edges(zb, R, X)
    clear_edges(zc, R, X)
    spread_halves(plan, at, own, even, odd, own2, even2, odd2, tw)
    tot[...] = own[XH, :1, :] + own2[XH, :1, :]
    rows = S + 2 * H - 2 * R
    mask = inside(plan, at, R, rows)

    def v_step(x, carry):
        v[x] = jnp.where(mask, tw[x, R : R + rows, :] / ku[x], 0.0)
        return carry

    lax.fori_loop(0, X, v_step, 0, unroll=4)
    step = functools.partial(scale_step, plan, at, taps, quad_ref)
    run_passes(plan, [
        step(zb, v, 0, u, sw, 2 * R, 0, rows - 2 * R),
        step(zc, u, 0, v2, tw, 3 * R, 0, rows - 4 * R),
        step(zb, v2, 0, u_out, sw, 4 * R, 0, rows - 6 * R),
    ])


def early_kernel(plan, taps_ref, quad_ref, mine, side, sw, tw, v, u, v2, win, zb, zc):
    R, S, H = plan.R, plan.S, plan.H
    c = lax.axis_index("gz")
    at = place_of(plan)
    taps = kernel_taps(plan, taps_ref)
    clear_edges(zb, R, plan.X)
    clear_edges(zc, R, plan.X)
    real = jnp.where(jnp.where(c == 0, at > 0, at < plan.P - 1), 1.0, 0.0)
    win[:, pl.ds(pl.multiple_of(H * c, 8), H), :] = side[...] * real
    win[:, pl.ds(pl.multiple_of(H * (1 - c), 8), S), :] = mine[...]
    step = functools.partial(scale_step, plan, at, taps, quad_ref)
    from_ = pl.multiple_of(S * c, 8)
    run_passes(plan, [
        step(zb, win, 0, v, tw, R, from_, S + H - 2 * R),
        step(zc, v, from_, u, sw, 2 * R, from_, S + H - 4 * R),
        step(zb, u, from_, v2, tw, 3 * R, from_, S + H - 6 * R),
    ])


def late_rows(plan, at, taps, quad_ref, mine, other, sw, tw, v, u, v2, win, zb, zc):
    R, S, H = plan.R, plan.S, plan.H
    c = lax.axis_index("gz")
    real = jnp.where(jnp.where(c == 1, at > 0, at < plan.P - 1), 1.0, 0.0)
    half = S // 2

    def lay(other_at, mine_at, mine_from):
        win[:, other_at : other_at + H, :] = other[...] * real
        win[:, mine_at : mine_at + half, :] = mine[:, mine_from : mine_from + half, :]

    pl.when(c == 0)(lambda: lay(half, 0, half))
    pl.when(c == 1)(lambda: lay(0, H, 0))
    step = functools.partial(scale_step, plan, at, taps, quad_ref)
    first = pl.multiple_of((S + H - 2 * R) * (1 - c), 8)
    second = pl.multiple_of((S + H - 4 * R) * (1 - c), 8)
    third = pl.multiple_of((S + H - 6 * R) * (1 - c), 8)
    return [
        step(zb, win, 0, v, tw, R, first, S),
        step(zc, v, second, u, sw, 2 * R, second, S),
        step(zb, u, third, v2, tw, 3 * R, third, S),
    ]


def late_kernel(plan, taps_ref, quad_ref, mine, other, sw, tw, v_in, u_in, v2_in,
                v, u, v2, u_out, win, zb, zc):
    del v_in, u_in, v2_in
    R, S = plan.R, plan.S
    at = place_of(plan)
    taps = kernel_taps(plan, taps_ref)
    clear_edges(zb, R, plan.X)
    clear_edges(zc, R, plan.X)
    passes = late_rows(plan, at, taps, quad_ref, mine, other, sw, tw, v, u, v2, win, zb, zc)
    passes.append(scale_step(plan, at, taps, quad_ref, zc, v2, 0, u_out, sw, 4 * R, 0, S))
    run_passes(plan, passes)


def smooth_taps(s_ref, reach):
    total = s_ref[0]
    tail = s_ref[1]
    for d in range(2, reach + 1):
        tail = tail + s_ref[d]
    scale = 1.0 / (jnp.zeros((1, LANES), jnp.float32) + (total + 2.0 * tail))
    return [scale * s_ref[d] for d in range(reach + 1)]


def last_kernel(plan, taps_ref, quad_ref, slope_ref, smooth_ref, mine, other, sw, tw, prev,
                gaps, tot, v_in, u_in, v2_in, v, u, v2, out_ref, win, zb, zc, zg, raw):
    del v_in, u_in, v2_in
    R, S, H, X, gs, Q = plan.R, plan.S, plan.H, plan.X, plan.gs, plan.Q
    half = S // 2
    size = 3 * half + 1
    c = lax.axis_index("gz")
    at = place_of(plan)
    taps = kernel_taps(plan, taps_ref)
    stap = [taps_ref[R + 1 + d, :1, :] for d in range(Q + 1)]
    clear_edges(zb, R, X)
    clear_edges(zc, R, X)
    clear_edges(zg, R, X)
    for comp in range(3):
        clear_edges(raw.at[comp], Q, X)
    real = jnp.where(jnp.where(c == 1, at > 0, at < plan.P - 1), 1.0, 0.0)

    @pl.when(c == 0)
    def _():
        win[:, :half, :] = mine[:, half:, :]
        win[:, half:, :] = other[:, :half, :] * real

    @pl.when(c == 1)
    def _():
        win[:, :half, :] = other[:, H - half :, :] * real
        win[:, half:, :] = mine[:, :half, :]

    step = functools.partial(scale_step, plan, at, taps, quad_ref)
    own = pl.multiple_of(half * c, 8)
    first = pl.multiple_of(S + half - S * c, 8)
    second = pl.multiple_of(S - half * c, 8)
    passes = [
        step(zb, win, 0, v, tw, R, first, half),
        step(zc, v, second, u, sw, 2 * R, second, half),
        step(zb, u, half, v2, tw, 3 * R, half, half),
    ]
    near = v2.at[:, pl.ds(own, S), :]

    def z_part(base):
        for x in range(base, base + MANY):
            load = lambda j: near[x, j : j + half, :]
            zc[R + x, :half, :] = unit_sum(load, taps, R)
            zg[R + x] = odd_sum(load, taps, R)

    def matmul_part(base):
        kk, gk, kg = [], [], []
        for q in range(MANY):
            flat = lambda j: zc[base + q + j, :half, :]
            kk.append(unit_sum(flat, taps, R))
            gk.append(odd_sum(flat, taps, R))
            kg.append(unit_sum(lambda j: zg[base + q + j], taps, R))
        kk, gk, kg = (jnp.concatenate(part, axis=0) for part in (kk, gk, kg))
        nums = lanes_times(gk, quad_ref), lanes_times(kk, slope_ref), lanes_times(kg, quad_ref)
        return lanes_times(kk, quad_ref), nums

    def emit_part(base, out):
        kvol, nums = out
        for comp, num in enumerate(nums):
            value = num / kvol
            for q in range(MANY):
                raw[comp, Q + base + q] = value[q * half : (q + 1) * half]

    run_passes(plan, passes + [(z_part, matmul_part, emit_part)])

    for i in range(plan.nx):
        for comp in range(3):
            x = plan.bx * i
            parts = [even_sum(lambda j: raw[comp, x + k + j], stap, Q) for k in range(plan.bx)]
            flat = lanes_times(jnp.concatenate(parts, axis=0), smooth_ref)
            for core in range(2):
                rows = range(gs * core, gs * (core + 1))
                turned = turn_groups(plan, [flat[k * half : (k + 1) * half] for k in rows])
                for j in range(plan.ny):
                    base = size * ((i * plan.ny + j) * 2 + core) + comp * half
                    out_ref[base : base + half, :] = turned[j]

    rows = gaps_of(plan, tot, tw, (prev, v), (v, v2))
    stat = gaps[...] + in_lanes(rows, ITERS - 2)
    for p in range(2 * plan.P):
        out_ref[size * (p + 1) - 1 : size * (p + 1), :] = stat


def smooth_z(plan, core, high_ref, low_ref, in_ref, data, emit):
    half = plan.S // 2
    size = 3 * half + 1
    for part in range(2 * plan.P):
        for comp in range(3):
            base = size * plan.device(part // 2, part % 2) + comp * half
            data[half * part : half * (part + 1), comp * LANES : (comp + 1) * LANES] = in_ref[
                base : base + half, :
            ]
    rows = pl.ds(pl.multiple_of(core * LANES, LANES), LANES)
    m_high, m_low = high_ref[rows, :], low_ref[rows, :]
    d_high, d_low = halves(data[...])
    dot = functools.partial(jnp.dot, preferred_element_type=jnp.float32)
    out = dot(m_high, d_high) + (dot(m_high, d_low) + dot(m_low, d_high))
    for comp in range(3):
        emit(comp, out[:, comp * LANES : (comp + 1) * LANES].T)


def away_kernel(plan, high_ref, low_ref, in_ref, send_ref, data):
    def emit(comp, value):
        send_ref[comp] = value

    smooth_z(plan, 1 - lax.axis_index("gz"), high_ref, low_ref, in_ref, data, emit)


def home_kernel(plan, high_ref, low_ref, in_ref, mis_ref, out_hbm, data, keep, sems):
    c = lax.axis_index("gz")
    gs = plan.gs
    gone = sum_rows(in_ref, 3 * plan.S // 2 + 1) / plan.cells
    for t in range(ITERS):
        mis_ref[t] = jnp.sum(jnp.where(lane_at() == t, gone, 0.0))
    copies = [
        pltpu.make_async_copy(keep.at[k], out_hbm.at[k, pl.ds(gs * c, gs)], sems.at[k])
        for k in range(3)
    ]

    def emit(comp, value):
        keep[comp] = value.reshape(gs, plan.by, LANES)
        copies[comp].start()

    smooth_z(plan, c, high_ref, low_ref, in_ref, data, emit)
    for copy in copies:
        copy.wait()


def place_kernel(plan, recv_ref, in_hbm, out_hbm, sems):
    del in_hbm
    at = pl.ds(plan.gs * (1 - lax.axis_index("gz")), plan.gs)
    copies = [
        pltpu.make_async_copy(recv_ref.at[k], out_hbm.at[k, at], sems.at[k]) for k in range(3)
    ]
    for copy in copies:
        copy.start()
    for copy in copies:
        copy.wait()


def slab_shards(plan, source, target, kernel_half, smooth_half):
    R, S, H, X, XH, Pn, Z = plan.R, plan.S, plan.H, plan.X, plan.XH, plan.P, plan.Z
    bind = lambda kernel, *more: functools.partial(kernel, plan, *more)
    half = f32(2, LANES, LANES)
    vm = lambda *shape: pltpu.VMEM(shape, jnp.float32)
    keep, stat = call(
        bind(pack_kernel), [half, f32(1, LANES)], 0, 0,
        [vm(*source.shape), vm(*source.shape), pltpu.SemaphoreType.DMA((2,))], n_any=2,
    )(*(pltpu.with_memory_space_constraint(a, pltpu.HBM) for a in (source, target)))
    (chunks,) = call(
        bind(chunk_kernel), [f32(Pn * (2 * S + 1), LANES)], 0, 4, [vm(*half.shape)]
    )(keep, swap_cores(plan, source), swap_cores(plan, target), stat)
    spread = trade_chunks(chunks, ("gx", "gy"))
    unpack = lambda st: call(bind(unpack_kernel, st), [f32(XH + st, S, LANES)], 0, 1)(spread)[0]
    own_s = unpack(0)
    own_t = unpack(1)
    square = jax.ShapeDtypeStruct((2 * LANES, 2 * LANES), jnp.bfloat16)
    table = jax.ShapeDtypeStruct((Z, Z), jnp.bfloat16)
    taps, quad_k, quad_g, quad_s, high, low, plane, line = call(
        bind(prep_kernel),
        [f32(R + plan.Q + 2, 8, LANES), square, square, square, table, table,
         f32(S + 2 * H, LANES), f32(X, LANES)],
        2, 0, n_any=1,
    )(kernel_half, smooth_half, own_s)
    even_s, odd_s = swap_even(plan, own_s), swap_odd(plan, own_s)
    even_t, odd_t = swap_even(plan, own_t), swap_odd(plan, own_t)
    own2_s, own2_t = swap_cores(plan, own_s), swap_cores(plan, own_t)
    even_s, odd_s, taps = lax.optimization_barrier((even_s, odd_s, taps))
    halos_s = swap_cores(plan, even_s), swap_cores(plan, odd_s)
    even_t, odd_t, own2_s = lax.optimization_barrier((even_t, odd_t, own2_s))
    halos_t = swap_cores(plan, even_t), swap_cores(plan, odd_t)

    slab = f32(X, S, LANES)
    width = S + 2 * H
    wide, v_shape, u_shape, v2_shape = (f32(X, width - 2 * k * R, LANES) for k in (0, 1, 2, 3))
    zb = vm(X + 2 * R, width - 2 * R, LANES)
    sw, ku = call(
        bind(open_kernel), [wide, v_shape], 0, 10, [vm(*wide.shape), zb]
    )(taps, quad_k, plane, line, own_s, even_s, odd_s, own2_s, *halos_s)
    tw, v1, v2, u, tot = call(
        bind(first_kernel), [wide, v_shape, v2_shape, slab, f32(1, LANES)], 0, 10,
        [vm(*u_shape.shape), zb, zb],
    )(taps, quad_k, own_t, even_t, odd_t, own2_t, *halos_t, sw, ku)

    def early(u, side):
        return call(
            bind(early_kernel), [v_shape, u_shape, v2_shape], 0, 6,
            [vm(X, S + H, LANES), zb, zb],
        )(taps, quad_k, u, side, sw, tw)

    rest = vm(X, H + S // 2, LANES)
    side = swap_sides(plan, u)
    other = swap_cores(plan, side)
    v3, u4, v4 = early(u, side)
    v3, _, v4, u = call(
        bind(late_kernel), [v_shape, u_shape, v2_shape, slab], 0, 9, [rest, zb, zb],
        aliases={6: 0, 7: 1, 8: 2},
    )(taps, quad_k, u, other, sw, tw, v3, u4, v4)
    side = swap_sides(plan, u)
    (gaps,) = call(bind(gaps_kernel), [f32(1, LANES)], 0, 6)(tot, tw, v1, v2, v3, v4)
    side, gaps = lax.optimization_barrier((side, gaps))
    other = swap_cores(plan, side)
    v5, u6, v6 = early(u, side)
    *_, chunks = call(
        bind(last_kernel), [v_shape, u_shape, v2_shape, f32(2 * Pn * (3 * S // 2 + 1), LANES)], 0, 14,
        [vm(X, S, LANES), zb, zb, vm(X + 2 * R, S // 2, LANES), vm(3, X + 2 * plan.Q, S // 2, LANES)],
        aliases={11: 0, 12: 1, 13: 2},
    )(taps, quad_k, quad_g, quad_s, u, other, sw, tw, v4, gaps, tot, v5, u6, v6)
    spread = trade_chunks(chunks, AXES)
    data = vm(Z, 3 * LANES)
    (send,) = call(bind(away_kernel), [f32(3, LANES, LANES)], 0, 3, [data])(high, low, spread)
    half = (3, plan.gs, plan.by, LANES)
    recv = swap_cores(plan, send.reshape(half))
    whole = f32(3, plan.bx, plan.by, LANES)
    mismatch, displacement = call(
        bind(home_kernel), [f32(ITERS), whole], 0, 3, [data, vm(*half), pltpu.SemaphoreType.DMA((3,))],
        smem_out=1, any_out=1,
    )(high, low, spread)
    (displacement,) = call(
        bind(place_kernel), [whole], 0, 1, [pltpu.SemaphoreType.DMA((3,))], n_any=1, any_out=1,
        aliases={1: 0},
    )(recv, displacement)
    return displacement, mismatch


def shards(sizes, source, target, kernel_half, smooth_half):
    plan = Plan(sizes, *source.shape, kernel_half.shape[0] - 1, smooth_half.shape[0] - 1)
    if plan.fits():
        return slab_shards(plan, source, target, kernel_half, smooth_half)
    return block_shards(source, target, kernel_half, smooth_half)


def solution(mesh):
    in_specs = (P("gx", "gy", "gz"), P("gx", "gy", "gz"), P(), P())
    out_specs = (P(None, "gx", "gy", "gz"), P())
    body = functools.partial(shards, dict(mesh.shape))
    return jax.shard_map(body, mesh=mesh, in_specs=in_specs, out_specs=out_specs, check_vma=False)
```

```python
import functools

import jax
import jax.numpy as jnp
from jax import lax
from jax.experimental import pallas as pl
from jax.experimental.pallas import tpu as pltpu
from jax.sharding import PartitionSpec as P


ITERS = 6
LANES = 128
AXES = ("gx", "gy", "gz")


def padded_2(block, sides, width):
    for axis, dim in sides:
        count = lax.axis_size(axis)
        forward = [(i, i + 1) for i in range(count - 1)]
        backward = [(target, source) for source, target in forward]
        low = lax.ppermute(
            lax.slice_in_dim(block, block.shape[dim] - width, None, axis=dim), axis, forward
        )
        high = lax.ppermute(lax.slice_in_dim(block, 0, width, axis=dim), axis, backward)
        block = jnp.concatenate([low, block, high], axis=dim)
    return block


def full_taps(half):
    return jnp.concatenate([half[:0:-1], half])


def along(padded, taps, axis, count):
    width = taps.shape[0]
    total = taps[0] * lax.slice_in_dim(padded, 0, count, axis=axis)
    for j in range(1, width):
        total = total + taps[j] * lax.slice_in_dim(padded, j, j + count, axis=axis)
    return total


def three_passes(padded, taps, size_x, size_y, size_z):
    padded = along(padded, taps, 0, size_x)
    padded = along(padded, taps, 1, size_y)
    return along(padded, taps, 2, size_z)


def block_shards(source, target, kernel_half, smooth_half):
    kern = full_taps(kernel_half)
    radius = kernel_half.shape[0] - 1
    reach = smooth_half.shape[0] - 1
    offsets = jnp.arange(-radius, radius + 1).astype(jnp.float32)
    slope = offsets * kern
    norm_total = smooth_half[0] + 2.0 * jnp.sum(smooth_half[1:])
    smooth = full_taps(smooth_half) / norm_total
    size_x, size_y, size_z = source.shape
    cells = float(source.size * lax.axis_size("gx") * lax.axis_size("gy") * lax.axis_size("gz"))
    totals = lax.psum((jnp.sum(source), jnp.sum(target)), AXES)
    first = source * (cells / totals[0])
    second = target * (cells / totals[1])
    first_wide = padded_2(first, (("gx", 0), ("gy", 1), ("gz", 2)), radius)
    scaling_v = jnp.ones_like(source)
    errors = []
    for _ in range(ITERS):
        padded = padded_2(scaling_v, (("gx", 0), ("gy", 1), ("gz", 2)), 2 * radius)
        kv_wide = three_passes(
            padded, kern, size_x + 2 * radius, size_y + 2 * radius, size_z + 2 * radius
        )
        u_wide = first_wide / kv_wide
        ku = three_passes(u_wide, kern, size_x, size_y, size_z)
        local_err = jnp.sum(jnp.abs(scaling_v * ku - second))
        errors.append(lax.psum(local_err, AXES) / cells)
        scaling_v = second / ku
    mismatch = jnp.stack(errors)
    padded = padded_2(scaling_v, (("gx", 0), ("gy", 1), ("gz", 2)), radius)
    pass_k = along(padded, kern, 0, size_x)
    pass_g = along(padded, slope, 0, size_x)
    kk = along(pass_k, kern, 1, size_y)
    kg = along(pass_k, slope, 1, size_y)
    gk = along(pass_g, kern, 1, size_y)
    kvol = along(kk, kern, 2, size_z)
    znum = along(kk, slope, 2, size_z)
    ynum = along(kg, kern, 2, size_z)
    xnum = along(gk, kern, 2, size_z)
    raw = jnp.stack([xnum, ynum, znum]) / kvol
    padded = padded_2(raw, (("gx", 1), ("gy", 2), ("gz", 3)), reach)
    padded = along(padded, smooth, 1, size_x)
    padded = along(padded, smooth, 2, size_y)
    displacement = along(padded, smooth, 3, size_z)
    return (displacement, mismatch)


class Plan:
    def __init__(self, mesh, bx, by, bz, radius, reach):
        self.nx, self.ny, self.nc = mesh["gx"], mesh["gy"], mesh["gz"]
        self.bx, self.by, self.bz = bx, by, bz
        self.R, self.Q = radius, reach
        self.P = self.nx * self.ny
        self.X, self.Y, self.Z = bx * self.nx, by * self.ny, bz * self.nc
        self.S = self.Z // self.P
        self.H = 4 * radius
        self.gs = LANES // by if by <= LANES else 0
        self.XH = self.X // 2
        self.cells = float(self.X * self.Y * self.Z)

    def fits(self):
        return (
            self.nc == 2
            and self.ny >= 2
            and self.ny & (self.ny - 1) == 0
            and self.nx >= 2
            and self.bz == LANES
            and self.Y == LANES
            and self.gs == self.ny
            and self.bx == 2 * self.gs
            and self.Z == self.P * self.S
            and self.S == self.H
            and self.S % 16 == 0
            and self.R % 4 == 0
            and ITERS == 6
        )

    def spot(self, at):
        at %= self.P
        col, q = divmod(at, self.nx)
        return (q if col % 2 == 0 else self.nx - 1 - q), col ^ (col >> 1)

    def chip(self, at):
        i, j = self.spot(at)
        return i * self.ny + j

    def device(self, at, core):
        return self.chip(at) * self.nc + core


def swap_cores(plan, value):
    pairs = [(plan.device(at, c), plan.device(at, 1 - c)) for at in range(plan.P) for c in range(2)]
    return lax.ppermute(value, AXES, pairs)


def swap_even(plan, value):
    pairs = [(plan.device(at, c), plan.device(at ^ 1, c)) for at in range(plan.P) for c in range(2)]
    return lax.ppermute(value, AXES, pairs)


def swap_odd(plan, value):
    pairs = [
        (plan.device(at, c), plan.device(((at + 1) ^ 1) - 1, c))
        for at in range(plan.P)
        for c in range(2)
    ]
    return lax.ppermute(value, AXES, pairs)


def swap_sides(plan, value):
    pairs = [(plan.device(at, 0), plan.device(at - 1, 1)) for at in range(plan.P)]
    pairs += [(plan.device(at, 1), plan.device(at + 1, 0)) for at in range(plan.P)]
    return lax.ppermute(value, AXES, pairs)


def trade_chunks(value, axes):
    rows, lanes = value.shape
    out = lax.all_to_all(value.reshape(rows, 1, lanes), axes, 0, 0, tiled=True)
    return out.reshape(rows, lanes)


def place_of(plan):
    i, j = lax.axis_index("gx"), lax.axis_index("gy")
    at = jnp.int32(0)
    for place in range(plan.P):
        a, b = plan.spot(place)
        at = at + jnp.where((i == a) & (j == b), place, 0)
    return at.astype(jnp.int32)


def call(kernel, out_shape, n_smem, n_vmem, scratch=(), smem_out=0, n_any=0, any_out=0, aliases=None):
    vm, sm = pl.BlockSpec(memory_space=pltpu.VMEM), pl.BlockSpec(memory_space=pltpu.SMEM)
    hbm = pl.BlockSpec(memory_space=pltpu.HBM)
    out_specs = [vm] * (len(out_shape) - smem_out - any_out) + [sm] * smem_out + [hbm] * any_out
    return pl.pallas_call(
        kernel,
        out_shape=out_shape,
        in_specs=[sm] * n_smem + [vm] * n_vmem + [hbm] * n_any,
        out_specs=out_specs,
        scratch_shapes=list(scratch),
        input_output_aliases=aliases or {},
        compiler_params=pltpu.CompilerParams(vmem_limit_bytes=48 << 20),
    )


def f32(*shape):
    return jax.ShapeDtypeStruct(shape, jnp.float32)


def turn_groups(plan, parts):
    n, w = plan.gs, plan.by
    group = lax.broadcasted_iota(jnp.int32, parts[0].shape, 1) // w
    outs = []
    for a in range(n):
        total = parts[a]
        for b in range(n):
            if b != a:
                moved = pltpu.roll(parts[b], (w * (b - a)) % LANES, 1)
                total = jnp.where(group == b, moved, total)
        outs.append(total)
    return outs


def pack_kernel(plan, src_hbm, tgt_hbm, keep_ref, stat_ref, src_ref, tgt_ref, sems):
    c = lax.axis_index("gz")
    copies = [
        pltpu.make_async_copy(src_hbm, src_ref, sems.at[0]),
        pltpu.make_async_copy(tgt_hbm, tgt_ref, sems.at[1]),
    ]
    for copy in copies:
        copy.start()
    sums = []
    for st, ref in enumerate((src_ref, tgt_ref)):
        copies[st].wait()
        keep_ref[st] = ref[pl.ds(plan.gs * c, plan.gs)].reshape(LANES, LANES).T
        row = jnp.sum(ref[...].reshape(plan.bx * plan.by, LANES), axis=0, keepdims=True)
        sums.append(row + pltpu.roll(row, LANES // 2, 1))
    stat_ref[...] = jnp.where(lane_at() < LANES // 2, *sums)


def lane_at():
    return lax.broadcasted_iota(jnp.int32, (1, LANES), 1)


def chunk_kernel(plan, keep_ref, src_ref, tgt_ref, stat_ref, out_ref, recv_ref):
    c = lax.axis_index("gz")
    half, S = plan.P // 2, plan.S
    size = 2 * S + 1
    for st, ref in enumerate((src_ref, tgt_ref)):
        recv_ref[st] = ref[pl.ds(plan.gs * c, plan.gs)].reshape(LANES, LANES).T

    def write(low_ref, high_ref):
        stat = stat_ref[...]
        for place in range(plan.P):
            ref, part = (low_ref, place) if place < half else (high_ref, place - half)
            base = size * plan.chip(place)
            for st in range(2):
                out_ref[base + S * st : base + S * st + S, :] = ref[st, S * part : S * part + S, :]
            out_ref[base + 2 * S : base + size, :] = stat

    pl.when(c == 0)(lambda: write(keep_ref, recv_ref))
    pl.when(c == 1)(lambda: write(recv_ref, keep_ref))


def unpack_kernel(plan, st, in_ref, out_ref):
    S, gs, XH = plan.S, plan.gs, plan.XH
    size = 2 * S + 1
    for i in range(plan.nx):
        bases = [size * (i * plan.ny + j) + S * st for j in range(plan.ny)]
        parts = [in_ref[base : base + S, :] for base in bases]
        for xx, value in enumerate(turn_groups(plan, parts)):
            out_ref[i * gs + xx] = value
    if st:
        out_ref[XH] = jnp.zeros((S, LANES), jnp.float32)
        out_ref[XH, :1, :] = sum_rows(in_ref, size)


def sum_rows(ref, size):
    total = ref[size - 1 : size, :]
    for p in range(1, ref.shape[0] // size):
        total = total + ref[size * p + size - 1 : size * p + size, :]
    return total


def banded(taps, n, odd):
    row = lax.broadcasted_iota(jnp.int32, (n, n), 0)
    col = lax.broadcasted_iota(jnp.int32, (n, n), 1)
    gap = row - col
    total = jnp.zeros((n, n), jnp.float32)
    for d, tap in enumerate(taps):
        if odd:
            if d:
                total = jnp.where(gap == d, d * tap, total)
                total = jnp.where(gap == -d, -(d * tap), total)
        else:
            total = jnp.where(jnp.abs(gap) == d, tap, total)
    return total


def halves(value):
    high = value.astype(jnp.bfloat16)
    return high, (value - high.astype(jnp.float32)).astype(jnp.bfloat16)


def quad(matrix):
    high, low = halves(matrix)
    row = jnp.concatenate([high, low], axis=1)
    return jnp.concatenate([row, row], axis=0)


def lanes_times(value, quad_ref):
    high, low = halves(value)
    both = jnp.concatenate([high, low], axis=1)
    out = jnp.dot(both, quad_ref[...], preferred_element_type=jnp.float32)
    return out[:, :LANES] + out[:, LANES:]


def even_sum(load, taps, mid):
    total = taps[0] * load(mid)
    for d in range(1, len(taps)):
        total = total + taps[d] * (load(mid - d) + load(mid + d))
    return total


def unit_sum(load, taps, mid):
    total = load(mid)
    for d in range(1, len(taps)):
        total = total + taps[d] * (load(mid - d) + load(mid + d))
    return total


def odd_sum(load, taps, mid):
    total = taps[1] * (load(mid + 1) - load(mid - 1))
    for d in range(2, len(taps)):
        total = total + (d * taps[d]) * (load(mid + d) - load(mid - d))
    return total


MANY = 16


def run_passes(plan, passes):
    chunks = range(0, plan.X, MANY)
    for base in chunks:
        passes[0][0](base)
    for (_, matmul_part, emit_part), after in zip(passes, passes[1:] + [None]):
        done = None

        def close(pair):
            emit_part(*pair)
            if after is not None:
                after[0](pair[0])

        for base in chunks:
            out = matmul_part(base)
            if done is not None:
                close(done)
            done = (base, out)
        close(done)


def kernel_pass(plan, taps, quad_ref, in_ref, zb_ref, rows, emit):
    R = plan.R

    def z_part(base):
        for x in range(base, base + MANY):
            zb_ref[R + x, :rows, :] = unit_sum(lambda j: in_ref[x, j : j + rows, :], taps, R)

    def matmul_part(base):
        parts = [
            unit_sum(lambda j: zb_ref[base + q + j, :rows, :], taps, R) for q in range(MANY)
        ]
        return lanes_times(jnp.concatenate(parts, axis=0), quad_ref)

    def emit_part(base, out):
        for q in range(MANY):
            emit(base + q, out[q * rows : (q + 1) * rows])

    return z_part, matmul_part, emit_part


def inside(plan, at, off, rows):
    z = lax.broadcasted_iota(jnp.int32, (rows, LANES), 0) + (at * plan.S - plan.H + off)
    return (z >= 0) & (z < plan.Z)


def scale_step(plan, at, taps, quad_ref, zb, src, top, dst, over, off, start, rows):
    mask = inside(plan, at, off + start, rows)
    src = src.at[:, pl.ds(top, rows + 2 * plan.R), :]
    lead = (off + 7) // 8 * 8
    over = over.at[:, pl.ds(start, rows + lead), :]

    def emit(x, value):
        dst[x, pl.ds(start, rows), :] = jnp.where(mask, over[x, off : off + rows, :] / value, 0.0)

    return kernel_pass(plan, taps, quad_ref, src, zb, rows, emit)


def clear_edges(ref, edge, size):
    blank = jnp.zeros((edge,) + ref.shape[1:], jnp.float32)
    ref[:edge] = blank
    ref[edge + size :] = blank


def prep_kernel(plan, k_ref, s_ref, own, taps_ref, quad_ref, slope_ref, smooth_ref, high_ref,
                low_ref, plane_ref, line_ref):
    del own
    R, Q = plan.R, plan.Q
    taps = [jnp.zeros((1, LANES), jnp.float32) + k_ref[d] for d in range(R + 1)]
    taps = [jnp.ones((1, LANES), jnp.float32)] + [tap / taps[0] for tap in taps[1:]]
    stap = smooth_taps(s_ref, Q)
    for d in range(R + 1):
        taps_ref[d] = jnp.broadcast_to(taps[d], (8, LANES))
    for d in range(Q + 1):
        taps_ref[R + 1 + d] = jnp.broadcast_to(stap[d], (8, LANES))
    quad_ref[...] = quad(banded(taps, LANES, False))
    slope_ref[...] = quad(banded(taps, LANES, True))
    smooth_ref[...] = quad(banded(stap, LANES, False))
    wide = [jnp.concatenate([t] * (plan.Z // LANES), axis=1) for t in stap]
    high_ref[...], low_ref[...] = halves(banded(wide, plan.Z, False))


    def reach_sum(shape, axis, start, size):
        place = lax.broadcasted_iota(jnp.int32, shape, axis) + start
        total = jnp.ones(shape, jnp.float32)
        for d in range(1, R + 1):
            total = total + jnp.where(place - d >= 0, taps[d], 0.0)
            total = total + jnp.where(place + d < size, taps[d], 0.0)
        return total

    at = place_of(plan)
    shape = plane_ref.shape
    over = reach_sum(shape, 0, at * plan.S - plan.H, plan.Z) * reach_sum(shape, 1, 0, plan.Y)
    plane_ref[...] = jnp.where(inside(plan, at, 0, shape[0]), 1.0 / over, 0.0)
    line_ref[...] = 1.0 / reach_sum(line_ref.shape, 0, 0, plan.X)


def kernel_taps(plan, taps_ref):
    return [taps_ref[d, :1, :] for d in range(plan.R + 1)]


def gaps_of(plan, tot, tw, olds, news):
    S = plan.S
    half = S // 2
    mine = pl.multiple_of(half * lax.axis_index("gz"), 8)
    first_half = lane_at() < LANES // 2
    both = tot[:1, :]
    sum_s = jnp.sum(jnp.where(first_half, both, 0.0), axis=1, keepdims=True)
    sum_t = jnp.sum(jnp.where(first_half, 0.0, both), axis=1, keepdims=True)
    scale_s = plan.cells / jnp.broadcast_to(sum_s, (1, LANES))
    scale_t = plan.cells / jnp.broadcast_to(sum_t, (1, LANES))

    def mid(ref):
        edge = (ref.shape[1] - S) // 2
        ref = ref.at[:, pl.ds(mine, ref.shape[1] - half), :]
        return lambda x: ref[x, edge : edge + half, :]

    t_at = mid(tw)
    olds = [old if old is None else mid(old) for old in olds]
    news = [mid(new) for new in news]

    def p_step(x, carry):
        t = t_at(x)
        want = scale_t * t
        have = scale_s * t
        result = []
        for part, old, new in zip(carry, olds, news):
            value = have / new(x)
            if old is not None:
                value = value * old(x)
            gap = jnp.abs(value - want)
            for r in range(0, half, 8):
                part = part + gap[r : r + 8]
            result.append(part)
        return tuple(result)

    zero = jnp.zeros((8, LANES), jnp.float32)
    gaps = lax.fori_loop(0, plan.X, p_step, (zero,) * len(news), unroll=4)
    return [jnp.sum(g, keepdims=True) for g in gaps]


def in_lanes(values, first=0):
    row = jnp.zeros((1, LANES), jnp.float32)
    for t, value in enumerate(values):
        row = jnp.where(lane_at() == first + t, value, row)
    return row


def gaps_kernel(plan, tot, tw, v1, v2, v3, v4, out_ref):
    out_ref[...] = in_lanes(gaps_of(plan, tot, tw, (None, v1, v2, v3), (v1, v2, v3, v4)))


def spread_halves(plan, at, own, even, odd, own2, even2, odd2, win):
    S, H, gs = plan.S, plan.H, plan.gs
    c = lax.axis_index("gz")

    def spread(low, high):
        for k, (mid, core) in enumerate(((own, c), (own2, 1 - c))):
            for i in range(plan.nx):
                x, here = plan.bx * i + gs * core, pl.ds(i * gs, gs)
                win[pl.ds(x, gs), H : H + S, :] = mid[here]
                win[pl.ds(x, gs), :H, :] = low[k][here]
                win[pl.ds(x, gs), H + S :, :] = high[k][here]

    pl.when(at % 2 == 0)(lambda: spread((odd, odd2), (even, even2)))
    pl.when(at % 2 == 1)(lambda: spread((even, even2), (odd, odd2)))


def open_kernel(plan, taps_ref, quad_ref, plane_ref, line_ref, own, even, odd, own2, even2, odd2,
                sw, ku, u, zb):
    R = plan.R
    at = place_of(plan)
    taps = kernel_taps(plan, taps_ref)
    clear_edges(zb, R, plan.X)
    spread_halves(plan, at, own, even, odd, own2, even2, odd2, sw)
    for x in range(plan.X):
        u[x] = sw[x] * (plane_ref[...] * line_ref[x : x + 1, :])

    def emit(x, value):
        ku[x] = value

    rows = ku.shape[1]
    run_passes(plan, [kernel_pass(plan, taps, quad_ref, u, zb, rows, emit)])


def first_kernel(plan, taps_ref, quad_ref, own, even, odd, own2, even2, odd2, sw, ku,
                 tw, v, v2, u_out, tot, u, zb, zc):
    R, S, H, X, XH = plan.R, plan.S, plan.H, plan.X, plan.XH
    at = place_of(plan)
    taps = kernel_taps(plan, taps_ref)
    clear_edges(zb, R, X)
    clear_edges(zc, R, X)
    spread_halves(plan, at, own, even, odd, own2, even2, odd2, tw)
    tot[...] = own[XH, :1, :] + own2[XH, :1, :]
    rows = S + 2 * H - 2 * R
    mask = inside(plan, at, R, rows)

    def v_step(x, carry):
        v[x] = jnp.where(mask, tw[x, R : R + rows, :] / ku[x], 0.0)
        return carry

    lax.fori_loop(0, X, v_step, 0, unroll=4)
    step = functools.partial(scale_step, plan, at, taps, quad_ref)
    run_passes(plan, [
        step(zb, v, 0, u, sw, 2 * R, 0, rows - 2 * R),
        step(zc, u, 0, v2, tw, 3 * R, 0, rows - 4 * R),
        step(zb, v2, 0, u_out, sw, 4 * R, 0, rows - 6 * R),
    ])


def early_kernel(plan, taps_ref, quad_ref, mine, side, sw, tw, v, u, v2, win, zb, zc):
    R, S, H = plan.R, plan.S, plan.H
    c = lax.axis_index("gz")
    at = place_of(plan)
    taps = kernel_taps(plan, taps_ref)
    clear_edges(zb, R, plan.X)
    clear_edges(zc, R, plan.X)
    real = jnp.where(jnp.where(c == 0, at > 0, at < plan.P - 1), 1.0, 0.0)
    win[:, pl.ds(pl.multiple_of(H * c, 8), H), :] = side[...] * real
    win[:, pl.ds(pl.multiple_of(H * (1 - c), 8), S), :] = mine[...]
    step = functools.partial(scale_step, plan, at, taps, quad_ref)
    from_ = pl.multiple_of(S * c, 8)
    run_passes(plan, [
        step(zb, win, 0, v, tw, R, from_, S + H - 2 * R),
        step(zc, v, from_, u, sw, 2 * R, from_, S + H - 4 * R),
        step(zb, u, from_, v2, tw, 3 * R, from_, S + H - 6 * R),
    ])


def late_rows(plan, at, taps, quad_ref, mine, other, sw, tw, v, u, v2, win, zb, zc):
    R, S, H = plan.R, plan.S, plan.H
    c = lax.axis_index("gz")
    real = jnp.where(jnp.where(c == 1, at > 0, at < plan.P - 1), 1.0, 0.0)
    half = S // 2

    def lay(other_at, mine_at, mine_from):
        win[:, other_at : other_at + H, :] = other[...] * real
        win[:, mine_at : mine_at + half, :] = mine[:, mine_from : mine_from + half, :]

    pl.when(c == 0)(lambda: lay(half, 0, half))
    pl.when(c == 1)(lambda: lay(0, H, 0))
    step = functools.partial(scale_step, plan, at, taps, quad_ref)
    first = pl.multiple_of((S + H - 2 * R) * (1 - c), 8)
    second = pl.multiple_of((S + H - 4 * R) * (1 - c), 8)
    third = pl.multiple_of((S + H - 6 * R) * (1 - c), 8)
    return [
        step(zb, win, 0, v, tw, R, first, S),
        step(zc, v, second, u, sw, 2 * R, second, S),
        step(zb, u, third, v2, tw, 3 * R, third, S),
    ]


def late_kernel(plan, taps_ref, quad_ref, mine, other, sw, tw, v_in, u_in, v2_in,
                v, u, v2, u_out, win, zb, zc):
    del v_in, u_in, v2_in
    R, S = plan.R, plan.S
    at = place_of(plan)
    taps = kernel_taps(plan, taps_ref)
    clear_edges(zb, R, plan.X)
    clear_edges(zc, R, plan.X)
    passes = late_rows(plan, at, taps, quad_ref, mine, other, sw, tw, v, u, v2, win, zb, zc)
    passes.append(scale_step(plan, at, taps, quad_ref, zc, v2, 0, u_out, sw, 4 * R, 0, S))
    run_passes(plan, passes)


def smooth_taps(s_ref, reach):
    total = s_ref[0]
    tail = s_ref[1]
    for d in range(2, reach + 1):
        tail = tail + s_ref[d]
    scale = 1.0 / (jnp.zeros((1, LANES), jnp.float32) + (total + 2.0 * tail))
    return [scale * s_ref[d] for d in range(reach + 1)]


def last_kernel(plan, taps_ref, quad_ref, slope_ref, smooth_ref, mine, other, sw, tw, prev,
                gaps, tot, v_in, u_in, v2_in, v, u, v2, out_ref, win, zb, zc, zg, raw):
    del v_in, u_in, v2_in
    R, S, H, X, gs, Q = plan.R, plan.S, plan.H, plan.X, plan.gs, plan.Q
    half = S // 2
    size = 3 * half + 1
    c = lax.axis_index("gz")
    at = place_of(plan)
    taps = kernel_taps(plan, taps_ref)
    stap = [taps_ref[R + 1 + d, :1, :] for d in range(Q + 1)]
    clear_edges(zb, R, X)
    clear_edges(zc, R, X)
    clear_edges(zg, R, X)
    for comp in range(3):
        clear_edges(raw.at[comp], Q, X)
    real = jnp.where(jnp.where(c == 1, at > 0, at < plan.P - 1), 1.0, 0.0)

    @pl.when(c == 0)
    def _():
        win[:, :half, :] = mine[:, half:, :]
        win[:, half:, :] = other[:, :half, :] * real

    @pl.when(c == 1)
    def _():
        win[:, :half, :] = other[:, H - half :, :] * real
        win[:, half:, :] = mine[:, :half, :]

    step = functools.partial(scale_step, plan, at, taps, quad_ref)
    own = pl.multiple_of(half * c, 8)
    first = pl.multiple_of(S + half - S * c, 8)
    second = pl.multiple_of(S - half * c, 8)
    passes = [
        step(zb, win, 0, v, tw, R, first, half),
        step(zc, v, second, u, sw, 2 * R, second, half),
        step(zb, u, half, v2, tw, 3 * R, half, half),
    ]
    near = v2.at[:, pl.ds(own, S), :]

    def z_part(base):
        for x in range(base, base + MANY):
            load = lambda j: near[x, j : j + half, :]
            zc[R + x, :half, :] = unit_sum(load, taps, R)
            zg[R + x] = odd_sum(load, taps, R)

    def matmul_part(base):
        kk, gk, kg = [], [], []
        for q in range(MANY):
            flat = lambda j: zc[base + q + j, :half, :]
            kk.append(unit_sum(flat, taps, R))
            gk.append(odd_sum(flat, taps, R))
            kg.append(unit_sum(lambda j: zg[base + q + j], taps, R))
        kk, gk, kg = (jnp.concatenate(part, axis=0) for part in (kk, gk, kg))
        nums = lanes_times(gk, quad_ref), lanes_times(kk, slope_ref), lanes_times(kg, quad_ref)
        return lanes_times(kk, quad_ref), nums

    def emit_part(base, out):
        kvol, nums = out
        for comp, num in enumerate(nums):
            value = num / kvol
            for q in range(MANY):
                raw[comp, Q + base + q] = value[q * half : (q + 1) * half]

    run_passes(plan, passes + [(z_part, matmul_part, emit_part)])

    for i in range(plan.nx):
        for comp in range(3):
            x = plan.bx * i
            parts = [even_sum(lambda j: raw[comp, x + k + j], stap, Q) for k in range(plan.bx)]
            flat = lanes_times(jnp.concatenate(parts, axis=0), smooth_ref)
            for core in range(2):
                rows = range(gs * core, gs * (core + 1))
                turned = turn_groups(plan, [flat[k * half : (k + 1) * half] for k in rows])
                for j in range(plan.ny):
                    base = size * ((i * plan.ny + j) * 2 + core) + comp * half
                    out_ref[base : base + half, :] = turned[j]

    rows = gaps_of(plan, tot, tw, (prev, v), (v, v2))
    stat = gaps[...] + in_lanes(rows, ITERS - 2)
    for p in range(2 * plan.P):
        out_ref[size * (p + 1) - 1 : size * (p + 1), :] = stat


def smooth_z(core, high_ref, low_ref, d_high, d_low, emit):
    rows = pl.ds(pl.multiple_of(core * LANES, LANES), LANES)
    m_high, m_low = high_ref[rows, :], low_ref[rows, :]
    dot = functools.partial(jnp.dot, preferred_element_type=jnp.float32)
    for comp in range(3):
        lanes = slice(comp * LANES, (comp + 1) * LANES)
        high, low = d_high[:, lanes], d_low[:, lanes]
        emit(comp, (dot(m_high, high) + (dot(m_high, low) + dot(m_low, high))).T)


def away_kernel(plan, high_ref, low_ref, in_ref, send_ref, d_high, d_low):
    half = plan.S // 2
    size = 3 * half + 1
    for comp in range(3):
        for place in range(plan.P):
            bases = [size * plan.device(place, core) + comp * half for core in range(2)]
            both = jnp.concatenate([in_ref[base : base + half, :] for base in bases], axis=0)
            here = slice(plan.S * place, plan.S * (place + 1))
            lanes = slice(comp * LANES, (comp + 1) * LANES)
            d_high[here, lanes], d_low[here, lanes] = halves(both)

    def emit(comp, value):
        send_ref[comp] = value

    smooth_z(1 - lax.axis_index("gz"), high_ref, low_ref, d_high, d_low, emit)


def home_kernel(plan, high_ref, low_ref, d_high, d_low, in_ref, mis_ref, out_hbm, keep, sems):
    c = lax.axis_index("gz")
    gs = plan.gs
    copies = [
        pltpu.make_async_copy(keep.at[k], out_hbm.at[k, pl.ds(gs * c, gs)], sems.at[k])
        for k in range(3)
    ]

    def emit(comp, value):
        keep[comp] = value.reshape(gs, plan.by, LANES)
        copies[comp].start()

    smooth_z(c, high_ref, low_ref, d_high, d_low, emit)
    gone = sum_rows(in_ref, 3 * plan.S // 2 + 1) / plan.cells
    for t in range(ITERS):
        mis_ref[t] = jnp.sum(jnp.where(lane_at() == t, gone, 0.0))
    for copy in copies:
        copy.wait()


def place_kernel(plan, recv_ref, in_hbm, out_hbm, sems):
    del in_hbm
    at = pl.ds(plan.gs * (1 - lax.axis_index("gz")), plan.gs)
    copies = [
        pltpu.make_async_copy(recv_ref.at[k], out_hbm.at[k, at], sems.at[k]) for k in range(3)
    ]
    for copy in copies:
        copy.start()
    for copy in copies:
        copy.wait()


def slab_shards(plan, source, target, kernel_half, smooth_half):
    R, S, H, X, XH, Pn, Z = plan.R, plan.S, plan.H, plan.X, plan.XH, plan.P, plan.Z
    bind = lambda kernel, *more: functools.partial(kernel, plan, *more)
    half = f32(2, LANES, LANES)
    vm = lambda *shape: pltpu.VMEM(shape, jnp.float32)
    keep, stat = call(
        bind(pack_kernel), [half, f32(1, LANES)], 0, 0,
        [vm(*source.shape), vm(*source.shape), pltpu.SemaphoreType.DMA((2,))], n_any=2,
    )(*(pltpu.with_memory_space_constraint(a, pltpu.HBM) for a in (source, target)))
    (chunks,) = call(
        bind(chunk_kernel), [f32(Pn * (2 * S + 1), LANES)], 0, 4, [vm(*half.shape)]
    )(keep, swap_cores(plan, source), swap_cores(plan, target), stat)
    spread = trade_chunks(chunks, ("gx", "gy"))
    unpack = lambda st: call(bind(unpack_kernel, st), [f32(XH + st, S, LANES)], 0, 1)(spread)[0]
    own_s = unpack(0)
    own_t = unpack(1)
    square = jax.ShapeDtypeStruct((2 * LANES, 2 * LANES), jnp.bfloat16)
    table = jax.ShapeDtypeStruct((Z, Z), jnp.bfloat16)
    taps, quad_k, quad_g, quad_s, high, low, plane, line = call(
        bind(prep_kernel),
        [f32(R + plan.Q + 2, 8, LANES), square, square, square, table, table,
         f32(S + 2 * H, LANES), f32(X, LANES)],
        2, 0, n_any=1,
    )(kernel_half, smooth_half, own_s)
    even_s, odd_s = swap_even(plan, own_s), swap_odd(plan, own_s)
    even_t, odd_t = swap_even(plan, own_t), swap_odd(plan, own_t)
    own2_s, own2_t = swap_cores(plan, own_s), swap_cores(plan, own_t)
    even_s, odd_s, taps = lax.optimization_barrier((even_s, odd_s, taps))
    halos_s = swap_cores(plan, even_s), swap_cores(plan, odd_s)
    even_t, odd_t, own2_s = lax.optimization_barrier((even_t, odd_t, own2_s))
    halos_t = swap_cores(plan, even_t), swap_cores(plan, odd_t)

    slab = f32(X, S, LANES)
    width = S + 2 * H
    wide, v_shape, u_shape, v2_shape = (f32(X, width - 2 * k * R, LANES) for k in (0, 1, 2, 3))
    zb = vm(X + 2 * R, width - 2 * R, LANES)
    sw, ku = call(
        bind(open_kernel), [wide, v_shape], 0, 10, [vm(*wide.shape), zb]
    )(taps, quad_k, plane, line, own_s, even_s, odd_s, own2_s, *halos_s)
    tw, v1, v2, u, tot = call(
        bind(first_kernel), [wide, v_shape, v2_shape, slab, f32(1, LANES)], 0, 10,
        [vm(*u_shape.shape), zb, zb],
    )(taps, quad_k, own_t, even_t, odd_t, own2_t, *halos_t, sw, ku)

    def early(u, side):
        return call(
            bind(early_kernel), [v_shape, u_shape, v2_shape], 0, 6,
            [vm(X, S + H, LANES), zb, zb],
        )(taps, quad_k, u, side, sw, tw)

    rest = vm(X, H + S // 2, LANES)
    side = swap_sides(plan, u)
    other = swap_cores(plan, side)
    v3, u4, v4 = early(u, side)
    v3, _, v4, u = call(
        bind(late_kernel), [v_shape, u_shape, v2_shape, slab], 0, 9, [rest, zb, zb],
        aliases={6: 0, 7: 1, 8: 2},
    )(taps, quad_k, u, other, sw, tw, v3, u4, v4)
    side = swap_sides(plan, u)
    (gaps,) = call(bind(gaps_kernel), [f32(1, LANES)], 0, 6)(tot, tw, v1, v2, v3, v4)
    side, gaps = lax.optimization_barrier((side, gaps))
    other = swap_cores(plan, side)
    v5, u6, v6 = early(u, side)
    *_, chunks = call(
        bind(last_kernel), [v_shape, u_shape, v2_shape, f32(2 * Pn * (3 * S // 2 + 1), LANES)], 0, 14,
        [vm(X, S, LANES), zb, zb, vm(X + 2 * R, S // 2, LANES), vm(3, X + 2 * plan.Q, S // 2, LANES)],
        aliases={11: 0, 12: 1, 13: 2},
    )(taps, quad_k, quad_g, quad_s, u, other, sw, tw, v4, gaps, tot, v5, u6, v6)
    spread = trade_chunks(chunks, AXES)
    split = jax.ShapeDtypeStruct((Z, 3 * LANES), jnp.bfloat16)
    send, *splits = call(
        bind(away_kernel), [f32(3, LANES, LANES), split, split], 0, 3
    )(high, low, spread)
    half = (3, plan.gs, plan.by, LANES)
    recv = swap_cores(plan, send.reshape(half))
    whole = f32(3, plan.bx, plan.by, LANES)
    mismatch, displacement = call(
        bind(home_kernel), [f32(ITERS), whole], 0, 5, [vm(*half), pltpu.SemaphoreType.DMA((3,))],
        smem_out=1, any_out=1,
    )(high, low, *splits, spread)
    (displacement,) = call(
        bind(place_kernel), [whole], 0, 1, [pltpu.SemaphoreType.DMA((3,))], n_any=1, any_out=1,
        aliases={1: 0},
    )(recv, displacement)
    return displacement, mismatch


def shards(sizes, source, target, kernel_half, smooth_half):
    plan = Plan(sizes, *source.shape, kernel_half.shape[0] - 1, smooth_half.shape[0] - 1)
    if plan.fits():
        return slab_shards(plan, source, target, kernel_half, smooth_half)
    return block_shards(source, target, kernel_half, smooth_half)


def solution(mesh):
    in_specs = (P("gx", "gy", "gz"), P("gx", "gy", "gz"), P(), P())
    out_specs = (P(None, "gx", "gy", "gz"), P())
    body = functools.partial(shards, dict(mesh.shape))
    return jax.shard_map(body, mesh=mesh, in_specs=in_specs, out_specs=out_specs, check_vma=False)
```

```python
import functools

import jax
import jax.numpy as jnp
from jax import lax
from jax.experimental import pallas as pl
from jax.experimental.pallas import tpu as pltpu
from jax.sharding import PartitionSpec as P


ITERS = 6
LANES = 128
AXES = ("gx", "gy", "gz")


def padded_2(block, sides, width):
    for axis, dim in sides:
        count = lax.axis_size(axis)
        forward = [(i, i + 1) for i in range(count - 1)]
        backward = [(target, source) for source, target in forward]
        low = lax.ppermute(
            lax.slice_in_dim(block, block.shape[dim] - width, None, axis=dim), axis, forward
        )
        high = lax.ppermute(lax.slice_in_dim(block, 0, width, axis=dim), axis, backward)
        block = jnp.concatenate([low, block, high], axis=dim)
    return block


def full_taps(half):
    return jnp.concatenate([half[:0:-1], half])


def along(padded, taps, axis, count):
    width = taps.shape[0]
    total = taps[0] * lax.slice_in_dim(padded, 0, count, axis=axis)
    for j in range(1, width):
        total = total + taps[j] * lax.slice_in_dim(padded, j, j + count, axis=axis)
    return total


def three_passes(padded, taps, size_x, size_y, size_z):
    padded = along(padded, taps, 0, size_x)
    padded = along(padded, taps, 1, size_y)
    return along(padded, taps, 2, size_z)


def block_shards(source, target, kernel_half, smooth_half):
    kern = full_taps(kernel_half)
    radius = kernel_half.shape[0] - 1
    reach = smooth_half.shape[0] - 1
    offsets = jnp.arange(-radius, radius + 1).astype(jnp.float32)
    slope = offsets * kern
    norm_total = smooth_half[0] + 2.0 * jnp.sum(smooth_half[1:])
    smooth = full_taps(smooth_half) / norm_total
    size_x, size_y, size_z = source.shape
    cells = float(source.size * lax.axis_size("gx") * lax.axis_size("gy") * lax.axis_size("gz"))
    totals = lax.psum((jnp.sum(source), jnp.sum(target)), AXES)
    first = source * (cells / totals[0])
    second = target * (cells / totals[1])
    first_wide = padded_2(first, (("gx", 0), ("gy", 1), ("gz", 2)), radius)
    scaling_v = jnp.ones_like(source)
    errors = []
    for _ in range(ITERS):
        padded = padded_2(scaling_v, (("gx", 0), ("gy", 1), ("gz", 2)), 2 * radius)
        kv_wide = three_passes(
            padded, kern, size_x + 2 * radius, size_y + 2 * radius, size_z + 2 * radius
        )
        u_wide = first_wide / kv_wide
        ku = three_passes(u_wide, kern, size_x, size_y, size_z)
        local_err = jnp.sum(jnp.abs(scaling_v * ku - second))
        errors.append(lax.psum(local_err, AXES) / cells)
        scaling_v = second / ku
    mismatch = jnp.stack(errors)
    padded = padded_2(scaling_v, (("gx", 0), ("gy", 1), ("gz", 2)), radius)
    pass_k = along(padded, kern, 0, size_x)
    pass_g = along(padded, slope, 0, size_x)
    kk = along(pass_k, kern, 1, size_y)
    kg = along(pass_k, slope, 1, size_y)
    gk = along(pass_g, kern, 1, size_y)
    kvol = along(kk, kern, 2, size_z)
    znum = along(kk, slope, 2, size_z)
    ynum = along(kg, kern, 2, size_z)
    xnum = along(gk, kern, 2, size_z)
    raw = jnp.stack([xnum, ynum, znum]) / kvol
    padded = padded_2(raw, (("gx", 1), ("gy", 2), ("gz", 3)), reach)
    padded = along(padded, smooth, 1, size_x)
    padded = along(padded, smooth, 2, size_y)
    displacement = along(padded, smooth, 3, size_z)
    return (displacement, mismatch)


class Plan:
    def __init__(self, mesh, bx, by, bz, radius, reach):
        self.nx, self.ny, self.nc = mesh["gx"], mesh["gy"], mesh["gz"]
        self.bx, self.by, self.bz = bx, by, bz
        self.R, self.Q = radius, reach
        self.P = self.nx * self.ny
        self.X, self.Y, self.Z = bx * self.nx, by * self.ny, bz * self.nc
        self.S = self.Z // self.P
        self.H = 4 * radius
        self.gs = LANES // by if by <= LANES else 0
        self.XH = self.X // 2
        self.cells = float(self.X * self.Y * self.Z)

    def fits(self):
        return (
            self.nc == 2
            and self.ny >= 2
            and self.ny & (self.ny - 1) == 0
            and self.nx >= 2
            and self.bz == LANES
            and self.Y == LANES
            and self.gs == self.ny
            and self.bx == 2 * self.gs
            and self.Z == self.P * self.S
            and self.S == self.H
            and self.S % 16 == 0
            and self.R % 4 == 0
            and ITERS == 6
        )

    def spot(self, at):
        at %= self.P
        col, q = divmod(at, self.nx)
        return (q if col % 2 == 0 else self.nx - 1 - q), col ^ (col >> 1)

    def chip(self, at):
        i, j = self.spot(at)
        return i * self.ny + j

    def device(self, at, core):
        return self.chip(at) * self.nc + core


def swap_cores(plan, value):
    pairs = [(plan.device(at, c), plan.device(at, 1 - c)) for at in range(plan.P) for c in range(2)]
    return lax.ppermute(value, AXES, pairs)


def swap_even(plan, value):
    pairs = [(plan.device(at, c), plan.device(at ^ 1, c)) for at in range(plan.P) for c in range(2)]
    return lax.ppermute(value, AXES, pairs)


def swap_odd(plan, value):
    pairs = [
        (plan.device(at, c), plan.device(((at + 1) ^ 1) - 1, c))
        for at in range(plan.P)
        for c in range(2)
    ]
    return lax.ppermute(value, AXES, pairs)


def swap_sides(plan, value):
    pairs = [(plan.device(at, 0), plan.device(at - 1, 1)) for at in range(plan.P)]
    pairs += [(plan.device(at, 1), plan.device(at + 1, 0)) for at in range(plan.P)]
    return lax.ppermute(value, AXES, pairs)


def trade_chunks(value, axes):
    rows, lanes = value.shape
    out = lax.all_to_all(value.reshape(rows, 1, lanes), axes, 0, 0, tiled=True)
    return out.reshape(rows, lanes)


def place_of(plan):
    i, j = lax.axis_index("gx"), lax.axis_index("gy")
    at = jnp.int32(0)
    for place in range(plan.P):
        a, b = plan.spot(place)
        at = at + jnp.where((i == a) & (j == b), place, 0)
    return at.astype(jnp.int32)


def call(kernel, out_shape, n_smem, n_vmem, scratch=(), smem_out=0, n_any=0, any_out=0, aliases=None):
    vm, sm = pl.BlockSpec(memory_space=pltpu.VMEM), pl.BlockSpec(memory_space=pltpu.SMEM)
    hbm = pl.BlockSpec(memory_space=pltpu.HBM)
    out_specs = [vm] * (len(out_shape) - smem_out - any_out) + [sm] * smem_out + [hbm] * any_out
    return pl.pallas_call(
        kernel,
        out_shape=out_shape,
        in_specs=[sm] * n_smem + [vm] * n_vmem + [hbm] * n_any,
        out_specs=out_specs,
        scratch_shapes=list(scratch),
        input_output_aliases=aliases or {},
        compiler_params=pltpu.CompilerParams(vmem_limit_bytes=48 << 20),
    )


def f32(*shape):
    return jax.ShapeDtypeStruct(shape, jnp.float32)


def turn_groups(plan, parts):
    n, w = plan.gs, plan.by
    group = lax.broadcasted_iota(jnp.int32, parts[0].shape, 1) // w
    outs = []
    for a in range(n):
        total = parts[a]
        for b in range(n):
            if b != a:
                moved = pltpu.roll(parts[b], (w * (b - a)) % LANES, 1)
                total = jnp.where(group == b, moved, total)
        outs.append(total)
    return outs


def pack_kernel(plan, src_hbm, tgt_hbm, keep_ref, stat_ref, src_ref, tgt_ref, sems):
    c = lax.axis_index("gz")
    copies = [
        pltpu.make_async_copy(src_hbm, src_ref, sems.at[0]),
        pltpu.make_async_copy(tgt_hbm, tgt_ref, sems.at[1]),
    ]
    for copy in copies:
        copy.start()
    sums = []
    for st, ref in enumerate((src_ref, tgt_ref)):
        copies[st].wait()
        keep_ref[st] = ref[pl.ds(plan.gs * c, plan.gs)].reshape(LANES, LANES).T
        row = jnp.sum(ref[...].reshape(plan.bx * plan.by, LANES), axis=0, keepdims=True)
        sums.append(row + pltpu.roll(row, LANES // 2, 1))
    stat_ref[...] = jnp.where(lane_at() < LANES // 2, *sums)


def lane_at():
    return lax.broadcasted_iota(jnp.int32, (1, LANES), 1)


def chunk_kernel(plan, keep_ref, src_ref, tgt_ref, stat_ref, out_ref, recv_ref):
    c = lax.axis_index("gz")
    half, S = plan.P // 2, plan.S
    size = 2 * S + 1
    for st, ref in enumerate((src_ref, tgt_ref)):
        recv_ref[st] = ref[pl.ds(plan.gs * c, plan.gs)].reshape(LANES, LANES).T

    def write(low_ref, high_ref):
        stat = stat_ref[...]
        for place in range(plan.P):
            ref, part = (low_ref, place) if place < half else (high_ref, place - half)
            base = size * plan.chip(place)
            for st in range(2):
                out_ref[base + S * st : base + S * st + S, :] = ref[st, S * part : S * part + S, :]
            out_ref[base + 2 * S : base + size, :] = stat

    pl.when(c == 0)(lambda: write(keep_ref, recv_ref))
    pl.when(c == 1)(lambda: write(recv_ref, keep_ref))


def unpack_kernel(plan, st, in_ref, out_ref):
    S, gs, XH = plan.S, plan.gs, plan.XH
    size = 2 * S + 1
    for i in range(plan.nx):
        bases = [size * (i * plan.ny + j) + S * st for j in range(plan.ny)]
        parts = [in_ref[base : base + S, :] for base in bases]
        for xx, value in enumerate(turn_groups(plan, parts)):
            out_ref[i * gs + xx] = value
    if st:
        out_ref[XH] = jnp.zeros((S, LANES), jnp.float32)
        out_ref[XH, :1, :] = sum_rows(in_ref, size)


def sum_rows(ref, size):
    total = ref[size - 1 : size, :]
    for p in range(1, ref.shape[0] // size):
        total = total + ref[size * p + size - 1 : size * p + size, :]
    return total


def banded(taps, n, odd):
    row = lax.broadcasted_iota(jnp.int32, (n, n), 0)
    col = lax.broadcasted_iota(jnp.int32, (n, n), 1)
    gap = row - col
    total = jnp.zeros((n, n), jnp.float32)
    for d, tap in enumerate(taps):
        if odd:
            if d:
                total = jnp.where(gap == d, d * tap, total)
                total = jnp.where(gap == -d, -(d * tap), total)
        else:
            total = jnp.where(jnp.abs(gap) == d, tap, total)
    return total


def halves(value):
    high = value.astype(jnp.bfloat16)
    return high, (value - high.astype(jnp.float32)).astype(jnp.bfloat16)


def quad(matrix):
    high, low = halves(matrix)
    row = jnp.concatenate([high, low], axis=1)
    return jnp.concatenate([row, row], axis=0)


def lanes_times(value, quad_ref):
    high, low = halves(value)
    both = jnp.concatenate([high, low], axis=1)
    out = jnp.dot(both, quad_ref[...], preferred_element_type=jnp.float32)
    return out[:, :LANES] + out[:, LANES:]


def even_sum(load, taps, mid):
    total = taps[0] * load(mid)
    for d in range(1, len(taps)):
        total = total + taps[d] * (load(mid - d) + load(mid + d))
    return total


def unit_sum(load, taps, mid):
    total = load(mid)
    for d in range(1, len(taps)):
        total = total + taps[d] * (load(mid - d) + load(mid + d))
    return total


def odd_sum(load, taps, mid):
    total = taps[1] * (load(mid + 1) - load(mid - 1))
    for d in range(2, len(taps)):
        total = total + (d * taps[d]) * (load(mid + d) - load(mid - d))
    return total


MANY = 16


def run_passes(plan, passes):
    chunks = range(0, plan.X, MANY)
    for base in chunks:
        passes[0][0](base)
    for (_, matmul_part, emit_part), after in zip(passes, passes[1:] + [None]):
        done = None

        def close(pair):
            emit_part(*pair)
            if after is not None:
                after[0](pair[0])

        for base in chunks:
            out = matmul_part(base)
            if done is not None:
                close(done)
            done = (base, out)
        close(done)


def kernel_pass(plan, taps, quad_ref, in_ref, zb_ref, rows, emit):
    R = plan.R

    def z_part(base):
        for x in range(base, base + MANY):
            zb_ref[R + x, :rows, :] = unit_sum(lambda j: in_ref[x, j : j + rows, :], taps, R)

    def matmul_part(base):
        parts = [
            unit_sum(lambda j: zb_ref[base + q + j, :rows, :], taps, R) for q in range(MANY)
        ]
        return lanes_times(jnp.concatenate(parts, axis=0), quad_ref)

    def emit_part(base, out):
        for q in range(MANY):
            emit(base + q, out[q * rows : (q + 1) * rows])

    return z_part, matmul_part, emit_part


def inside(plan, at, off, rows):
    z = lax.broadcasted_iota(jnp.int32, (rows, LANES), 0) + (at * plan.S - plan.H + off)
    return (z >= 0) & (z < plan.Z)


def scale_step(plan, at, taps, quad_ref, zb, src, top, dst, over, off, start, rows):
    mask = inside(plan, at, off + start, rows)
    src = src.at[:, pl.ds(top, rows + 2 * plan.R), :]
    lead = (off + 7) // 8 * 8
    over = over.at[:, pl.ds(start, rows + lead), :]

    def emit(x, value):
        dst[x, pl.ds(start, rows), :] = jnp.where(mask, over[x, off : off + rows, :] / value, 0.0)

    return kernel_pass(plan, taps, quad_ref, src, zb, rows, emit)


def clear_edges(ref, edge, size):
    blank = jnp.zeros((edge,) + ref.shape[1:], jnp.float32)
    ref[:edge] = blank
    ref[edge + size :] = blank


def prep_kernel(plan, k_ref, s_ref, own, taps_ref, quad_ref, slope_ref, smooth_ref, high_ref,
                low_ref, plane_ref, line_ref):
    del own
    R, Q = plan.R, plan.Q
    taps = [jnp.zeros((1, LANES), jnp.float32) + k_ref[d] for d in range(R + 1)]
    taps = [jnp.ones((1, LANES), jnp.float32)] + [tap / taps[0] for tap in taps[1:]]
    stap = smooth_taps(s_ref, Q)
    for d in range(R + 1):
        taps_ref[d] = jnp.broadcast_to(taps[d], (8, LANES))
    for d in range(Q + 1):
        taps_ref[R + 1 + d] = jnp.broadcast_to(stap[d], (8, LANES))
    quad_ref[...] = quad(banded(taps, LANES, False))
    slope_ref[...] = quad(banded(taps, LANES, True))
    smooth_ref[...] = quad(banded(stap, LANES, False))
    wide = [jnp.concatenate([t] * (plan.Z // LANES), axis=1) for t in stap]
    high_ref[...], low_ref[...] = halves(banded(wide, plan.Z, False))


    def reach_sum(shape, axis, start, size):
        place = lax.broadcasted_iota(jnp.int32, shape, axis) + start
        total = jnp.ones(shape, jnp.float32)
        for d in range(1, R + 1):
            total = total + jnp.where(place - d >= 0, taps[d], 0.0)
            total = total + jnp.where(place + d < size, taps[d], 0.0)
        return total

    at = place_of(plan)
    shape = plane_ref.shape
    over = reach_sum(shape, 0, at * plan.S - plan.H, plan.Z) * reach_sum(shape, 1, 0, plan.Y)
    plane_ref[...] = jnp.where(inside(plan, at, 0, shape[0]), 1.0 / over, 0.0)
    line_ref[...] = 1.0 / reach_sum(line_ref.shape, 0, 0, plan.X)


def kernel_taps(plan, taps_ref):
    return [taps_ref[d, :1, :] for d in range(plan.R + 1)]


def gaps_of(plan, tot, tw, olds, news):
    S = plan.S
    half = S // 2
    mine = pl.multiple_of(half * lax.axis_index("gz"), 8)
    first_half = lane_at() < LANES // 2
    both = tot[:1, :]
    sum_s = jnp.sum(jnp.where(first_half, both, 0.0), axis=1, keepdims=True)
    sum_t = jnp.sum(jnp.where(first_half, 0.0, both), axis=1, keepdims=True)
    scale_s = plan.cells / jnp.broadcast_to(sum_s, (1, LANES))
    scale_t = plan.cells / jnp.broadcast_to(sum_t, (1, LANES))

    def mid(ref):
        edge = (ref.shape[1] - S) // 2
        ref = ref.at[:, pl.ds(mine, ref.shape[1] - half), :]
        return lambda x: ref[x, edge : edge + half, :]

    t_at = mid(tw)
    olds = [old if old is None else mid(old) for old in olds]
    news = [mid(new) for new in news]

    def p_step(x, carry):
        t = t_at(x)
        want = scale_t * t
        have = scale_s * t
        result = []
        for part, old, new in zip(carry, olds, news):
            value = have / new(x)
            if old is not None:
                value = value * old(x)
            gap = jnp.abs(value - want)
            for r in range(0, half, 8):
                part = part + gap[r : r + 8]
            result.append(part)
        return tuple(result)

    zero = jnp.zeros((8, LANES), jnp.float32)
    gaps = lax.fori_loop(0, plan.X, p_step, (zero,) * len(news), unroll=4)
    return [jnp.sum(g, keepdims=True) for g in gaps]


def in_lanes(values, first=0):
    row = jnp.zeros((1, LANES), jnp.float32)
    for t, value in enumerate(values):
        row = jnp.where(lane_at() == first + t, value, row)
    return row


def gaps_kernel(plan, tot, tw, v1, v2, v3, v4, out_ref):
    out_ref[...] = in_lanes(gaps_of(plan, tot, tw, (None, v1, v2, v3), (v1, v2, v3, v4)))


def spread_halves(plan, at, own, even, odd, own2, even2, odd2, win):
    S, H, gs = plan.S, plan.H, plan.gs
    c = lax.axis_index("gz")

    def spread(low, high):
        for k, (mid, core) in enumerate(((own, c), (own2, 1 - c))):
            for i in range(plan.nx):
                x, here = plan.bx * i + gs * core, pl.ds(i * gs, gs)
                win[pl.ds(x, gs), H : H + S, :] = mid[here]
                win[pl.ds(x, gs), :H, :] = low[k][here]
                win[pl.ds(x, gs), H + S :, :] = high[k][here]

    pl.when(at % 2 == 0)(lambda: spread((odd, odd2), (even, even2)))
    pl.when(at % 2 == 1)(lambda: spread((even, even2), (odd, odd2)))


def open_kernel(plan, taps_ref, quad_ref, plane_ref, line_ref, own, even, odd, own2, even2, odd2,
                sw, ku, u, zb):
    R = plan.R
    at = place_of(plan)
    taps = kernel_taps(plan, taps_ref)
    clear_edges(zb, R, plan.X)
    spread_halves(plan, at, own, even, odd, own2, even2, odd2, sw)
    for x in range(plan.X):
        u[x] = sw[x] * (plane_ref[...] * line_ref[x : x + 1, :])

    def emit(x, value):
        ku[x] = value

    rows = ku.shape[1]
    run_passes(plan, [kernel_pass(plan, taps, quad_ref, u, zb, rows, emit)])


def first_kernel(plan, taps_ref, quad_ref, own, even, odd, own2, even2, odd2, sw, ku,
                 tw, v, v2, u_out, tot, u, zb, zc):
    R, S, H, X, XH = plan.R, plan.S, plan.H, plan.X, plan.XH
    at = place_of(plan)
    taps = kernel_taps(plan, taps_ref)
    clear_edges(zb, R, X)
    clear_edges(zc, R, X)
    spread_halves(plan, at, own, even, odd, own2, even2, odd2, tw)
    tot[...] = own[XH, :1, :] + own2[XH, :1, :]
    rows = S + 2 * H - 2 * R
    mask = inside(plan, at, R, rows)

    for x in range(X):
        v[x] = jnp.where(mask, tw[x, R : R + rows, :] / ku[x], 0.0)
    step = functools.partial(scale_step, plan, at, taps, quad_ref)
    run_passes(plan, [
        step(zb, v, 0, u, sw, 2 * R, 0, rows - 2 * R),
        step(zc, u, 0, v2, tw, 3 * R, 0, rows - 4 * R),
        step(zb, v2, 0, u_out, sw, 4 * R, 0, rows - 6 * R),
    ])


def early_kernel(plan, taps_ref, quad_ref, mine, side, sw, tw, v, u, v2, win, zb, zc):
    R, S, H = plan.R, plan.S, plan.H
    c = lax.axis_index("gz")
    at = place_of(plan)
    taps = kernel_taps(plan, taps_ref)
    clear_edges(zb, R, plan.X)
    clear_edges(zc, R, plan.X)
    real = jnp.where(jnp.where(c == 0, at > 0, at < plan.P - 1), 1.0, 0.0)
    win[:, pl.ds(pl.multiple_of(H * c, 8), H), :] = side[...] * real
    win[:, pl.ds(pl.multiple_of(H * (1 - c), 8), S), :] = mine[...]
    step = functools.partial(scale_step, plan, at, taps, quad_ref)
    from_ = pl.multiple_of(S * c, 8)
    run_passes(plan, [
        step(zb, win, 0, v, tw, R, from_, S + H - 2 * R),
        step(zc, v, from_, u, sw, 2 * R, from_, S + H - 4 * R),
        step(zb, u, from_, v2, tw, 3 * R, from_, S + H - 6 * R),
    ])


def late_rows(plan, at, taps, quad_ref, mine, other, sw, tw, v, u, v2, win, zb, zc):
    R, S, H = plan.R, plan.S, plan.H
    c = lax.axis_index("gz")
    real = jnp.where(jnp.where(c == 1, at > 0, at < plan.P - 1), 1.0, 0.0)
    half = S // 2

    def lay(other_at, mine_at, mine_from):
        win[:, other_at : other_at + H, :] = other[...] * real
        win[:, mine_at : mine_at + half, :] = mine[:, mine_from : mine_from + half, :]

    pl.when(c == 0)(lambda: lay(half, 0, half))
    pl.when(c == 1)(lambda: lay(0, H, 0))
    step = functools.partial(scale_step, plan, at, taps, quad_ref)
    first = pl.multiple_of((S + H - 2 * R) * (1 - c), 8)
    second = pl.multiple_of((S + H - 4 * R) * (1 - c), 8)
    third = pl.multiple_of((S + H - 6 * R) * (1 - c), 8)
    return [
        step(zb, win, 0, v, tw, R, first, S),
        step(zc, v, second, u, sw, 2 * R, second, S),
        step(zb, u, third, v2, tw, 3 * R, third, S),
    ]


def late_kernel(plan, taps_ref, quad_ref, mine, other, sw, tw, v_in, u_in, v2_in,
                v, u, v2, u_out, win, zb, zc):
    del v_in, u_in, v2_in
    R, S = plan.R, plan.S
    at = place_of(plan)
    taps = kernel_taps(plan, taps_ref)
    clear_edges(zb, R, plan.X)
    clear_edges(zc, R, plan.X)
    passes = late_rows(plan, at, taps, quad_ref, mine, other, sw, tw, v, u, v2, win, zb, zc)
    passes.append(scale_step(plan, at, taps, quad_ref, zc, v2, 0, u_out, sw, 4 * R, 0, S))
    run_passes(plan, passes)


def smooth_taps(s_ref, reach):
    total = s_ref[0]
    tail = s_ref[1]
    for d in range(2, reach + 1):
        tail = tail + s_ref[d]
    scale = 1.0 / (jnp.zeros((1, LANES), jnp.float32) + (total + 2.0 * tail))
    return [scale * s_ref[d] for d in range(reach + 1)]


def last_kernel(plan, taps_ref, quad_ref, slope_ref, smooth_ref, mine, other, sw, tw, prev,
                gaps, tot, v_in, u_in, v2_in, v, u, v2, out_ref, win, zb, zc, zg, raw):
    del v_in, u_in, v2_in
    R, S, H, X, gs, Q = plan.R, plan.S, plan.H, plan.X, plan.gs, plan.Q
    half = S // 2
    size = 3 * half + 1
    c = lax.axis_index("gz")
    at = place_of(plan)
    taps = kernel_taps(plan, taps_ref)
    stap = [taps_ref[R + 1 + d, :1, :] for d in range(Q + 1)]
    clear_edges(zb, R, X)
    clear_edges(zc, R, X)
    clear_edges(zg, R, X)
    for comp in range(3):
        clear_edges(raw.at[comp], Q, X)
    real = jnp.where(jnp.where(c == 1, at > 0, at < plan.P - 1), 1.0, 0.0)

    @pl.when(c == 0)
    def _():
        win[:, :half, :] = mine[:, half:, :]
        win[:, half:, :] = other[:, :half, :] * real

    @pl.when(c == 1)
    def _():
        win[:, :half, :] = other[:, H - half :, :] * real
        win[:, half:, :] = mine[:, :half, :]

    step = functools.partial(scale_step, plan, at, taps, quad_ref)
    own = pl.multiple_of(half * c, 8)
    first = pl.multiple_of(S + half - S * c, 8)
    second = pl.multiple_of(S - half * c, 8)
    passes = [
        step(zb, win, 0, v, tw, R, first, half),
        step(zc, v, second, u, sw, 2 * R, second, half),
        step(zb, u, half, v2, tw, 3 * R, half, half),
    ]
    near = v2.at[:, pl.ds(own, S), :]

    def z_part(base):
        for x in range(base, base + MANY):
            load = lambda j: near[x, j : j + half, :]
            zc[R + x, :half, :] = unit_sum(load, taps, R)
            zg[R + x] = odd_sum(load, taps, R)

    def matmul_part(base):
        kk, gk, kg = [], [], []
        for q in range(MANY):
            flat = lambda j: zc[base + q + j, :half, :]
            kk.append(unit_sum(flat, taps, R))
            gk.append(odd_sum(flat, taps, R))
            kg.append(unit_sum(lambda j: zg[base + q + j], taps, R))
        kk, gk, kg = (jnp.concatenate(part, axis=0) for part in (kk, gk, kg))
        nums = lanes_times(gk, quad_ref), lanes_times(kk, slope_ref), lanes_times(kg, quad_ref)
        return lanes_times(kk, quad_ref), nums

    def emit_part(base, out):
        kvol, nums = out
        for comp, num in enumerate(nums):
            value = num / kvol
            for q in range(MANY):
                raw[comp, Q + base + q] = value[q * half : (q + 1) * half]

    run_passes(plan, passes + [(z_part, matmul_part, emit_part)])

    for i in range(plan.nx):
        for comp in range(3):
            x = plan.bx * i
            parts = [even_sum(lambda j: raw[comp, x + k + j], stap, Q) for k in range(plan.bx)]
            flat = lanes_times(jnp.concatenate(parts, axis=0), smooth_ref)
            for core in range(2):
                rows = range(gs * core, gs * (core + 1))
                turned = turn_groups(plan, [flat[k * half : (k + 1) * half] for k in rows])
                for j in range(plan.ny):
                    base = size * ((i * plan.ny + j) * 2 + core) + comp * half
                    out_ref[base : base + half, :] = turned[j]

    rows = gaps_of(plan, tot, tw, (prev, v), (v, v2))
    stat = gaps[...] + in_lanes(rows, ITERS - 2)
    for p in range(2 * plan.P):
        out_ref[size * (p + 1) - 1 : size * (p + 1), :] = stat


def smooth_z(core, high_ref, low_ref, d_high, d_low, emit):
    rows = pl.ds(pl.multiple_of(core * LANES, LANES), LANES)
    m_high, m_low = high_ref[rows, :], low_ref[rows, :]
    dot = functools.partial(jnp.dot, preferred_element_type=jnp.float32)
    for comp in range(3):
        lanes = slice(comp * LANES, (comp + 1) * LANES)
        high, low = d_high[:, lanes], d_low[:, lanes]
        emit(comp, (dot(m_high, high) + (dot(m_high, low) + dot(m_low, high))).T)


def away_kernel(plan, high_ref, low_ref, in_ref, send_ref, d_high, d_low):
    half = plan.S // 2
    size = 3 * half + 1
    for comp in range(3):
        for place in range(plan.P):
            bases = [size * plan.device(place, core) + comp * half for core in range(2)]
            both = jnp.concatenate([in_ref[base : base + half, :] for base in bases], axis=0)
            here = slice(plan.S * place, plan.S * (place + 1))
            lanes = slice(comp * LANES, (comp + 1) * LANES)
            d_high[here, lanes], d_low[here, lanes] = halves(both)

    def emit(comp, value):
        send_ref[comp] = value

    smooth_z(1 - lax.axis_index("gz"), high_ref, low_ref, d_high, d_low, emit)


def home_kernel(plan, high_ref, low_ref, d_high, d_low, in_ref, mis_hbm, out_hbm, keep, mis_ref, sems):
    c = lax.axis_index("gz")
    gs = plan.gs
    copies = [
        pltpu.make_async_copy(keep.at[k], out_hbm.at[k, pl.ds(gs * c, gs)], sems.at[k])
        for k in range(3)
    ]

    def emit(comp, value):
        keep[comp] = value.reshape(gs, plan.by, LANES)
        copies[comp].start()

    smooth_z(c, high_ref, low_ref, d_high, d_low, emit)
    gone = sum_rows(in_ref, 3 * plan.S // 2 + 1) / plan.cells
    for t in range(ITERS):
        mis_ref[t] = jnp.sum(jnp.where(lane_at() == t, gone, 0.0))
    copies.append(pltpu.make_async_copy(mis_ref, mis_hbm, sems.at[3]))
    copies[-1].start()
    for copy in copies:
        copy.wait()


def place_kernel(plan, recv_ref, in_hbm, out_hbm, sems):
    del in_hbm
    at = pl.ds(plan.gs * (1 - lax.axis_index("gz")), plan.gs)
    copies = [
        pltpu.make_async_copy(recv_ref.at[k], out_hbm.at[k, at], sems.at[k]) for k in range(3)
    ]
    for copy in copies:
        copy.start()
    for copy in copies:
        copy.wait()


def slab_shards(plan, source, target, kernel_half, smooth_half):
    R, S, H, X, XH, Pn, Z = plan.R, plan.S, plan.H, plan.X, plan.XH, plan.P, plan.Z
    bind = lambda kernel, *more: functools.partial(kernel, plan, *more)
    half = f32(2, LANES, LANES)
    vm = lambda *shape: pltpu.VMEM(shape, jnp.float32)
    keep, stat = call(
        bind(pack_kernel), [half, f32(1, LANES)], 0, 0,
        [vm(*source.shape), vm(*source.shape), pltpu.SemaphoreType.DMA((2,))], n_any=2,
    )(*(pltpu.with_memory_space_constraint(a, pltpu.HBM) for a in (source, target)))
    (chunks,) = call(
        bind(chunk_kernel), [f32(Pn * (2 * S + 1), LANES)], 0, 4, [vm(*half.shape)]
    )(keep, swap_cores(plan, source), swap_cores(plan, target), stat)
    spread = trade_chunks(chunks, ("gx", "gy"))
    unpack = lambda st: call(bind(unpack_kernel, st), [f32(XH + st, S, LANES)], 0, 1)(spread)[0]
    own_s = unpack(0)
    own_t = unpack(1)
    square = jax.ShapeDtypeStruct((2 * LANES, 2 * LANES), jnp.bfloat16)
    table = jax.ShapeDtypeStruct((Z, Z), jnp.bfloat16)
    taps, quad_k, quad_g, quad_s, high, low, plane, line = call(
        bind(prep_kernel),
        [f32(R + plan.Q + 2, 8, LANES), square, square, square, table, table,
         f32(S + 2 * H, LANES), f32(X, LANES)],
        2, 0, n_any=1,
    )(kernel_half, smooth_half, own_s)
    even_s, odd_s = swap_even(plan, own_s), swap_odd(plan, own_s)
    even_t, odd_t = swap_even(plan, own_t), swap_odd(plan, own_t)
    own2_s, own2_t = swap_cores(plan, own_s), swap_cores(plan, own_t)
    even_s, odd_s, taps = lax.optimization_barrier((even_s, odd_s, taps))
    halos_s = swap_cores(plan, even_s), swap_cores(plan, odd_s)
    even_t, odd_t, own2_s = lax.optimization_barrier((even_t, odd_t, own2_s))
    halos_t = swap_cores(plan, even_t), swap_cores(plan, odd_t)

    slab = f32(X, S, LANES)
    width = S + 2 * H
    wide, v_shape, u_shape, v2_shape = (f32(X, width - 2 * k * R, LANES) for k in (0, 1, 2, 3))
    zb = vm(X + 2 * R, width - 2 * R, LANES)
    sw, ku = call(
        bind(open_kernel), [wide, v_shape], 0, 10, [vm(*wide.shape), zb]
    )(taps, quad_k, plane, line, own_s, even_s, odd_s, own2_s, *halos_s)
    tw, v1, v2, u, tot = call(
        bind(first_kernel), [wide, v_shape, v2_shape, slab, f32(1, LANES)], 0, 10,
        [vm(*u_shape.shape), zb, zb],
    )(taps, quad_k, own_t, even_t, odd_t, own2_t, *halos_t, sw, ku)

    def early(u, side):
        return call(
            bind(early_kernel), [v_shape, u_shape, v2_shape], 0, 6,
            [vm(X, S + H, LANES), zb, zb],
        )(taps, quad_k, u, side, sw, tw)

    rest = vm(X, H + S // 2, LANES)
    side = swap_sides(plan, u)
    other = swap_cores(plan, side)
    v3, u4, v4 = early(u, side)
    v3, _, v4, u = call(
        bind(late_kernel), [v_shape, u_shape, v2_shape, slab], 0, 9, [rest, zb, zb],
        aliases={6: 0, 7: 1, 8: 2},
    )(taps, quad_k, u, other, sw, tw, v3, u4, v4)
    side = swap_sides(plan, u)
    (gaps,) = call(bind(gaps_kernel), [f32(1, LANES)], 0, 6)(tot, tw, v1, v2, v3, v4)
    side, gaps = lax.optimization_barrier((side, gaps))
    other = swap_cores(plan, side)
    v5, u6, v6 = early(u, side)
    *_, chunks = call(
        bind(last_kernel), [v_shape, u_shape, v2_shape, f32(2 * Pn * (3 * S // 2 + 1), LANES)], 0, 14,
        [vm(X, S, LANES), zb, zb, vm(X + 2 * R, S // 2, LANES), vm(3, X + 2 * plan.Q, S // 2, LANES)],
        aliases={11: 0, 12: 1, 13: 2},
    )(taps, quad_k, quad_g, quad_s, u, other, sw, tw, v4, gaps, tot, v5, u6, v6)
    spread = trade_chunks(chunks, AXES)
    split = jax.ShapeDtypeStruct((Z, 3 * LANES), jnp.bfloat16)
    send, *splits = call(
        bind(away_kernel), [f32(3, LANES, LANES), split, split], 0, 3
    )(high, low, spread)
    half = (3, plan.gs, plan.by, LANES)
    recv = swap_cores(plan, send.reshape(half))
    whole = f32(3, plan.bx, plan.by, LANES)
    mismatch, displacement = call(
        bind(home_kernel), [f32(ITERS), whole], 0, 5, [vm(*half), pltpu.SMEM((ITERS,), jnp.float32), pltpu.SemaphoreType.DMA((4,))],
        any_out=2,
    )(high, low, *splits, spread)
    (displacement,) = call(
        bind(place_kernel), [whole], 0, 1, [pltpu.SemaphoreType.DMA((3,))], n_any=1, any_out=1,
        aliases={1: 0},
    )(recv, displacement)
    return displacement, mismatch


def shards(sizes, source, target, kernel_half, smooth_half):
    plan = Plan(sizes, *source.shape, kernel_half.shape[0] - 1, smooth_half.shape[0] - 1)
    if plan.fits():
        return slab_shards(plan, source, target, kernel_half, smooth_half)
    return block_shards(source, target, kernel_half, smooth_half)


def solution(mesh):
    in_specs = (P("gx", "gy", "gz"), P("gx", "gy", "gz"), P(), P())
    out_specs = (P(None, "gx", "gy", "gz"), P())
    body = functools.partial(shards, dict(mesh.shape))
    return jax.shard_map(body, mesh=mesh, in_specs=in_specs, out_specs=out_specs, check_vma=False)
```
